32 devices in a mesh: batch: 2 (over y), freq: 16 (over z, x, core).
Axes of the slice: x: 2, y: 2, z: 4, core: 2. Of those that a mesh axis runs over, the one named last changes fastest.
Arguments:
- images: bfloat16 [128, 128, 512], P(('batch', 'freq')), may hold values from -50 to 50
- radial_counts: int32 [256], replicated, may hold values from 1 to 120, as said below
- order: int32 [256], replicated, may hold values from 0 to 255, as said below
- zeros_table: int32 [256, 128], replicated, may hold values from 1 to 128, as said below
- noise_var: float32 [256], replicated, may hold values from 0.25 to 4
Outputs:
- denoised: bfloat16 [128, 128, 512], P(('batch', 'freq'))
- wiener_blocks: float32 [256, 128, 128], P('freq')
The draws below stay inside these ranges and needn't reach their ends.
Inputs may be any that keep to these rules, and one draw needn't show every extreme that they name: `radial_counts`: frequencies from 128 on have at most 64 radial modes, and frequency 128 has exactly 64; frequency 0 has exactly 120. `order`: A permutation of the 256 frequencies. For every d, slots 16d and 16d + 1 hold frequencies below 128, and the other 8 slots of d hold frequencies from 128 on. `zeros_table`: the values of one row are distinct.
All inputs are finite; a program needn't handle non-finite values.
Results may differ from the reference program's by a relative error of at most 0.0085.
Values may be sent and summed in bfloat16 or wider, within the bound.
No kernel may reach another device: no remote copies, remote signals or barrier semaphores. Data moves between devices by JAX's collectives and lax.ppermute only.
A program may use at most 64 MiB of HBM per device.

```python
import math
import jax
import jax.numpy as jnp
from jax import lax

IMG_DEV = 4
R = 128
A = 512
K = 256
QMAX = 120
QH = 64
NIMG = 128
N_BATCH = 2
N_FREQ = 16


def draw_images(key, part):
    key_scale, key_profile, key_noise = jax.random.split(key, 3)
    rows = jnp.arange(NIMG, dtype=jnp.int32)
    per_batch = NIMG // N_BATCH
    position = (rows // per_batch).astype(jnp.float32)
    trend = 1.0 + 2.0 * position / max(N_BATCH - 1, 1)
    scale = jnp.exp(jax.random.uniform(key_scale, (NIMG,), jnp.float32, math.log(0.5), math.log(1.5))) * trend * 0.5
    profile = jnp.exp(jax.random.uniform(key_profile, (R,), jnp.float32, math.log(0.3), math.log(3.0)))
    noise = jax.random.normal(key_noise, (NIMG, R, A), jnp.float32)
    values = scale[:, None, None] * profile[None, :, None] * noise
    return jnp.clip(values, -50.0, 50.0).astype(jnp.bfloat16)


def draw_radial_counts(key, part):
    freqs = jnp.arange(K, dtype=jnp.int32)
    half_freq = K // 2
    upper = jnp.where(freqs < half_freq, QMAX - (QMAX - QH) * freqs // half_freq, QH - (QH - 1) * (freqs - half_freq) // half_freq)
    raw = jax.random.randint(key, (K,), 0, 1000000, jnp.int32)
    cut = raw % (upper // 4 + 1)
    counts = jnp.maximum(1, upper - cut)
    fixed = (freqs == 0) | (freqs == half_freq)
    return jnp.where(fixed, upper, counts).astype(jnp.int32)


def draw_order(key, part):
    key_low, key_high = jax.random.split(key, 2)
    half_freq = K // 2
    per_owner = K // N_FREQ
    lower = jax.random.permutation(key_low, half_freq).astype(jnp.int32)
    higher = half_freq + jax.random.permutation(key_high, half_freq).astype(jnp.int32)
    joined = jnp.concatenate([lower.reshape(-1, per_owner // 2), higher.reshape(-1, per_owner // 2)], axis=1)
    return joined.reshape(K).astype(jnp.int32)


def draw_zeros_table(key, part):
    row_keys = jax.random.split(key, K)
    rows = jax.vmap(lambda row_key: jax.random.permutation(row_key, R))(row_keys)
    return (rows + 1).astype(jnp.int32)


def setup_inputs(seed: int = 0) -> dict:
    arg_keys = jax.random.split(jax.random.key(seed), 6)
    return {
        "images": draw_images(jax.random.fold_in(arg_keys[5], 71), 0),
        "radial_counts": draw_radial_counts(jax.random.fold_in(arg_keys[5], 71), 0),
        "order": draw_order(jax.random.fold_in(arg_keys[5], 71), 0),
        "zeros_table": draw_zeros_table(jax.random.fold_in(arg_keys[5], 71), 0),
        "noise_var": jnp.clip(jnp.exp(jax.random.uniform(arg_keys[4], (K,), jnp.float32, math.log(0.25), math.log(4.0))), 0.25, 4.0),
    }


def make_table(freqs, angles):
    angle_index = jnp.arange(angles, dtype=jnp.int32)
    product = angle_index[:, None] * freqs[None, :] % angles
    phase = 2.0 * math.pi / angles * product.astype(jnp.float32)
    factor = math.sqrt(2.0 / angles)
    return jnp.concatenate([factor * jnp.cos(phase), factor * jnp.sin(phase)], axis=1).astype(jnp.bfloat16)

def make_basis(freqs, zero_rows, counts, radial):
    slots = zero_rows.shape[1]
    freq_float = freqs.astype(jnp.float32)[:, None, None]
    scaled = math.pi * (zero_rows.astype(jnp.float32)[:, :, None] + 0.5 * freq_float - 0.25)
    grid = (jnp.arange(radial, dtype=jnp.float32) + 0.5) / radial
    phase = scaled * grid[None, None, :] - 0.5 * math.pi * freq_float - 0.25 * math.pi
    keep = jnp.arange(slots, dtype=jnp.int32)[None, :, None] < counts[:, None, None]
    values = math.sqrt(2.0 / radial) * jnp.cos(phase)
    return jnp.where(keep, values, jnp.zeros_like(values)).astype(jnp.bfloat16)

def shrink_from(gram, noise, vectors):
    width = gram.shape[1]
    eye = jnp.eye(width, dtype=jnp.float32)
    covariance = gram / vectors + noise[:, None, None] * eye
    lower = jnp.linalg.cholesky(covariance)
    inv_lower = jax.scipy.linalg.solve_triangular(lower, jnp.broadcast_to(eye, covariance.shape), lower=True)
    inverse = jnp.einsum('kmq,kmp->kqp', inv_lower, inv_lower, precision=lax.Precision.HIGHEST)
    return eye - noise[:, None, None] * inverse

def reference(images, radial_counts, order, zeros_table, noise_var):
    freqs = jnp.arange(K, dtype=jnp.int32)
    table = make_table(freqs, A)
    basis = make_basis(freqs, zeros_table, radial_counts, R)
    basis_wide = basis.astype(jnp.float32)
    group = IMG_DEV * N_FREQ
    stack = images.reshape(NIMG // group, group, R, A)

    def expand(block):
        spectrum = jnp.dot(block.reshape(group * R, A).astype(jnp.float32), table.astype(jnp.float32), preferred_element_type=jnp.float32)
        spectrum = spectrum.astype(jnp.bfloat16).reshape(group, R, 2, K)
        return jnp.einsum('ircj,jqr->jciq', spectrum.astype(jnp.float32), basis_wide).astype(jnp.bfloat16)

    def accumulate(total, block):
        coeffs = expand(block).astype(jnp.float32)
        return (total + jnp.einsum('jciq,jcip->jqp', coeffs, coeffs), None)
    gram, unused = lax.scan(accumulate, jnp.zeros((K, R, R), jnp.float32), stack)
    shrinkage = shrink_from(gram, noise_var, 2.0 * NIMG)
    shrink_low = lax.optimization_barrier(shrinkage.astype(jnp.bfloat16)).astype(jnp.float32)
    table_wide = table.astype(jnp.float32)

    def rebuild(block):
        coeffs = expand(block).astype(jnp.float32)
        filtered = jnp.einsum('kqp,kcip->kciq', shrink_low, coeffs).astype(jnp.bfloat16)
        spectrum_out = jnp.einsum('jciq,jqr->ircj', filtered.astype(jnp.float32), basis_wide).astype(jnp.bfloat16)
        flat = spectrum_out.reshape(group * R, 2 * K).astype(jnp.float32)
        return jnp.dot(flat, table_wide.T).astype(jnp.bfloat16).reshape(group, R, A)
    denoised = lax.map(rebuild, stack).reshape(NIMG, R, A)
    wiener_blocks = jnp.take(shrinkage, order, axis=0)
    return (denoised, wiener_blocks)
```

```python
import functools
import math

import jax
import jax.numpy as jnp
from jax import lax
from jax.experimental import pallas as pl
from jax.experimental.pallas import tpu as pltpu
from jax.sharding import PartitionSpec as P


def make_table(freqs, angles):
    angle_index = jnp.arange(angles, dtype=jnp.int32)
    product = angle_index[:, None] * freqs[None, :] % angles
    phase = 2.0 * math.pi / angles * product.astype(jnp.float32)
    factor = math.sqrt(2.0 / angles)
    return jnp.concatenate([factor * jnp.cos(phase), factor * jnp.sin(phase)], axis=1).astype(
        jnp.bfloat16
    )


def make_basis(freqs, zero_rows, counts, radial):
    slots = zero_rows.shape[1]
    freq_float = freqs.astype(jnp.float32)[:, None, None]
    scaled = math.pi * (zero_rows.astype(jnp.float32)[:, :, None] + 0.5 * freq_float - 0.25)
    grid = (jnp.arange(radial, dtype=jnp.float32) + 0.5) / radial
    phase = scaled * grid[None, None, :] - 0.5 * math.pi * freq_float - 0.25 * math.pi
    keep = jnp.arange(slots, dtype=jnp.int32)[None, :, None] < counts[:, None, None]
    values = math.sqrt(2.0 / radial) * jnp.cos(phase)
    return jnp.where(keep, values, jnp.zeros_like(values)).astype(jnp.bfloat16)


def gram_of(blocks):
    return jnp.einsum("kvq,kvp->kqp", blocks, blocks, preferred_element_type=jnp.float32)


def shrink_from(gram, noise, vectors):
    width = gram.shape[1]
    eye = jnp.eye(width, dtype=jnp.float32)
    covariance = gram / vectors + noise[:, None, None] * eye
    lower = jnp.linalg.cholesky(covariance)
    inv_lower = jax.scipy.linalg.solve_triangular(
        lower, jnp.broadcast_to(eye, covariance.shape), lower=True
    )
    inverse = jnp.einsum("kmq,kmp->kqp", inv_lower, inv_lower, precision=lax.Precision.HIGHEST)
    return eye - noise[:, None, None] * inverse


def apply_shrink(shrinkage, blocks):
    return jnp.einsum(
        "kqp,kvp->kvq", shrinkage.astype(jnp.bfloat16), blocks, preferred_element_type=jnp.float32
    ).astype(jnp.bfloat16)


def per_device(images, radial_counts, order, zeros_table, noise_var):
    count_img, radial, angles = images.shape
    total_freq = order.shape[0]
    block = min(64, total_freq)
    nblocks = total_freq // block
    flat = images.reshape(count_img * radial, angles)
    slot_rows = jnp.take(zeros_table, order, axis=0)
    slot_counts = jnp.take(radial_counts, order)

    def block_tools(index):
        start = index * block
        freqs = lax.dynamic_slice_in_dim(order, start, block)
        table = make_table(freqs, angles)
        rows_here = lax.dynamic_slice_in_dim(slot_rows, start, block, 0)
        counts_here = lax.dynamic_slice_in_dim(slot_counts, start, block)
        return (table, make_basis(freqs, rows_here, counts_here, radial))

    def analyse(index):
        table, basis = block_tools(index)
        spectrum = jnp.dot(flat, table, preferred_element_type=jnp.float32)
        spectrum = spectrum.astype(jnp.bfloat16).reshape(count_img, radial, 2, block)
        return jnp.einsum(
            "ircj,jqr->jciq", spectrum, basis, preferred_element_type=jnp.float32
        ).astype(jnp.bfloat16)

    pieces = lax.map(analyse, jnp.arange(nblocks, dtype=jnp.int32))
    moved = pieces.reshape(total_freq, 2 * count_img, radial)
    owners = lax.axis_size("freq")
    owned = total_freq // owners
    batches = lax.axis_size("batch")
    mine = lax.dynamic_slice_in_dim(order, lax.axis_index("freq") * owned, owned)
    noise_mine = jnp.take(noise_var, mine)
    half_slots = owned // 2
    narrow = radial // 2
    grouped = moved.reshape(owners, owned, 2 * count_img, radial)
    lower_part = grouped[:, :half_slots].reshape(owners * half_slots, 2 * count_img, radial)
    upper_part = grouped[:, half_slots:, :, :narrow].reshape(
        owners * half_slots, 2 * count_img, narrow
    )
    low_recv, high_recv = (
        lax.all_to_all(lower_part, "freq", split_axis=0, concat_axis=1, tiled=True),
        lax.all_to_all(upper_part, "freq", split_axis=0, concat_axis=1, tiled=True),
    )
    gram_low, gram_high = lax.psum((gram_of(low_recv), gram_of(high_recv)), "batch")
    vectors = low_recv.shape[1] * batches
    shrink_lower = shrink_from(gram_low, noise_mine[:half_slots], vectors)
    shrink_upper = shrink_from(gram_high, noise_mine[half_slots:], vectors)
    low_back, high_back = (
        lax.all_to_all(
            apply_shrink(shrink_lower, low_recv), "freq", split_axis=1, concat_axis=0, tiled=True
        ),
        lax.all_to_all(
            apply_shrink(shrink_upper, high_recv), "freq", split_axis=1, concat_axis=0, tiled=True
        ),
    )
    high_wide = jnp.pad(high_back, ((0, 0), (0, 0), (0, radial - narrow)))
    returned = jnp.concatenate(
        [
            low_back.reshape(owners, half_slots, 2 * count_img, radial),
            high_wide.reshape(owners, half_slots, 2 * count_img, radial),
        ],
        axis=1,
    )
    returned = returned.reshape(total_freq, 2 * count_img, radial)
    upper_wide = jnp.pad(shrink_upper, ((0, 0), (0, radial - narrow), (0, radial - narrow)))
    wiener_blocks = jnp.concatenate([shrink_lower, upper_wide], axis=0)
    filtered_blocks = returned.reshape(nblocks, block, 2, count_img, radial)

    def synthesise(index, total):
        table, basis = block_tools(index)
        piece = lax.dynamic_index_in_dim(filtered_blocks, index, 0, keepdims=False)
        spectrum_out = jnp.einsum(
            "jciq,jqr->ircj", piece, basis, preferred_element_type=jnp.float32
        )
        spectrum_out = spectrum_out.astype(jnp.bfloat16).reshape(count_img * radial, 2 * block)
        return total + lax.dot_general(
            spectrum_out, table, (((1,), (1,)), ((), ())), preferred_element_type=jnp.float32
        )

    summed = lax.fori_loop(
        0, nblocks, synthesise, jnp.zeros((count_img * radial, angles), jnp.float32)
    )
    denoised = summed.astype(jnp.bfloat16).reshape(count_img, radial, angles)
    return (denoised, wiener_blocks)


MASKED = 0


def cos_sin(turns, steps):
    quarter = steps // 4
    eighth = steps // 8
    shifted = turns + eighth
    quadrant = jnp.right_shift(shifted, int(math.log2(quarter)))
    x = ((shifted & (quarter - 1)) - eighth).astype(jnp.float32) * (2.0 * math.pi / steps)
    x2 = x * x
    s = x * (1.0 + x2 * (-1.0 / 6 + x2 * (1.0 / 120 + x2 * (-1.0 / 5040 + x2 / 362880))))
    c = 1.0 + x2 * (-0.5 + x2 * (1.0 / 24 + x2 * (-1.0 / 720 + x2 * (1.0 / 40320))))
    odd = (quadrant & 1) == 1
    cosine = jnp.where(odd, s, c)
    sine = jnp.where(odd, c, s)
    cosine = jnp.where(((quadrant + 1) & 2) != 0, -cosine, cosine)
    sine = jnp.where((quadrant & 2) != 0, -sine, sine)
    return cosine, sine


def iota(shape, dim):
    return lax.broadcasted_iota(jnp.int32, shape, dim)


class Plan:
    def __init__(self, images, order, owners, batches):
        self.count_img, self.radial, self.angles = images
        self.total = order
        self.owners, self.batches = owners, batches
        self.devices = owners * batches
        self.owned = order // owners
        self.half = self.owned // 2
        self.quota = self.half // batches if self.half % batches == 0 else 0
        self.slots = 2 * self.quota
        self.vecs = 2 * self.count_img
        power = lambda n: n > 0 and n & (n - 1) == 0
        self.fits = (
            self.slots == 8
            and self.radial == 128
            and all(power(n) for n in (self.angles, self.total, owners, batches))
        )


def analysis_kernel(plan, order_ref, images_ref, coef_ref, table_ref, cb_ref, sb_ref, wave_ref):
    n, radial, angles, total = plan.count_img, plan.radial, plan.angles, plan.total
    row = iota((total, total), 0)
    place = row & (plan.quota - 1)
    side = (row // plan.quota) & 1
    owner = (row // plan.slots) & (plan.owners - 1)
    batch = row // (plan.slots * plan.owners)
    slot = owner * plan.owned + side * plan.half + batch * plan.quota + place
    pick = (slot == iota((total, total), 1)).astype(jnp.float32).astype(jnp.bfloat16)
    held = jnp.broadcast_to(order_ref[...].astype(jnp.float32), (128, total)).astype(jnp.bfloat16)
    freq = lax.dot_general(pick, held, (((1,), (1,)), ((), ())), preferred_element_type=jnp.float32)
    freq = freq.astype(jnp.int32)
    lane = iota((total, 128), 1)
    for part in range(angles // 128):
        turns = ((lane + part * 128) * freq) & (angles - 1)
        cosine, sine = cos_sin(turns, angles)
        factor = math.sqrt(2.0 / angles)
        cols = slice(part * 128, part * 128 + 128)
        table_ref[0:total, cols] = (factor * cosine).astype(jnp.bfloat16)
        table_ref[total : 2 * total, cols] = (factor * sine).astype(jnp.bfloat16)
    steps = 16 * radial
    turns = ((2 * freq - 1) * (2 * lane + 1) - 4 * radial * freq - 2 * radial) & (steps - 1)
    cosine, sine = cos_sin(turns, steps)
    cb_ref[...] = cosine
    sb_ref[...] = sine
    zero = iota((radial, radial), 1) + 1
    turns = (zero * (2 * iota((radial, radial), 0) + 1)) & (4 * radial - 1)
    cosine, sine = cos_sin(turns, 4 * radial)
    factor = math.sqrt(2.0 / radial)
    wave_ref[0:radial, :] = (factor * cosine).astype(jnp.bfloat16)
    wave_ref[radial : 2 * radial, :] = (-factor * sine).astype(jnp.bfloat16)
    for i in range(n):
        spectrum = lax.dot_general(
            table_ref[...],
            images_ref[i],
            (((1,), (1,)), ((), ())),
            preferred_element_type=jnp.float32,
        )
        pieces = []
        for c in range(2):
            part = spectrum[c * total : (c + 1) * total]
            turned = jnp.concatenate(
                [(part * cb_ref[...]).astype(jnp.bfloat16), (part * sb_ref[...]).astype(jnp.bfloat16)],
                axis=1,
            )
            coef = jnp.dot(turned, wave_ref[...], preferred_element_type=jnp.float32)
            pieces.append(coef.reshape(plan.devices, plan.slots, radial))
        both = jnp.concatenate(pieces, axis=1).astype(jnp.bfloat16)
        coef_ref[:, 2 * plan.slots * i : 2 * plan.slots * (i + 1), :] = both


def sweep(ref, base, step, lanes_of):
    height = ref.shape[1]
    shape = (8, 128)
    start = pl.multiple_of(step * 8, 8)
    panel = ref[base, pl.ds(start, 8), :]
    sub = iota(shape, 0)
    lane = iota(shape, 1)
    for i in range(8):
        index = lanes_of(lane, step * 8 + i)
        here = lane == index
        col = jnp.take_along_axis(panel, index, axis=1)
        pivot = jnp.broadcast_to(col[i : i + 1], shape)
        line = jnp.broadcast_to(panel[i : i + 1], shape)
        scaled = jnp.where(here, 1.0, line) / pivot
        rest = jnp.where(here, 0.0, panel) - col * scaled
        panel = jnp.where(sub == i, scaled, rest)
    full = (height, 128)
    lane = iota(full, 1)
    block = ref[base]
    total = block
    first = lanes_of(lane, step * 8)
    total = jnp.where((lane >= first) & (lane < first + 8), 0.0, block)
    for j in range(8):
        col = jnp.take_along_axis(block, lanes_of(lane, step * 8 + j), axis=1)
        total = total - col * panel[j : j + 1]
    ref[base] = total
    ref[base, pl.ds(start, 8), :] = panel


def filter_kernel(
    plan, order_ref, noise_ref, counts_ref, zeros_ref, recv_ref,
    back_ref, low_ref, high_ref, wide_ref, full_ref, pair_ref, pick_ref,
):
    radial, quota, slots = plan.radial, plan.quota, plan.slots
    narrow = radial // 2
    rows = plan.devices * plan.vecs
    freq_at, batch_at = lax.axis_index("freq"), lax.axis_index("batch")
    wide_ref[...] = recv_ref[...].astype(jnp.float32).reshape(rows * slots, radial)
    square = (radial, radial)
    eye = (iota(square, 0) == iota(square, 1)).astype(jnp.float32)
    noises = []
    for s in range(slots):
        side = s // quota
        slot = freq_at * plan.owned + side * plan.half + batch_at * quota + (s - side * quota)
        k = order_ref[slot]
        noise = noise_ref[k]
        noises.append(noise)
        zero = zeros_ref[pl.ds(k, 1), :]
        zero = jnp.where(iota((1, radial), 1) < counts_ref[k], zero, MASKED)
        pick = (iota(square, 0) + 1 == zero).astype(jnp.float32).astype(jnp.bfloat16)
        pick_ref[s] = pick
        vectors = wide_ref[pl.ds(s, rows, stride=slots), :].astype(jnp.bfloat16)
        coef = jnp.dot(vectors, pick, preferred_element_type=jnp.float32).astype(jnp.bfloat16)
        gram = lax.dot_general(
            coef, coef, (((0,), (0,)), ((), ())), preferred_element_type=jnp.float32
        )
        covariance = gram / float(rows) + noise * eye
        if side == 0:
            full_ref[s] = covariance
        else:
            at = s - quota
            upper = covariance[:narrow]
            if at % 2:
                upper = pltpu.roll(upper, narrow, axis=1)
                held = pair_ref[at // 2]
                upper = jnp.where(iota((narrow, radial), 1) < narrow, held, upper)
            pair_ref[at // 2] = upper
    whole_lane = lambda lane, k: jnp.zeros_like(lane) + k
    half_lane = lambda lane, k: (lane & narrow) + k

    def both(step, carry):
        for m in range(quota):
            sweep(full_ref, m, step, whole_lane)
        for m in range(quota // 2):
            sweep(pair_ref, m, step, half_lane)
        return carry

    def lower(step, carry):
        for m in range(quota):
            sweep(full_ref, m, step, whole_lane)
        return carry

    lax.fori_loop(0, narrow // 8, both, 0)
    lax.fori_loop(narrow // 8, radial // 8, lower, 0)
    for s in range(slots):
        side = s // quota
        if side == 0:
            shrink = eye - noises[s] * full_ref[s]
            low_ref[s] = shrink
        else:
            at = s - quota
            upper = pair_ref[at // 2]
            if at % 2:
                upper = pltpu.roll(upper, narrow, axis=1)
            lane = iota((narrow, radial), 1)
            upper = jnp.where(lane < narrow, eye[:narrow] - noises[s] * upper, 0.0)
            shrink = jnp.concatenate([upper, jnp.zeros((radial - narrow, radial), jnp.float32)], axis=0)
            high_ref[at] = upper
        pick = pick_ref[s]
        shrink = shrink.astype(jnp.bfloat16)
        moved = lax.dot_general(
            shrink, pick, (((0,), (1,)), ((), ())), preferred_element_type=jnp.float32
        ).astype(jnp.bfloat16)
        spread = jnp.dot(pick, moved, preferred_element_type=jnp.float32).astype(jnp.bfloat16)
        vectors = wide_ref[pl.ds(s, rows, stride=slots), :].astype(jnp.bfloat16)
        filtered = jnp.dot(vectors, spread, preferred_element_type=jnp.float32)
        wide_ref[pl.ds(s, rows, stride=slots), :] = filtered
    back_ref[...] = wide_ref[...].reshape(back_ref.shape).astype(jnp.bfloat16)


def synthesis_kernel(
    plan, table_ref, cb_ref, sb_ref, wave_ref, low_ref, high_ref, other_low_ref, other_high_ref,
    recv_ref, out_ref, wiener_ref,
):
    n, radial, total = plan.count_img, plan.radial, plan.total
    slots, quota = plan.slots, plan.quota
    batch_at = lax.axis_index("batch")
    for i in range(n):
        both = recv_ref[:, 2 * slots * i : 2 * slots * (i + 1), :].astype(jnp.float32)
        pieces = []
        for c in range(2):
            filtered = both[:, c * slots : (c + 1) * slots, :].reshape(total, radial)
            turned = lax.dot_general(
                filtered.astype(jnp.bfloat16),
                wave_ref[...],
                (((1,), (1,)), ((), ())),
                preferred_element_type=jnp.float32,
            )
            part = turned[:, :radial] * cb_ref[...] + turned[:, radial:] * sb_ref[...]
            pieces.append(part.astype(jnp.bfloat16))
        spectrum = jnp.concatenate(pieces, axis=0)
        image = lax.dot_general(
            spectrum, table_ref[...], (((0,), (0,)), ((), ())), preferred_element_type=jnp.float32
        )
        out_ref[i] = image.astype(jnp.bfloat16)
    for here, low, high in ((batch_at, low_ref, high_ref), (1 - batch_at, other_low_ref, other_high_ref)):
        for s in range(quota):
            wiener_ref[here * quota + s] = low[s]
            narrow = radial // 2
            at = plan.half + here * quota + s
            wiener_ref[at, 0:narrow, :] = high[s]
            wiener_ref[at, narrow:radial, :] = jnp.zeros((radial - narrow, radial), jnp.float32)


VMEM = pl.BlockSpec(memory_space=pltpu.VMEM)
SMEM = pl.BlockSpec(memory_space=pltpu.SMEM)


def call(kernel, outs, ins, scratch=()):
    return pl.pallas_call(
        kernel,
        out_shape=outs,
        in_specs=ins,
        out_specs=jax.tree.map(lambda _: VMEM, outs),
        scratch_shapes=scratch,
    )


def fast_device(plan, images, radial_counts, order, zeros_table, noise_var):
    both = ("batch", "freq")
    radial, total, slots, quota = plan.radial, plan.total, plan.slots, plan.quota
    narrow = radial // 2
    width = plan.vecs * slots
    shape = jax.ShapeDtypeStruct
    coef, table, cb, sb, wave = call(
        functools.partial(analysis_kernel, plan),
        (
            shape((plan.devices, width, radial), jnp.bfloat16),
            shape((2 * total, plan.angles), jnp.bfloat16),
            shape((total, radial), jnp.float32),
            shape((total, radial), jnp.float32),
            shape((2 * radial, radial), jnp.bfloat16),
        ),
        [VMEM, VMEM],
    )(order.reshape(1, total), images)
    recv = lax.all_to_all(coef, both, split_axis=0, concat_axis=0, tiled=True)
    back, low, high = call(
        functools.partial(filter_kernel, plan),
        (
            shape((plan.devices, width, radial), jnp.bfloat16),
            shape((quota, radial, radial), jnp.float32),
            shape((quota, narrow, radial), jnp.float32),
        ),
        [SMEM, SMEM, SMEM, VMEM, VMEM],
        [
            pltpu.VMEM((plan.devices * width, radial), jnp.float32),
            pltpu.VMEM((quota, radial, radial), jnp.float32),
            pltpu.VMEM((quota // 2, narrow, radial), jnp.float32),
            pltpu.VMEM((slots, radial, radial), jnp.bfloat16),
        ],
    )(order, noise_var, radial_counts, zeros_table, recv)
    swap = [(0, 1), (1, 0)]
    other_low = lax.ppermute(low, "batch", swap)
    other_high = lax.ppermute(high, "batch", swap)
    returned = lax.all_to_all(back, both, split_axis=0, concat_axis=0, tiled=True)
    return call(
        functools.partial(synthesis_kernel, plan),
        (
            shape((plan.count_img, radial, plan.angles), jnp.bfloat16),
            shape((plan.owned, radial, radial), jnp.float32),
        ),
        [VMEM] * 9,
    )(table, cb, sb, wave, low, high, other_low, other_high, returned)


def solution(mesh):
    owners, batches = mesh.shape["freq"], mesh.shape["batch"]

    def body(images, radial_counts, order, zeros_table, noise_var):
        plan = Plan(images.shape, order.shape[0], owners, batches)
        if plan.fits and batches == 2:
            return fast_device(plan, images, radial_counts, order, zeros_table, noise_var)
        return per_device(images, radial_counts, order, zeros_table, noise_var)

    return jax.shard_map(
        body,
        mesh=mesh,
        in_specs=(P(("batch", "freq"), None, None), P(), P(), P(), P()),
        out_specs=(P(("batch", "freq"), None, None), P("freq", None, None)),
        check_vma=False,
    )
```

```python
import functools
import math

import jax
import jax.numpy as jnp
from jax import lax
from jax.experimental import pallas as pl
from jax.experimental.pallas import tpu as pltpu
from jax.sharding import PartitionSpec as P


def make_table(freqs, angles):
    angle_index = jnp.arange(angles, dtype=jnp.int32)
    product = angle_index[:, None] * freqs[None, :] % angles
    phase = 2.0 * math.pi / angles * product.astype(jnp.float32)
    factor = math.sqrt(2.0 / angles)
    return jnp.concatenate([factor * jnp.cos(phase), factor * jnp.sin(phase)], axis=1).astype(
        jnp.bfloat16
    )


def make_basis(freqs, zero_rows, counts, radial):
    slots = zero_rows.shape[1]
    freq_float = freqs.astype(jnp.float32)[:, None, None]
    scaled = math.pi * (zero_rows.astype(jnp.float32)[:, :, None] + 0.5 * freq_float - 0.25)
    grid = (jnp.arange(radial, dtype=jnp.float32) + 0.5) / radial
    phase = scaled * grid[None, None, :] - 0.5 * math.pi * freq_float - 0.25 * math.pi
    keep = jnp.arange(slots, dtype=jnp.int32)[None, :, None] < counts[:, None, None]
    values = math.sqrt(2.0 / radial) * jnp.cos(phase)
    return jnp.where(keep, values, jnp.zeros_like(values)).astype(jnp.bfloat16)


def gram_of(blocks):
    return jnp.einsum("kvq,kvp->kqp", blocks, blocks, preferred_element_type=jnp.float32)


def shrink_from(gram, noise, vectors):
    width = gram.shape[1]
    eye = jnp.eye(width, dtype=jnp.float32)
    covariance = gram / vectors + noise[:, None, None] * eye
    lower = jnp.linalg.cholesky(covariance)
    inv_lower = jax.scipy.linalg.solve_triangular(
        lower, jnp.broadcast_to(eye, covariance.shape), lower=True
    )
    inverse = jnp.einsum("kmq,kmp->kqp", inv_lower, inv_lower, precision=lax.Precision.HIGHEST)
    return eye - noise[:, None, None] * inverse


def apply_shrink(shrinkage, blocks):
    return jnp.einsum(
        "kqp,kvp->kvq", shrinkage.astype(jnp.bfloat16), blocks, preferred_element_type=jnp.float32
    ).astype(jnp.bfloat16)


def per_device(images, radial_counts, order, zeros_table, noise_var):
    count_img, radial, angles = images.shape
    total_freq = order.shape[0]
    block = min(64, total_freq)
    nblocks = total_freq // block
    flat = images.reshape(count_img * radial, angles)
    slot_rows = jnp.take(zeros_table, order, axis=0)
    slot_counts = jnp.take(radial_counts, order)

    def block_tools(index):
        start = index * block
        freqs = lax.dynamic_slice_in_dim(order, start, block)
        table = make_table(freqs, angles)
        rows_here = lax.dynamic_slice_in_dim(slot_rows, start, block, 0)
        counts_here = lax.dynamic_slice_in_dim(slot_counts, start, block)
        return (table, make_basis(freqs, rows_here, counts_here, radial))

    def analyse(index):
        table, basis = block_tools(index)
        spectrum = jnp.dot(flat, table, preferred_element_type=jnp.float32)
        spectrum = spectrum.astype(jnp.bfloat16).reshape(count_img, radial, 2, block)
        return jnp.einsum(
            "ircj,jqr->jciq", spectrum, basis, preferred_element_type=jnp.float32
        ).astype(jnp.bfloat16)

    pieces = lax.map(analyse, jnp.arange(nblocks, dtype=jnp.int32))
    moved = pieces.reshape(total_freq, 2 * count_img, radial)
    owners = lax.axis_size("freq")
    owned = total_freq // owners
    batches = lax.axis_size("batch")
    mine = lax.dynamic_slice_in_dim(order, lax.axis_index("freq") * owned, owned)
    noise_mine = jnp.take(noise_var, mine)
    half_slots = owned // 2
    narrow = radial // 2
    grouped = moved.reshape(owners, owned, 2 * count_img, radial)
    lower_part = grouped[:, :half_slots].reshape(owners * half_slots, 2 * count_img, radial)
    upper_part = grouped[:, half_slots:, :, :narrow].reshape(
        owners * half_slots, 2 * count_img, narrow
    )
    low_recv, high_recv = (
        lax.all_to_all(lower_part, "freq", split_axis=0, concat_axis=1, tiled=True),
        lax.all_to_all(upper_part, "freq", split_axis=0, concat_axis=1, tiled=True),
    )
    gram_low, gram_high = lax.psum((gram_of(low_recv), gram_of(high_recv)), "batch")
    vectors = low_recv.shape[1] * batches
    shrink_lower = shrink_from(gram_low, noise_mine[:half_slots], vectors)
    shrink_upper = shrink_from(gram_high, noise_mine[half_slots:], vectors)
    low_back, high_back = (
        lax.all_to_all(
            apply_shrink(shrink_lower, low_recv), "freq", split_axis=1, concat_axis=0, tiled=True
        ),
        lax.all_to_all(
            apply_shrink(shrink_upper, high_recv), "freq", split_axis=1, concat_axis=0, tiled=True
        ),
    )
    high_wide = jnp.pad(high_back, ((0, 0), (0, 0), (0, radial - narrow)))
    returned = jnp.concatenate(
        [
            low_back.reshape(owners, half_slots, 2 * count_img, radial),
            high_wide.reshape(owners, half_slots, 2 * count_img, radial),
        ],
        axis=1,
    )
    returned = returned.reshape(total_freq, 2 * count_img, radial)
    upper_wide = jnp.pad(shrink_upper, ((0, 0), (0, radial - narrow), (0, radial - narrow)))
    wiener_blocks = jnp.concatenate([shrink_lower, upper_wide], axis=0)
    filtered_blocks = returned.reshape(nblocks, block, 2, count_img, radial)

    def synthesise(index, total):
        table, basis = block_tools(index)
        piece = lax.dynamic_index_in_dim(filtered_blocks, index, 0, keepdims=False)
        spectrum_out = jnp.einsum(
            "jciq,jqr->ircj", piece, basis, preferred_element_type=jnp.float32
        )
        spectrum_out = spectrum_out.astype(jnp.bfloat16).reshape(count_img * radial, 2 * block)
        return total + lax.dot_general(
            spectrum_out, table, (((1,), (1,)), ((), ())), preferred_element_type=jnp.float32
        )

    summed = lax.fori_loop(
        0, nblocks, synthesise, jnp.zeros((count_img * radial, angles), jnp.float32)
    )
    denoised = summed.astype(jnp.bfloat16).reshape(count_img, radial, angles)
    return (denoised, wiener_blocks)


MASKED = 0


def cos_sin(turns, steps):
    quarter = steps // 4
    eighth = steps // 8
    shifted = turns + eighth
    quadrant = jnp.right_shift(shifted, int(math.log2(quarter)))
    x = ((shifted & (quarter - 1)) - eighth).astype(jnp.float32) * (2.0 * math.pi / steps)
    x2 = x * x
    s = x * (1.0 + x2 * (-1.0 / 6 + x2 * (1.0 / 120 + x2 * (-1.0 / 5040 + x2 / 362880))))
    c = 1.0 + x2 * (-0.5 + x2 * (1.0 / 24 + x2 * (-1.0 / 720 + x2 * (1.0 / 40320))))
    odd = (quadrant & 1) == 1
    cosine = jnp.where(odd, s, c)
    sine = jnp.where(odd, c, s)
    cosine = jnp.where(((quadrant + 1) & 2) != 0, -cosine, cosine)
    sine = jnp.where((quadrant & 2) != 0, -sine, sine)
    return cosine, sine


def iota(shape, dim):
    return lax.broadcasted_iota(jnp.int32, shape, dim)


class Plan:
    def __init__(self, images, order, owners, batches):
        self.count_img, self.radial, self.angles = images
        self.total = order
        self.owners, self.batches = owners, batches
        self.devices = owners * batches
        self.owned = order // owners
        self.half = self.owned // 2
        self.quota = self.half // batches if self.half % batches == 0 else 0
        self.slots = 2 * self.quota
        self.vecs = 2 * self.count_img
        power = lambda n: n > 0 and n & (n - 1) == 0
        self.fits = (
            self.slots == 8
            and self.radial == 128
            and all(power(n) for n in (self.angles, self.total, owners, batches))
        )


def analysis_kernel(plan, order_ref, images_ref, coef_ref, table_ref, cb_ref, sb_ref, wave_ref):
    n, radial, angles, total = plan.count_img, plan.radial, plan.angles, plan.total
    row = iota((total, total), 0)
    place = row & (plan.quota - 1)
    side = (row // plan.quota) & 1
    owner = (row // plan.slots) & (plan.owners - 1)
    batch = row // (plan.slots * plan.owners)
    slot = owner * plan.owned + side * plan.half + batch * plan.quota + place
    pick = (slot == iota((total, total), 1)).astype(jnp.float32).astype(jnp.bfloat16)
    held = jnp.broadcast_to(order_ref[...].astype(jnp.float32), (128, total)).astype(jnp.bfloat16)
    freq = lax.dot_general(pick, held, (((1,), (1,)), ((), ())), preferred_element_type=jnp.float32)
    freq = freq.astype(jnp.int32)
    lane = iota((total, 128), 1)
    for part in range(angles // 128):
        turns = ((lane + part * 128) * freq) & (angles - 1)
        cosine, sine = cos_sin(turns, angles)
        factor = math.sqrt(2.0 / angles)
        cols = slice(part * 128, part * 128 + 128)
        table_ref[0:total, cols] = (factor * cosine).astype(jnp.bfloat16)
        table_ref[total : 2 * total, cols] = (factor * sine).astype(jnp.bfloat16)
    steps = 16 * radial
    turns = ((2 * freq - 1) * (2 * lane + 1) - 4 * radial * freq - 2 * radial) & (steps - 1)
    cosine, sine = cos_sin(turns, steps)
    cb_ref[...] = cosine
    sb_ref[...] = sine
    zero = iota((radial, radial), 1) + 1
    turns = (zero * (2 * iota((radial, radial), 0) + 1)) & (4 * radial - 1)
    cosine, sine = cos_sin(turns, 4 * radial)
    factor = math.sqrt(2.0 / radial)
    wave_ref[0:radial, :] = (factor * cosine).astype(jnp.bfloat16)
    wave_ref[radial : 2 * radial, :] = (-factor * sine).astype(jnp.bfloat16)
    for i in range(n):
        spectrum = lax.dot_general(
            table_ref[...],
            images_ref[i],
            (((1,), (1,)), ((), ())),
            preferred_element_type=jnp.float32,
        )
        pieces = []
        for c in range(2):
            part = spectrum[c * total : (c + 1) * total]
            turned = jnp.concatenate(
                [(part * cb_ref[...]).astype(jnp.bfloat16), (part * sb_ref[...]).astype(jnp.bfloat16)],
                axis=1,
            )
            coef = jnp.dot(turned, wave_ref[...], preferred_element_type=jnp.float32)
            pieces.append(coef.reshape(plan.devices, plan.slots, radial))
        both = jnp.concatenate(pieces, axis=1).astype(jnp.bfloat16)
        coef_ref[:, 2 * plan.slots * i : 2 * plan.slots * (i + 1), :] = both


def thirds(x):
    first = x.astype(jnp.bfloat16)
    rest = x - first.astype(jnp.float32)
    second = rest.astype(jnp.bfloat16)
    third = (rest - second.astype(jnp.float32)).astype(jnp.bfloat16)
    return first, second, third


def outer(u, v):
    u1, u2, u3 = thirds(u)
    v1, v2, v3 = thirds(v)
    return lax.dot_general(
        jnp.concatenate([u1, u1, u1, u2, u2, u3], axis=0),
        jnp.concatenate([v1, v2, v3, v1, v2, v1], axis=0),
        (((0,), (0,)), ((), ())),
        preferred_element_type=jnp.float32,
    )


def first_lane(halved, lane, step):
    return (lane & 64 if halved else jnp.zeros_like(lane)) + step * 8


def pivot_panels(panels, halves, step):
    shape = (8, 128)
    sub, lane = iota(shape, 0), iota(shape, 1)
    blocks = [
        [
            jnp.take_along_axis(panel, first_lane(halved, lane, step) + j, axis=1)
            for j in range(8)
        ]
        for panel, halved in zip(panels, halves)
    ]
    for i in range(8):
        for at, cols in enumerate(blocks):
            inverse = 1.0 / jnp.broadcast_to(cols[i][i : i + 1], shape)
            fresh = []
            for j in range(8):
                if j == i:
                    fresh.append(jnp.where(sub == i, inverse, -cols[i] * inverse))
                else:
                    line = jnp.broadcast_to(cols[j][i : i + 1], shape) * inverse
                    fresh.append(jnp.where(sub == i, line, cols[j] - cols[i] * line))
            blocks[at] = fresh
    solved = []
    for panel, halved, cols in zip(panels, halves, blocks):
        offset = lane - first_lane(halved, lane, step)
        outside = (offset < 0) | (offset >= 8)
        total = jnp.zeros(shape, jnp.float32)
        for j in range(8):
            line = jnp.broadcast_to(panel[j : j + 1], shape)
            line = jnp.where(outside, line, jnp.where(offset == j, 1.0, 0.0))
            total = total + cols[j] * line
        solved.append(total)
    return solved


def sweep(matrices, step, carry):
    start = pl.multiple_of(step * 8, 8)
    halves = [halved for _, _, halved in matrices]
    panels = [ref[m, pl.ds(start, 8), :] for ref, m, _ in matrices]
    solved = pivot_panels(panels, halves, step)
    for (ref, m, halved), panel, fresh in zip(matrices, panels, solved):
        height = ref.shape[1]
        lane = iota((8, 128), 1)
        done = (lane & 63 if halved else lane) < step * 8
        update = outer(jnp.where(done, -panel, panel), fresh)
        lane = iota((height, 128), 1)
        if halved:
            update = jnp.where(lane < 64, update[:height], update[height:])
        offset = lane - first_lane(halved, lane, step)
        rest = jnp.where((offset >= 0) & (offset < 8), 0.0, ref[m])
        ref[m] = rest - update
        ref[m, pl.ds(start, 8), :] = fresh
    return carry


def filter_kernel(
    plan, order_ref, noise_ref, counts_ref, zeros_ref, recv_ref,
    back_ref, low_ref, high_ref, wide_ref, full_ref, pair_ref, pick_ref,
):
    radial, quota, slots = plan.radial, plan.quota, plan.slots
    narrow = radial // 2
    rows = plan.devices * plan.vecs
    freq_at, batch_at = lax.axis_index("freq"), lax.axis_index("batch")
    wide_ref[...] = recv_ref[...].astype(jnp.float32).reshape(rows * slots, radial)
    square = (radial, radial)
    eye = (iota(square, 0) == iota(square, 1)).astype(jnp.float32)
    noises = []
    for s in range(slots):
        side = s // quota
        slot = freq_at * plan.owned + side * plan.half + batch_at * quota + (s - side * quota)
        k = order_ref[slot]
        noise = noise_ref[k]
        noises.append(noise)
        zero = zeros_ref[pl.ds(k, 1), :]
        zero = jnp.where(iota((1, radial), 1) < counts_ref[k], zero, MASKED)
        pick = (iota(square, 0) + 1 == zero).astype(jnp.float32).astype(jnp.bfloat16)
        pick_ref[s] = pick
        vectors = wide_ref[pl.ds(s, rows, stride=slots), :].astype(jnp.bfloat16)
        coef = jnp.dot(vectors, pick, preferred_element_type=jnp.float32).astype(jnp.bfloat16)
        gram = lax.dot_general(
            coef, coef, (((0,), (0,)), ((), ())), preferred_element_type=jnp.float32
        )
        covariance = gram / float(rows) + noise * eye
        if side == 0:
            full_ref[s] = covariance
        else:
            at = s - quota
            upper = covariance[:narrow]
            if at % 2:
                upper = pltpu.roll(upper, narrow, axis=1)
                held = pair_ref[at // 2]
                upper = jnp.where(iota((narrow, radial), 1) < narrow, held, upper)
            pair_ref[at // 2] = upper
    lower = [(full_ref, m, False) for m in range(quota)]
    upper_pairs = [(pair_ref, m, True) for m in range(quota // 2)]
    both = functools.partial(sweep, lower + upper_pairs)
    lax.fori_loop(0, narrow // 8, both, 0)
    lax.fori_loop(narrow // 8, radial // 8, functools.partial(sweep, lower), 0)
    for s in range(slots):
        side = s // quota
        if side == 0:
            shrink = eye - noises[s] * full_ref[s]
            low_ref[s] = shrink
        else:
            at = s - quota
            upper = pair_ref[at // 2]
            if at % 2:
                upper = pltpu.roll(upper, narrow, axis=1)
            lane = iota((narrow, radial), 1)
            upper = jnp.where(lane < narrow, eye[:narrow] - noises[s] * upper, 0.0)
            shrink = jnp.concatenate([upper, jnp.zeros((radial - narrow, radial), jnp.float32)], axis=0)
            high_ref[at] = upper
        pick = pick_ref[s]
        shrink = shrink.astype(jnp.bfloat16)
        moved = lax.dot_general(
            shrink, pick, (((0,), (1,)), ((), ())), preferred_element_type=jnp.float32
        ).astype(jnp.bfloat16)
        spread = jnp.dot(pick, moved, preferred_element_type=jnp.float32).astype(jnp.bfloat16)
        vectors = wide_ref[pl.ds(s, rows, stride=slots), :].astype(jnp.bfloat16)
        filtered = jnp.dot(vectors, spread, preferred_element_type=jnp.float32)
        wide_ref[pl.ds(s, rows, stride=slots), :] = filtered
    back_ref[...] = wide_ref[...].reshape(back_ref.shape).astype(jnp.bfloat16)


def synthesis_kernel(
    plan, table_ref, cb_ref, sb_ref, wave_ref, low_ref, high_ref, other_low_ref, other_high_ref,
    recv_ref, out_ref, wiener_ref,
):
    n, radial, total = plan.count_img, plan.radial, plan.total
    slots, quota = plan.slots, plan.quota
    batch_at = lax.axis_index("batch")
    for i in range(n):
        both = recv_ref[:, 2 * slots * i : 2 * slots * (i + 1), :].astype(jnp.float32)
        pieces = []
        for c in range(2):
            filtered = both[:, c * slots : (c + 1) * slots, :].reshape(total, radial)
            turned = lax.dot_general(
                filtered.astype(jnp.bfloat16),
                wave_ref[...],
                (((1,), (1,)), ((), ())),
                preferred_element_type=jnp.float32,
            )
            part = turned[:, :radial] * cb_ref[...] + turned[:, radial:] * sb_ref[...]
            pieces.append(part.astype(jnp.bfloat16))
        spectrum = jnp.concatenate(pieces, axis=0)
        image = lax.dot_general(
            spectrum, table_ref[...], (((0,), (0,)), ((), ())), preferred_element_type=jnp.float32
        )
        out_ref[i] = image.astype(jnp.bfloat16)
    for here, low, high in ((batch_at, low_ref, high_ref), (1 - batch_at, other_low_ref, other_high_ref)):
        for s in range(quota):
            wiener_ref[here * quota + s] = low[s]
            narrow = radial // 2
            at = plan.half + here * quota + s
            wiener_ref[at, 0:narrow, :] = high[s]
            wiener_ref[at, narrow:radial, :] = jnp.zeros((radial - narrow, radial), jnp.float32)


VMEM = pl.BlockSpec(memory_space=pltpu.VMEM)
SMEM = pl.BlockSpec(memory_space=pltpu.SMEM)


def call(kernel, outs, ins, scratch=()):
    return pl.pallas_call(
        kernel,
        out_shape=outs,
        in_specs=ins,
        out_specs=jax.tree.map(lambda _: VMEM, outs),
        scratch_shapes=scratch,
    )


def fast_device(plan, images, radial_counts, order, zeros_table, noise_var):
    both = ("batch", "freq")
    radial, total, slots, quota = plan.radial, plan.total, plan.slots, plan.quota
    narrow = radial // 2
    width = plan.vecs * slots
    shape = jax.ShapeDtypeStruct
    coef, table, cb, sb, wave = call(
        functools.partial(analysis_kernel, plan),
        (
            shape((plan.devices, width, radial), jnp.bfloat16),
            shape((2 * total, plan.angles), jnp.bfloat16),
            shape((total, radial), jnp.float32),
            shape((total, radial), jnp.float32),
            shape((2 * radial, radial), jnp.bfloat16),
        ),
        [VMEM, VMEM],
    )(order.reshape(1, total), images)
    recv = lax.all_to_all(coef, both, split_axis=0, concat_axis=0, tiled=True)
    back, low, high = call(
        functools.partial(filter_kernel, plan),
        (
            shape((plan.devices, width, radial), jnp.bfloat16),
            shape((quota, radial, radial), jnp.float32),
            shape((quota, narrow, radial), jnp.float32),
        ),
        [SMEM, SMEM, SMEM, VMEM, VMEM],
        [
            pltpu.VMEM((plan.devices * width, radial), jnp.float32),
            pltpu.VMEM((quota, radial, radial), jnp.float32),
            pltpu.VMEM((quota // 2, narrow, radial), jnp.float32),
            pltpu.VMEM((slots, radial, radial), jnp.bfloat16),
        ],
    )(order, noise_var, radial_counts, zeros_table, recv)
    swap = [(0, 1), (1, 0)]
    other_low = lax.ppermute(low, "batch", swap)
    other_high = lax.ppermute(high, "batch", swap)
    returned = lax.all_to_all(back, both, split_axis=0, concat_axis=0, tiled=True)
    return call(
        functools.partial(synthesis_kernel, plan),
        (
            shape((plan.count_img, radial, plan.angles), jnp.bfloat16),
            shape((plan.owned, radial, radial), jnp.float32),
        ),
        [VMEM] * 9,
    )(table, cb, sb, wave, low, high, other_low, other_high, returned)


def solution(mesh):
    owners, batches = mesh.shape["freq"], mesh.shape["batch"]

    def body(images, radial_counts, order, zeros_table, noise_var):
        plan = Plan(images.shape, order.shape[0], owners, batches)
        if plan.fits and batches == 2:
            return fast_device(plan, images, radial_counts, order, zeros_table, noise_var)
        return per_device(images, radial_counts, order, zeros_table, noise_var)

    return jax.shard_map(
        body,
        mesh=mesh,
        in_specs=(P(("batch", "freq"), None, None), P(), P(), P(), P()),
        out_specs=(P(("batch", "freq"), None, None), P("freq", None, None)),
        check_vma=False,
    )
```

```python
import functools
import math

import jax
import jax.numpy as jnp
from jax import lax
from jax.experimental import pallas as pl
from jax.experimental.pallas import tpu as pltpu
from jax.sharding import PartitionSpec as P


def make_table(freqs, angles):
    angle_index = jnp.arange(angles, dtype=jnp.int32)
    product = angle_index[:, None] * freqs[None, :] % angles
    phase = 2.0 * math.pi / angles * product.astype(jnp.float32)
    factor = math.sqrt(2.0 / angles)
    return jnp.concatenate([factor * jnp.cos(phase), factor * jnp.sin(phase)], axis=1).astype(
        jnp.bfloat16
    )


def make_basis(freqs, zero_rows, counts, radial):
    slots = zero_rows.shape[1]
    freq_float = freqs.astype(jnp.float32)[:, None, None]
    scaled = math.pi * (zero_rows.astype(jnp.float32)[:, :, None] + 0.5 * freq_float - 0.25)
    grid = (jnp.arange(radial, dtype=jnp.float32) + 0.5) / radial
    phase = scaled * grid[None, None, :] - 0.5 * math.pi * freq_float - 0.25 * math.pi
    keep = jnp.arange(slots, dtype=jnp.int32)[None, :, None] < counts[:, None, None]
    values = math.sqrt(2.0 / radial) * jnp.cos(phase)
    return jnp.where(keep, values, jnp.zeros_like(values)).astype(jnp.bfloat16)


def gram_of(blocks):
    return jnp.einsum("kvq,kvp->kqp", blocks, blocks, preferred_element_type=jnp.float32)


def shrink_from(gram, noise, vectors):
    width = gram.shape[1]
    eye = jnp.eye(width, dtype=jnp.float32)
    covariance = gram / vectors + noise[:, None, None] * eye
    lower = jnp.linalg.cholesky(covariance)
    inv_lower = jax.scipy.linalg.solve_triangular(
        lower, jnp.broadcast_to(eye, covariance.shape), lower=True
    )
    inverse = jnp.einsum("kmq,kmp->kqp", inv_lower, inv_lower, precision=lax.Precision.HIGHEST)
    return eye - noise[:, None, None] * inverse


def apply_shrink(shrinkage, blocks):
    return jnp.einsum(
        "kqp,kvp->kvq", shrinkage.astype(jnp.bfloat16), blocks, preferred_element_type=jnp.float32
    ).astype(jnp.bfloat16)


def per_device(images, radial_counts, order, zeros_table, noise_var):
    count_img, radial, angles = images.shape
    total_freq = order.shape[0]
    block = min(64, total_freq)
    nblocks = total_freq // block
    flat = images.reshape(count_img * radial, angles)
    slot_rows = jnp.take(zeros_table, order, axis=0)
    slot_counts = jnp.take(radial_counts, order)

    def block_tools(index):
        start = index * block
        freqs = lax.dynamic_slice_in_dim(order, start, block)
        table = make_table(freqs, angles)
        rows_here = lax.dynamic_slice_in_dim(slot_rows, start, block, 0)
        counts_here = lax.dynamic_slice_in_dim(slot_counts, start, block)
        return (table, make_basis(freqs, rows_here, counts_here, radial))

    def analyse(index):
        table, basis = block_tools(index)
        spectrum = jnp.dot(flat, table, preferred_element_type=jnp.float32)
        spectrum = spectrum.astype(jnp.bfloat16).reshape(count_img, radial, 2, block)
        return jnp.einsum(
            "ircj,jqr->jciq", spectrum, basis, preferred_element_type=jnp.float32
        ).astype(jnp.bfloat16)

    pieces = lax.map(analyse, jnp.arange(nblocks, dtype=jnp.int32))
    moved = pieces.reshape(total_freq, 2 * count_img, radial)
    owners = lax.axis_size("freq")
    owned = total_freq // owners
    batches = lax.axis_size("batch")
    mine = lax.dynamic_slice_in_dim(order, lax.axis_index("freq") * owned, owned)
    noise_mine = jnp.take(noise_var, mine)
    half_slots = owned // 2
    narrow = radial // 2
    grouped = moved.reshape(owners, owned, 2 * count_img, radial)
    lower_part = grouped[:, :half_slots].reshape(owners * half_slots, 2 * count_img, radial)
    upper_part = grouped[:, half_slots:, :, :narrow].reshape(
        owners * half_slots, 2 * count_img, narrow
    )
    low_recv, high_recv = (
        lax.all_to_all(lower_part, "freq", split_axis=0, concat_axis=1, tiled=True),
        lax.all_to_all(upper_part, "freq", split_axis=0, concat_axis=1, tiled=True),
    )
    gram_low, gram_high = lax.psum((gram_of(low_recv), gram_of(high_recv)), "batch")
    vectors = low_recv.shape[1] * batches
    shrink_lower = shrink_from(gram_low, noise_mine[:half_slots], vectors)
    shrink_upper = shrink_from(gram_high, noise_mine[half_slots:], vectors)
    low_back, high_back = (
        lax.all_to_all(
            apply_shrink(shrink_lower, low_recv), "freq", split_axis=1, concat_axis=0, tiled=True
        ),
        lax.all_to_all(
            apply_shrink(shrink_upper, high_recv), "freq", split_axis=1, concat_axis=0, tiled=True
        ),
    )
    high_wide = jnp.pad(high_back, ((0, 0), (0, 0), (0, radial - narrow)))
    returned = jnp.concatenate(
        [
            low_back.reshape(owners, half_slots, 2 * count_img, radial),
            high_wide.reshape(owners, half_slots, 2 * count_img, radial),
        ],
        axis=1,
    )
    returned = returned.reshape(total_freq, 2 * count_img, radial)
    upper_wide = jnp.pad(shrink_upper, ((0, 0), (0, radial - narrow), (0, radial - narrow)))
    wiener_blocks = jnp.concatenate([shrink_lower, upper_wide], axis=0)
    filtered_blocks = returned.reshape(nblocks, block, 2, count_img, radial)

    def synthesise(index, total):
        table, basis = block_tools(index)
        piece = lax.dynamic_index_in_dim(filtered_blocks, index, 0, keepdims=False)
        spectrum_out = jnp.einsum(
            "jciq,jqr->ircj", piece, basis, preferred_element_type=jnp.float32
        )
        spectrum_out = spectrum_out.astype(jnp.bfloat16).reshape(count_img * radial, 2 * block)
        return total + lax.dot_general(
            spectrum_out, table, (((1,), (1,)), ((), ())), preferred_element_type=jnp.float32
        )

    summed = lax.fori_loop(
        0, nblocks, synthesise, jnp.zeros((count_img * radial, angles), jnp.float32)
    )
    denoised = summed.astype(jnp.bfloat16).reshape(count_img, radial, angles)
    return (denoised, wiener_blocks)


COSINE = (
    -0.9999999889445799,
    4.934801116644238,
    -4.058694745523659,
    1.3351580223122241,
    -0.23502902263765682,
    0.025358285764913842,
    -0.0015936782168350142,
)


def cosine_of(turns, steps):
    x = ((turns & (steps - 1)) - steps // 2).astype(jnp.float32) * (2.0 / steps)
    y = x * x
    total = jnp.full_like(y, COSINE[-1])
    for term in COSINE[-2::-1]:
        total = total * y + term
    return total


def iota(shape, dim):
    return lax.broadcasted_iota(jnp.int32, shape, dim)


def nt(a, b):
    return lax.dot_general(a, b, (((1,), (1,)), ((), ())), preferred_element_type=jnp.float32)


def tn(a, b):
    return lax.dot_general(a, b, (((0,), (0,)), ((), ())), preferred_element_type=jnp.float32)


def nn(a, b):
    return jnp.dot(a, b, preferred_element_type=jnp.float32)


def low_bits(mask):
    return mask.astype(jnp.float32).astype(jnp.bfloat16)


class Plan:
    def __init__(self, images, order, owners, batches):
        self.count_img, self.radial, self.angles = images
        self.total = order
        self.owners, self.batches = owners, batches
        self.devices = owners * batches
        self.owned = order // owners
        self.half = self.owned // 2
        self.vecs = 2 * self.count_img
        self.quota = 4
        self.pairs = self.quota // 2
        self.narrow = self.radial // 2
        self.low_rows = self.vecs * self.quota
        self.rows = self.low_rows + self.vecs * self.pairs
        self.all_pairs = self.devices * self.pairs
        power = lambda n: n > 0 and n & (n - 1) == 0
        self.fits = (
            batches == 2
            and self.half == batches * self.quota
            and self.radial == 128
            and self.count_img == 4
            and all(power(n) for n in (self.angles, self.total, owners))
            and self.angles == 2 * self.total
        )

    def slot_of(self, device, place):
        batch, owner = device // self.owners, device & (self.owners - 1)
        return owner * self.owned + batch * self.quota + place


def analysis_kernel(
    plan, order_ref, counts_ref, zeros_ref, images_ref,
    coef_ref, table_ref, cb_ref, sb_ref, wave_ref, zero_ref, wide_ref,
):
    radial, angles, total = plan.radial, plan.angles, plan.total
    quota, pairs, narrow = plan.quota, plan.pairs, plan.narrow
    row = iota((2 * total, total), 0)
    high = row - total
    low_slot = plan.slot_of(row // (2 * quota), row & (quota - 1))
    pair = high & (plan.all_pairs - 1)
    side = high // (2 * plan.all_pairs)
    place = plan.half + 2 * (pair & (pairs - 1)) + side
    high_slot = plan.slot_of(pair // pairs, place)
    slot = jnp.where(row < total, low_slot, high_slot)
    pick = low_bits(slot == iota((2 * total, total), 1))
    spread = lambda ref: jnp.broadcast_to(ref[...].astype(jnp.float32), (128, total)).astype(jnp.bfloat16)
    held = spread(order_ref)
    freq = nt(pick, held).astype(jnp.int32)
    row = iota((2 * total, 128), 0)
    lane = iota((2 * total, 128), 1)
    sine_row = jnp.where(row < total, row // quota, row // plan.all_pairs) & 1
    lag = sine_row * (angles // 4)
    flip = (1 - 2 * (freq & 1)).astype(jnp.float32)
    factor = math.sqrt(2.0 / angles)
    for part in range(angles // 256):
        cosine = cosine_of((lane + part * 128) * freq - lag, angles) * factor
        table_ref[:, part * 128 : part * 128 + 128] = cosine.astype(jnp.bfloat16)
        start = angles // 2 + part * 128
        table_ref[:, start : start + 128] = (cosine * flip).astype(jnp.bfloat16)
    steps = 16 * radial
    turns = (2 * freq - 1) * (2 * lane + 1) - 4 * radial * freq - 2 * radial
    cb_ref[...] = cosine_of(turns, steps)
    sb_ref[...] = cosine_of(turns - steps // 4, steps)
    turns = (iota((radial, radial), 1) + 1) * (2 * iota((radial, radial), 0) + 1)
    factor = math.sqrt(2.0 / radial)
    wave_ref[0:radial, :] = (factor * cosine_of(turns, 4 * radial)).astype(jnp.bfloat16)
    wave_ref[radial : 2 * radial, :] = (-factor * cosine_of(turns - radial, 4 * radial)).astype(
        jnp.bfloat16
    )
    by_freq = low_bits(iota((total, total), 0) == iota((total, total), 1))
    counts = nt(by_freq, spread(counts_ref)).astype(jnp.int32)
    zeros = jnp.where(iota((total, radial), 1) < counts, zeros_ref[...], 0)
    zeros = zeros.astype(jnp.float32).astype(jnp.bfloat16)
    freq_lane = iota((plan.all_pairs, total), 1)
    sides = []
    for e in range(2):
        start = total + e * 2 * plan.all_pairs
        named = freq[start : start + plan.all_pairs]
        named = jnp.concatenate([named] * (total // 128), axis=1)
        sides.append(nn(low_bits(named == freq_lane), zeros))
    lane = iota((plan.all_pairs, radial), 1)
    zero_ref[...] = jnp.where(lane < narrow, sides[0], pltpu.roll(sides[1], narrow, axis=1)).astype(
        jnp.int32
    )
    images = images_ref[...].reshape(plan.count_img * radial, angles)
    for two in range(plan.count_img // 2):
        spectrum = nt(table_ref[...], images[2 * two * radial : 2 * (two + 1) * radial])
        lows = []
        for i in range(2):
            part = spectrum[:, i * radial : (i + 1) * radial]
            turned = jnp.concatenate(
                [(part * cb_ref[...]).astype(jnp.bfloat16), (part * sb_ref[...]).astype(jnp.bfloat16)],
                axis=1,
            )
            coef = nn(turned, wave_ref[...])
            lows.append(coef[:total].reshape(plan.devices, 2 * quota, radial))
            span = 2 * plan.all_pairs
            for e in range(2):
                at = (e * plan.count_img + 2 * two + i) * span
                wide_ref[at : at + span, :] = coef[total + e * span : total + (e + 1) * span]
        size = 4 * quota
        coef_ref[:, size * two : size * (two + 1), :] = jnp.concatenate(lows, axis=1).astype(
            jnp.bfloat16
        )
    lane = iota((plan.vecs, radial), 1)
    zero_here = iota((radial, radial), 0) + 1
    for device in range(plan.devices):
        tiles = []
        for i in range(pairs):
            at = device * pairs + i
            vectors = wide_ref[pl.ds(at, 2 * plan.vecs, stride=plan.all_pairs), :]
            chosen = low_bits(zero_here == zero_ref[at : at + 1, :])
            both = nn(vectors.astype(jnp.bfloat16), chosen)
            tiles.append(jnp.where(lane < narrow, both[: plan.vecs], both[plan.vecs :]))
        coef_ref[device, plan.low_rows : plan.rows, :] = jnp.concatenate(tiles, axis=0).astype(
            jnp.bfloat16
        )


def thirds(x):
    first = x.astype(jnp.bfloat16)
    rest = x - first.astype(jnp.float32)
    second = rest.astype(jnp.bfloat16)
    third = (rest - second.astype(jnp.float32)).astype(jnp.bfloat16)
    return first, second, third


def outer(u, v):
    u1, u2, u3 = thirds(u)
    v1, v2, v3 = thirds(v)
    return lax.dot_general(
        jnp.concatenate([u1, u1, u1, u2, u2, u3], axis=0),
        jnp.concatenate([v1, v2, v3, v1, v2, v1], axis=0),
        (((0,), (0,)), ((), ())),
        preferred_element_type=jnp.float32,
    )


def first_lane(halved, lane, step):
    return (lane & 64 if halved else jnp.zeros_like(lane)) + step * 8


def pivot_panels(panels, halves, step):
    shape = (8, 128)
    sub, lane = iota(shape, 0), iota(shape, 1)
    blocks = [
        [
            jnp.take_along_axis(panel, first_lane(halved, lane, step) + j, axis=1)
            for j in range(8)
        ]
        for panel, halved in zip(panels, halves)
    ]
    for i in range(8):
        for at, cols in enumerate(blocks):
            inverse = 1.0 / jnp.broadcast_to(cols[i][i : i + 1], shape)
            fresh = []
            for j in range(8):
                if j == i:
                    fresh.append(jnp.where(sub == i, inverse, -cols[i] * inverse))
                else:
                    line = jnp.broadcast_to(cols[j][i : i + 1], shape) * inverse
                    fresh.append(jnp.where(sub == i, line, cols[j] - cols[i] * line))
            blocks[at] = fresh
    solved = []
    for panel, halved, cols in zip(panels, halves, blocks):
        offset = lane - first_lane(halved, lane, step)
        outside = (offset < 0) | (offset >= 8)
        total = jnp.zeros(shape, jnp.float32)
        for j in range(8):
            line = jnp.broadcast_to(panel[j : j + 1], shape)
            line = jnp.where(outside, line, jnp.where(offset == j, 1.0, 0.0))
            total = total + cols[j] * line
        solved.append(total)
    return solved


def sweep(matrices, step, carry):
    start = pl.multiple_of(step * 8, 8)
    halves = [halved for _, _, halved in matrices]
    panels = [ref[m, pl.ds(start, 8), :] for ref, m, _ in matrices]
    solved = pivot_panels(panels, halves, step)
    for (ref, m, halved), panel, fresh in zip(matrices, panels, solved):
        height = ref.shape[1]
        lane = iota((8, 128), 1)
        done = (lane & 63 if halved else lane) < step * 8
        update = outer(jnp.where(done, -panel, panel), fresh)
        lane = iota((height, 128), 1)
        if halved:
            update = jnp.where(lane < 64, update[:height], update[height:])
        offset = lane - first_lane(halved, lane, step)
        rest = jnp.where((offset >= 0) & (offset < 8), 0.0, ref[m])
        ref[m] = rest - update
        ref[m, pl.ds(start, 8), :] = fresh
    return carry


def filter_kernel(
    plan, order_ref, noise_ref, counts_ref, zeros_ref, recv_ref,
    back_ref, shrink_ref, wide_ref, full_ref, pair_ref, pick_ref, held_ref,
):
    radial, quota, pairs, narrow = plan.radial, plan.quota, plan.pairs, plan.narrow
    low_rows = plan.low_rows
    rows = plan.devices * plan.vecs
    base = lax.axis_index("freq") * plan.owned + lax.axis_index("batch") * quota
    low_part = recv_ref[:, :low_rows, :].astype(jnp.float32)
    wide_ref[...] = low_part.reshape(plan.devices * low_rows, radial)
    square = (radial, radial)
    strip = (narrow, radial)
    eye = (iota(square, 0) == iota(square, 1)).astype(jnp.float32)
    twins = (iota(strip, 0) == (iota(strip, 1) & (narrow - 1))).astype(jnp.float32)
    first = iota(strip, 1) < narrow
    noises = []
    for s in range(quota):
        k = order_ref[base + s]
        noises.append(noise_ref[k])
        zero = zeros_ref[pl.ds(k, 1), :]
        zero = jnp.where(iota((1, radial), 1) < counts_ref[k], zero, 0)
        pick = low_bits(iota(square, 0) + 1 == zero)
        pick_ref[s] = pick
        vectors = wide_ref[pl.ds(s, rows, stride=quota), :].astype(jnp.bfloat16)
        coef = nn(vectors, pick).astype(jnp.bfloat16)
        full_ref[s] = tn(coef, coef) / float(rows) + noises[s] * eye
    high_part = recv_ref[:, low_rows:, :].astype(jnp.float32)
    for i in range(pairs):
        coef = high_part[:, i * plan.vecs : (i + 1) * plan.vecs, :].reshape(rows, radial)
        coef = coef.astype(jnp.bfloat16)
        held_ref[i] = coef
        gram = tn(coef, coef)
        gram = jnp.where(first, gram[:narrow], gram[narrow:])
        at = base + plan.half + 2 * i
        noise = jnp.where(first, noise_ref[order_ref[at]], noise_ref[order_ref[at + 1]])
        noises.append(noise)
        pair_ref[i] = gram / float(rows) + noise * twins
    lower = [(full_ref, m, False) for m in range(quota)]
    upper = [(pair_ref, m, True) for m in range(pairs)]
    lax.fori_loop(0, narrow // 8, functools.partial(sweep, lower + upper), 0)
    lax.fori_loop(narrow // 8, radial // 8, functools.partial(sweep, lower), 0)
    for s in range(quota):
        shrink = eye - noises[s] * full_ref[s]
        shrink_ref[s * radial : (s + 1) * radial, :] = shrink
        pick = pick_ref[s]
        moved = lax.dot_general(
            shrink.astype(jnp.bfloat16),
            pick,
            (((0,), (1,)), ((), ())),
            preferred_element_type=jnp.float32,
        ).astype(jnp.bfloat16)
        spread = nn(pick, moved).astype(jnp.bfloat16)
        vectors = wide_ref[pl.ds(s, rows, stride=quota), :].astype(jnp.bfloat16)
        wide_ref[pl.ds(s, rows, stride=quota), :] = nn(vectors, spread)
    shape = (plan.devices, low_rows, radial)
    back_ref[:, :low_rows, :] = wide_ref[...].reshape(shape).astype(jnp.bfloat16)
    tiles = []
    for i in range(pairs):
        shrink = twins - noises[quota + i] * pair_ref[i]
        start = quota * radial + i * narrow
        shrink_ref[start : start + narrow, :] = shrink
        blocks = jnp.concatenate(
            [jnp.where(first, shrink, 0.0), jnp.where(first, 0.0, shrink)], axis=0
        )
        filtered = nt(held_ref[i], blocks.astype(jnp.bfloat16))
        tiles.append(filtered.reshape(plan.devices, plan.vecs, radial))
    back_ref[:, low_rows:, :] = jnp.concatenate(tiles, axis=1).astype(jnp.bfloat16)


def synthesis_kernel(plan, table_ref, cb_ref, sb_ref, wave_ref, zero_ref, recv_ref, out_ref, wide_ref):
    radial, total, quota, pairs = plan.radial, plan.total, plan.quota, plan.pairs
    lane = iota((plan.vecs, radial), 1)
    zero_here = iota((radial, radial), 0) + 1
    for device in range(plan.devices):
        tile = recv_ref[device, plan.low_rows : plan.rows, :].astype(jnp.float32)
        for i in range(pairs):
            at = device * pairs + i
            packed = tile[i * plan.vecs : (i + 1) * plan.vecs]
            both = jnp.concatenate(
                [jnp.where(lane < plan.narrow, packed, 0.0), jnp.where(lane < plan.narrow, 0.0, packed)],
                axis=0,
            )
            chosen = low_bits(zero_here == zero_ref[at : at + 1, :])
            spread = nt(both.astype(jnp.bfloat16), chosen)
            wide_ref[pl.ds(at, 2 * plan.vecs, stride=plan.all_pairs), :] = spread
    span = 2 * plan.all_pairs
    for i in range(plan.count_img):
        low = recv_ref[:, 2 * quota * i : 2 * quota * (i + 1), :].astype(jnp.float32)
        at = [(e * plan.count_img + i) * span for e in range(2)]
        filtered = jnp.concatenate(
            [low.reshape(total, radial)] + [wide_ref[a : a + span, :] for a in at], axis=0
        )
        turned = nt(filtered.astype(jnp.bfloat16), wave_ref[...])
        spectrum = turned[:, :radial] * cb_ref[...] + turned[:, radial:] * sb_ref[...]
        out_ref[i] = tn(spectrum.astype(jnp.bfloat16), table_ref[...]).astype(jnp.bfloat16)


def wiener_kernel(plan, own_ref, other_ref, out_ref):
    radial, quota, narrow = plan.radial, plan.quota, plan.narrow
    batch_at = lax.axis_index("batch")
    lane = iota((narrow, radial), 1)
    for batch, ref in ((batch_at, own_ref), (1 - batch_at, other_ref)):
        for s in range(quota):
            out_ref[batch * quota + s] = ref[s * radial : (s + 1) * radial, :]
            at = plan.half + batch * quota + s
            start = quota * radial + (s // 2) * narrow
            pair = ref[start : start + narrow, :]
            if s % 2:
                pair = pltpu.roll(pair, narrow, axis=1)
            out_ref[at, 0:narrow, :] = jnp.where(lane < narrow, pair, 0.0)
            out_ref[at, narrow:radial, :] = jnp.zeros((radial - narrow, radial), jnp.float32)


VMEM = pl.BlockSpec(memory_space=pltpu.VMEM)
SMEM = pl.BlockSpec(memory_space=pltpu.SMEM)


def call(kernel, outs, ins, scratch=()):
    return pl.pallas_call(
        kernel,
        out_shape=outs,
        in_specs=ins,
        out_specs=jax.tree.map(lambda _: VMEM, outs),
        scratch_shapes=scratch,
    )


def fast_device(plan, images, radial_counts, order, zeros_table, noise_var):
    both = ("batch", "freq")
    radial, total, quota, pairs = plan.radial, plan.total, plan.quota, plan.pairs
    shape = jax.ShapeDtypeStruct
    block = shape((plan.devices, plan.rows, radial), jnp.bfloat16)
    coef, table, cb, sb, wave, zero = call(
        functools.partial(analysis_kernel, plan),
        (
            block,
            shape((2 * total, plan.angles), jnp.bfloat16),
            shape((2 * total, radial), jnp.float32),
            shape((2 * total, radial), jnp.float32),
            shape((2 * radial, radial), jnp.bfloat16),
            shape((plan.all_pairs, radial), jnp.int32),
        ),
        [VMEM] * 4,
        [pltpu.VMEM((2 * plan.vecs * plan.all_pairs, radial), jnp.float32)],
    )(order.reshape(1, total), radial_counts.reshape(1, total), zeros_table, images)
    recv = lax.all_to_all(coef, both, split_axis=0, concat_axis=0, tiled=True)
    back, shrink = call(
        functools.partial(filter_kernel, plan),
        (block, shape((quota * radial + pairs * plan.narrow, radial), jnp.float32)),
        [SMEM, SMEM, SMEM, VMEM, VMEM],
        [
            pltpu.VMEM((plan.devices * plan.low_rows, radial), jnp.float32),
            pltpu.VMEM((quota, radial, radial), jnp.float32),
            pltpu.VMEM((pairs, plan.narrow, radial), jnp.float32),
            pltpu.VMEM((quota, radial, radial), jnp.bfloat16),
            pltpu.VMEM((pairs, plan.devices * plan.vecs, radial), jnp.bfloat16),
        ],
    )(order, noise_var, radial_counts, zeros_table, recv)
    returned = lax.all_to_all(back, both, split_axis=0, concat_axis=0, tiled=True)
    other = lax.ppermute(shrink, "batch", [(0, 1), (1, 0)])
    wiener_blocks = call(
        functools.partial(wiener_kernel, plan),
        shape((plan.owned, radial, radial), jnp.float32),
        [VMEM] * 2,
    )(shrink, other)
    denoised = call(
        functools.partial(synthesis_kernel, plan),
        shape((plan.count_img, radial, plan.angles), jnp.bfloat16),
        [VMEM] * 6,
        [pltpu.VMEM((2 * plan.vecs * plan.all_pairs, radial), jnp.float32)],
    )(table, cb, sb, wave, zero, returned)
    return denoised, wiener_blocks


def solution(mesh):
    owners, batches = mesh.shape["freq"], mesh.shape["batch"]

    def body(images, radial_counts, order, zeros_table, noise_var):
        plan = Plan(images.shape, order.shape[0], owners, batches)
        device = functools.partial(fast_device, plan) if plan.fits else per_device
        return device(images, radial_counts, order, zeros_table, noise_var)

    return jax.shard_map(
        body,
        mesh=mesh,
        in_specs=(P(("batch", "freq"), None, None), P(), P(), P(), P()),
        out_specs=(P(("batch", "freq"), None, None), P("freq", None, None)),
        check_vma=False,
    )
```

```python
import functools
import math

import jax
import jax.numpy as jnp
from jax import lax
from jax.experimental import pallas as pl
from jax.experimental.pallas import tpu as pltpu
from jax.sharding import PartitionSpec as P


def make_table(freqs, angles):
    angle_index = jnp.arange(angles, dtype=jnp.int32)
    product = angle_index[:, None] * freqs[None, :] % angles
    phase = 2.0 * math.pi / angles * product.astype(jnp.float32)
    factor = math.sqrt(2.0 / angles)
    return jnp.concatenate([factor * jnp.cos(phase), factor * jnp.sin(phase)], axis=1).astype(
        jnp.bfloat16
    )


def make_basis(freqs, zero_rows, counts, radial):
    slots = zero_rows.shape[1]
    freq_float = freqs.astype(jnp.float32)[:, None, None]
    scaled = math.pi * (zero_rows.astype(jnp.float32)[:, :, None] + 0.5 * freq_float - 0.25)
    grid = (jnp.arange(radial, dtype=jnp.float32) + 0.5) / radial
    phase = scaled * grid[None, None, :] - 0.5 * math.pi * freq_float - 0.25 * math.pi
    keep = jnp.arange(slots, dtype=jnp.int32)[None, :, None] < counts[:, None, None]
    values = math.sqrt(2.0 / radial) * jnp.cos(phase)
    return jnp.where(keep, values, jnp.zeros_like(values)).astype(jnp.bfloat16)


def gram_of(blocks):
    return jnp.einsum("kvq,kvp->kqp", blocks, blocks, preferred_element_type=jnp.float32)


def shrink_from(gram, noise, vectors):
    width = gram.shape[1]
    eye = jnp.eye(width, dtype=jnp.float32)
    covariance = gram / vectors + noise[:, None, None] * eye
    lower = jnp.linalg.cholesky(covariance)
    inv_lower = jax.scipy.linalg.solve_triangular(
        lower, jnp.broadcast_to(eye, covariance.shape), lower=True
    )
    inverse = jnp.einsum("kmq,kmp->kqp", inv_lower, inv_lower, precision=lax.Precision.HIGHEST)
    return eye - noise[:, None, None] * inverse


def apply_shrink(shrinkage, blocks):
    return jnp.einsum(
        "kqp,kvp->kvq", shrinkage.astype(jnp.bfloat16), blocks, preferred_element_type=jnp.float32
    ).astype(jnp.bfloat16)


def per_device(images, radial_counts, order, zeros_table, noise_var):
    count_img, radial, angles = images.shape
    total_freq = order.shape[0]
    block = min(64, total_freq)
    nblocks = total_freq // block
    flat = images.reshape(count_img * radial, angles)
    slot_rows = jnp.take(zeros_table, order, axis=0)
    slot_counts = jnp.take(radial_counts, order)

    def block_tools(index):
        start = index * block
        freqs = lax.dynamic_slice_in_dim(order, start, block)
        table = make_table(freqs, angles)
        rows_here = lax.dynamic_slice_in_dim(slot_rows, start, block, 0)
        counts_here = lax.dynamic_slice_in_dim(slot_counts, start, block)
        return (table, make_basis(freqs, rows_here, counts_here, radial))

    def analyse(index):
        table, basis = block_tools(index)
        spectrum = jnp.dot(flat, table, preferred_element_type=jnp.float32)
        spectrum = spectrum.astype(jnp.bfloat16).reshape(count_img, radial, 2, block)
        return jnp.einsum(
            "ircj,jqr->jciq", spectrum, basis, preferred_element_type=jnp.float32
        ).astype(jnp.bfloat16)

    pieces = lax.map(analyse, jnp.arange(nblocks, dtype=jnp.int32))
    moved = pieces.reshape(total_freq, 2 * count_img, radial)
    owners = lax.axis_size("freq")
    owned = total_freq // owners
    batches = lax.axis_size("batch")
    mine = lax.dynamic_slice_in_dim(order, lax.axis_index("freq") * owned, owned)
    noise_mine = jnp.take(noise_var, mine)
    half_slots = owned // 2
    narrow = radial // 2
    grouped = moved.reshape(owners, owned, 2 * count_img, radial)
    lower_part = grouped[:, :half_slots].reshape(owners * half_slots, 2 * count_img, radial)
    upper_part = grouped[:, half_slots:, :, :narrow].reshape(
        owners * half_slots, 2 * count_img, narrow
    )
    low_recv, high_recv = (
        lax.all_to_all(lower_part, "freq", split_axis=0, concat_axis=1, tiled=True),
        lax.all_to_all(upper_part, "freq", split_axis=0, concat_axis=1, tiled=True),
    )
    gram_low, gram_high = lax.psum((gram_of(low_recv), gram_of(high_recv)), "batch")
    vectors = low_recv.shape[1] * batches
    shrink_lower = shrink_from(gram_low, noise_mine[:half_slots], vectors)
    shrink_upper = shrink_from(gram_high, noise_mine[half_slots:], vectors)
    low_back, high_back = (
        lax.all_to_all(
            apply_shrink(shrink_lower, low_recv), "freq", split_axis=1, concat_axis=0, tiled=True
        ),
        lax.all_to_all(
            apply_shrink(shrink_upper, high_recv), "freq", split_axis=1, concat_axis=0, tiled=True
        ),
    )
    high_wide = jnp.pad(high_back, ((0, 0), (0, 0), (0, radial - narrow)))
    returned = jnp.concatenate(
        [
            low_back.reshape(owners, half_slots, 2 * count_img, radial),
            high_wide.reshape(owners, half_slots, 2 * count_img, radial),
        ],
        axis=1,
    )
    returned = returned.reshape(total_freq, 2 * count_img, radial)
    upper_wide = jnp.pad(shrink_upper, ((0, 0), (0, radial - narrow), (0, radial - narrow)))
    wiener_blocks = jnp.concatenate([shrink_lower, upper_wide], axis=0)
    filtered_blocks = returned.reshape(nblocks, block, 2, count_img, radial)

    def synthesise(index, total):
        table, basis = block_tools(index)
        piece = lax.dynamic_index_in_dim(filtered_blocks, index, 0, keepdims=False)
        spectrum_out = jnp.einsum(
            "jciq,jqr->ircj", piece, basis, preferred_element_type=jnp.float32
        )
        spectrum_out = spectrum_out.astype(jnp.bfloat16).reshape(count_img * radial, 2 * block)
        return total + lax.dot_general(
            spectrum_out, table, (((1,), (1,)), ((), ())), preferred_element_type=jnp.float32
        )

    summed = lax.fori_loop(
        0, nblocks, synthesise, jnp.zeros((count_img * radial, angles), jnp.float32)
    )
    denoised = summed.astype(jnp.bfloat16).reshape(count_img, radial, angles)
    return (denoised, wiener_blocks)


COSINE = (
    -0.9999999889445799,
    4.934801116644238,
    -4.058694745523659,
    1.3351580223122241,
    -0.23502902263765682,
    0.025358285764913842,
    -0.0015936782168350142,
)


def cosine_of(turns, steps):
    x = ((turns & (steps - 1)) - steps // 2).astype(jnp.float32) * (2.0 / steps)
    y = x * x
    total = jnp.full_like(y, COSINE[-1])
    for term in COSINE[-2::-1]:
        total = total * y + term
    return total


def iota(shape, dim):
    return lax.broadcasted_iota(jnp.int32, shape, dim)


def nt(a, b):
    return lax.dot_general(a, b, (((1,), (1,)), ((), ())), preferred_element_type=jnp.float32)


def tn(a, b):
    return lax.dot_general(a, b, (((0,), (0,)), ((), ())), preferred_element_type=jnp.float32)


def nn(a, b):
    return jnp.dot(a, b, preferred_element_type=jnp.float32)


def low_bits(mask):
    return mask.astype(jnp.float32).astype(jnp.bfloat16)


class Plan:
    def __init__(self, images, order, owners, batches):
        self.count_img, self.radial, self.angles = images
        self.total = order
        self.owners, self.batches = owners, batches
        self.devices = owners * batches
        self.owned = order // owners
        self.half = self.owned // 2
        self.vecs = 2 * self.count_img
        self.quota = 4
        self.pairs = self.quota // 2
        self.narrow = self.radial // 2
        self.low_rows = self.vecs * self.quota
        self.rows = self.low_rows + self.vecs * self.pairs
        self.all_pairs = self.devices * self.pairs
        power = lambda n: n > 0 and n & (n - 1) == 0
        self.fits = (
            batches == 2
            and self.half == batches * self.quota
            and self.radial == 128
            and self.count_img == 4
            and all(power(n) for n in (self.angles, self.total, owners))
            and self.angles == 2 * self.total
        )

    def slot_of(self, device, place):
        batch, owner = device // self.owners, device & (self.owners - 1)
        return owner * self.owned + batch * self.quota + place


def analysis_kernel(
    plan, order_ref, counts_ref, zeros_ref, images_ref,
    coef_ref, table_ref, cb_ref, sb_ref, wave_ref, zero_ref, wide_ref,
):
    radial, angles, total = plan.radial, plan.angles, plan.total
    quota, pairs, narrow = plan.quota, plan.pairs, plan.narrow
    row = iota((2 * total, total), 0)
    high = row - total
    low_slot = plan.slot_of(row // (2 * quota), row & (quota - 1))
    pair = high & (plan.all_pairs - 1)
    side = high // (2 * plan.all_pairs)
    place = plan.half + 2 * (pair & (pairs - 1)) + side
    high_slot = plan.slot_of(pair // pairs, place)
    slot = jnp.where(row < total, low_slot, high_slot)
    pick = low_bits(slot == iota((2 * total, total), 1))
    spread = lambda ref: jnp.broadcast_to(ref[...].astype(jnp.float32), (128, total)).astype(jnp.bfloat16)
    held = spread(order_ref)
    freq = nt(pick, held).astype(jnp.int32)
    row = iota((2 * total, 128), 0)
    lane = iota((2 * total, 128), 1)
    sine_row = jnp.where(row < total, row // quota, row // plan.all_pairs) & 1
    lag = sine_row * (angles // 4)
    flip = (1 - 2 * (freq & 1)).astype(jnp.float32)
    factor = math.sqrt(2.0 / angles)
    for part in range(angles // 256):
        cosine = cosine_of((lane + part * 128) * freq - lag, angles) * factor
        table_ref[:, part * 128 : part * 128 + 128] = cosine.astype(jnp.bfloat16)
        start = angles // 2 + part * 128
        table_ref[:, start : start + 128] = (cosine * flip).astype(jnp.bfloat16)
    steps = 16 * radial
    turns = (2 * freq - 1) * (2 * lane + 1) - 4 * radial * freq - 2 * radial
    cb_ref[...] = cosine_of(turns, steps)
    sb_ref[...] = cosine_of(turns - steps // 4, steps)
    turns = (iota((radial, radial), 1) + 1) * (2 * iota((radial, radial), 0) + 1)
    factor = math.sqrt(2.0 / radial)
    wave_ref[0:radial, :] = (factor * cosine_of(turns, 4 * radial)).astype(jnp.bfloat16)
    wave_ref[radial : 2 * radial, :] = (-factor * cosine_of(turns - radial, 4 * radial)).astype(
        jnp.bfloat16
    )
    by_freq = low_bits(iota((total, total), 0) == iota((total, total), 1))
    counts = nt(by_freq, spread(counts_ref)).astype(jnp.int32)
    zeros = jnp.where(iota((total, radial), 1) < counts, zeros_ref[...], 0)
    zeros = zeros.astype(jnp.float32).astype(jnp.bfloat16)
    freq_lane = iota((plan.all_pairs, total), 1)
    sides = []
    for e in range(2):
        start = total + e * 2 * plan.all_pairs
        named = freq[start : start + plan.all_pairs]
        named = jnp.concatenate([named] * (total // 128), axis=1)
        sides.append(nn(low_bits(named == freq_lane), zeros))
    lane = iota((plan.all_pairs, radial), 1)
    zero_ref[...] = jnp.where(lane < narrow, sides[0], pltpu.roll(sides[1], narrow, axis=1)).astype(
        jnp.int32
    )
    images = images_ref[...].reshape(plan.count_img * radial, angles)
    for two in range(plan.count_img // 2):
        spectrum = nt(table_ref[...], images[2 * two * radial : 2 * (two + 1) * radial])
        lows = []
        for i in range(2):
            part = spectrum[:, i * radial : (i + 1) * radial]
            turned = jnp.concatenate(
                [(part * cb_ref[...]).astype(jnp.bfloat16), (part * sb_ref[...]).astype(jnp.bfloat16)],
                axis=1,
            )
            coef = nn(turned, wave_ref[...])
            lows.append(coef[:total].reshape(plan.devices, 2 * quota, radial))
            span = 2 * plan.all_pairs
            for e in range(2):
                at = (e * plan.count_img + 2 * two + i) * span
                wide_ref[at : at + span, :] = coef[total + e * span : total + (e + 1) * span]
        size = 4 * quota
        coef_ref[:, size * two : size * (two + 1), :] = jnp.concatenate(lows, axis=1).astype(
            jnp.bfloat16
        )
    lane = iota((plan.vecs, radial), 1)
    zero_here = iota((radial, radial), 0) + 1
    for device in range(plan.devices):
        tiles = []
        for i in range(pairs):
            at = device * pairs + i
            vectors = wide_ref[pl.ds(at, 2 * plan.vecs, stride=plan.all_pairs), :]
            chosen = low_bits(zero_here == zero_ref[at : at + 1, :])
            both = nn(vectors.astype(jnp.bfloat16), chosen)
            tiles.append(jnp.where(lane < narrow, both[: plan.vecs], both[plan.vecs :]))
        coef_ref[device, plan.low_rows : plan.rows, :] = jnp.concatenate(tiles, axis=0).astype(
            jnp.bfloat16
        )


def thirds(x):
    first = x.astype(jnp.bfloat16)
    rest = x - first.astype(jnp.float32)
    second = rest.astype(jnp.bfloat16)
    third = (rest - second.astype(jnp.float32)).astype(jnp.bfloat16)
    return first, second, third


def outer(u, v):
    u1, u2, u3 = thirds(u)
    v1, v2, v3 = thirds(v)
    return lax.dot_general(
        jnp.concatenate([u1, u1, u1, u2, u2, u3], axis=0),
        jnp.concatenate([v1, v2, v3, v1, v2, v1], axis=0),
        (((0,), (0,)), ((), ())),
        preferred_element_type=jnp.float32,
    )


def first_lane(halved, lane, step):
    return (lane & 64 if halved else jnp.zeros_like(lane)) + step * 8


def pivot_panels(panels, halves, step):
    shape = (8, 128)
    sub, lane = iota(shape, 0), iota(shape, 1)
    blocks = [
        [
            jnp.take_along_axis(panel, first_lane(halved, lane, step) + j, axis=1)
            for j in range(8)
        ]
        for panel, halved in zip(panels, halves)
    ]
    for i in range(8):
        for at, cols in enumerate(blocks):
            inverse = 1.0 / jnp.broadcast_to(cols[i][i : i + 1], shape)
            fresh = []
            for j in range(8):
                if j == i:
                    fresh.append(jnp.where(sub == i, inverse, -cols[i] * inverse))
                else:
                    line = jnp.broadcast_to(cols[j][i : i + 1], shape) * inverse
                    fresh.append(jnp.where(sub == i, line, cols[j] - cols[i] * line))
            blocks[at] = fresh
    solved = []
    for panel, halved, cols in zip(panels, halves, blocks):
        offset = lane - first_lane(halved, lane, step)
        outside = (offset < 0) | (offset >= 8)
        total = jnp.zeros(shape, jnp.float32)
        for j in range(8):
            line = jnp.broadcast_to(panel[j : j + 1], shape)
            line = jnp.where(outside, line, jnp.where(offset == j, 1.0, 0.0))
            total = total + cols[j] * line
        solved.append(total)
    return solved


def sweep(matrices, step, carry):
    start = pl.multiple_of(step * 8, 8)
    halves = [halved for _, _, halved in matrices]
    panels = [ref[m, pl.ds(start, 8), :] for ref, m, _ in matrices]
    solved = pivot_panels(panels, halves, step)
    for (ref, m, halved), panel, fresh in zip(matrices, panels, solved):
        height = ref.shape[1]
        lane = iota((8, 128), 1)
        done = (lane & 63 if halved else lane) < step * 8
        update = outer(jnp.where(done, -panel, panel), fresh)
        lane = iota((height, 128), 1)
        if halved:
            update = jnp.where(lane < 64, update[:height], update[height:])
        offset = lane - first_lane(halved, lane, step)
        rest = jnp.where((offset >= 0) & (offset < 8), 0.0, ref[m])
        ref[m] = rest - update
        ref[m, pl.ds(start, 8), :] = fresh
    return carry


def filter_kernel(
    plan, order_ref, noise_ref, counts_ref, zeros_ref, recv_ref,
    back_ref, shrink_ref, wide_ref, full_ref, pair_ref, pick_ref, held_ref,
):
    radial, quota, pairs, narrow = plan.radial, plan.quota, plan.pairs, plan.narrow
    low_rows = plan.low_rows
    rows = plan.devices * plan.vecs
    base = lax.axis_index("freq") * plan.owned + lax.axis_index("batch") * quota
    low_part = recv_ref[:, :low_rows, :].astype(jnp.float32)
    wide_ref[...] = low_part.reshape(plan.devices * low_rows, radial)
    square = (radial, radial)
    strip = (narrow, radial)
    eye = (iota(square, 0) == iota(square, 1)).astype(jnp.float32)
    twins = (iota(strip, 0) == (iota(strip, 1) & (narrow - 1))).astype(jnp.float32)
    first = iota(strip, 1) < narrow
    noises = []
    for s in range(quota):
        k = order_ref[base + s]
        noises.append(noise_ref[k])
        zero = zeros_ref[pl.ds(k, 1), :]
        zero = jnp.where(iota((1, radial), 1) < counts_ref[k], zero, 0)
        pick = low_bits(iota(square, 0) + 1 == zero)
        pick_ref[s] = pick
        vectors = wide_ref[pl.ds(s, rows, stride=quota), :].astype(jnp.bfloat16)
        coef = nn(vectors, pick).astype(jnp.bfloat16)
        full_ref[s] = tn(coef, coef) / float(rows) + noises[s] * eye
    high_part = recv_ref[:, low_rows:, :].astype(jnp.float32)
    for i in range(pairs):
        coef = high_part[:, i * plan.vecs : (i + 1) * plan.vecs, :].reshape(rows, radial)
        coef = coef.astype(jnp.bfloat16)
        held_ref[i] = coef
        gram = tn(coef, coef)
        gram = jnp.where(first, gram[:narrow], gram[narrow:])
        at = base + plan.half + 2 * i
        noise = jnp.where(first, noise_ref[order_ref[at]], noise_ref[order_ref[at + 1]])
        noises.append(noise)
        pair_ref[i] = gram / float(rows) + noise * twins
    lower = [(full_ref, m, False) for m in range(quota)]
    upper = [(pair_ref, m, True) for m in range(pairs)]
    lax.fori_loop(0, narrow // 8, functools.partial(sweep, lower + upper), 0)
    lax.fori_loop(narrow // 8, radial // 8, functools.partial(sweep, lower), 0)
    for s in range(quota):
        shrink = eye - noises[s] * full_ref[s]
        shrink_ref[s * radial : (s + 1) * radial, :] = shrink.astype(jnp.bfloat16)
        pick = pick_ref[s]
        moved = lax.dot_general(
            shrink.astype(jnp.bfloat16),
            pick,
            (((0,), (1,)), ((), ())),
            preferred_element_type=jnp.float32,
        ).astype(jnp.bfloat16)
        spread = nn(pick, moved).astype(jnp.bfloat16)
        vectors = wide_ref[pl.ds(s, rows, stride=quota), :].astype(jnp.bfloat16)
        wide_ref[pl.ds(s, rows, stride=quota), :] = nn(vectors, spread)
    shape = (plan.devices, low_rows, radial)
    back_ref[:, :low_rows, :] = wide_ref[...].reshape(shape).astype(jnp.bfloat16)
    tiles = []
    for i in range(pairs):
        shrink = twins - noises[quota + i] * pair_ref[i]
        start = quota * radial + i * narrow
        shrink_ref[start : start + narrow, :] = shrink.astype(jnp.bfloat16)
        blocks = jnp.concatenate(
            [jnp.where(first, shrink, 0.0), jnp.where(first, 0.0, shrink)], axis=0
        )
        filtered = nt(held_ref[i], blocks.astype(jnp.bfloat16))
        tiles.append(filtered.reshape(plan.devices, plan.vecs, radial))
    back_ref[:, low_rows:, :] = jnp.concatenate(tiles, axis=1).astype(jnp.bfloat16)


def synthesis_kernel(plan, table_ref, cb_ref, sb_ref, wave_ref, zero_ref, recv_ref, out_ref, wide_ref):
    radial, total, quota, pairs = plan.radial, plan.total, plan.quota, plan.pairs
    lane = iota((plan.vecs, radial), 1)
    zero_here = iota((radial, radial), 0) + 1
    for device in range(plan.devices):
        tile = recv_ref[device, plan.low_rows : plan.rows, :].astype(jnp.float32)
        for i in range(pairs):
            at = device * pairs + i
            packed = tile[i * plan.vecs : (i + 1) * plan.vecs]
            both = jnp.concatenate(
                [jnp.where(lane < plan.narrow, packed, 0.0), jnp.where(lane < plan.narrow, 0.0, packed)],
                axis=0,
            )
            chosen = low_bits(zero_here == zero_ref[at : at + 1, :])
            spread = nt(both.astype(jnp.bfloat16), chosen)
            wide_ref[pl.ds(at, 2 * plan.vecs, stride=plan.all_pairs), :] = spread
    span = 2 * plan.all_pairs
    for i in range(plan.count_img):
        low = recv_ref[:, 2 * quota * i : 2 * quota * (i + 1), :].astype(jnp.float32)
        at = [(e * plan.count_img + i) * span for e in range(2)]
        filtered = jnp.concatenate(
            [low.reshape(total, radial)] + [wide_ref[a : a + span, :] for a in at], axis=0
        )
        turned = nt(filtered.astype(jnp.bfloat16), wave_ref[...])
        spectrum = turned[:, :radial] * cb_ref[...] + turned[:, radial:] * sb_ref[...]
        out_ref[i] = tn(spectrum.astype(jnp.bfloat16), table_ref[...]).astype(jnp.bfloat16)


def wiener_kernel(plan, own_ref, other_ref, out_ref):
    radial, quota, narrow = plan.radial, plan.quota, plan.narrow
    batch_at = lax.axis_index("batch")
    lane = iota((narrow, radial), 1)
    for batch, ref in ((batch_at, own_ref), (1 - batch_at, other_ref)):
        for s in range(quota):
            out_ref[batch * quota + s] = ref[s * radial : (s + 1) * radial, :].astype(jnp.float32)
            at = plan.half + batch * quota + s
            start = quota * radial + (s // 2) * narrow
            pair = ref[start : start + narrow, :].astype(jnp.float32)
            if s % 2:
                pair = pltpu.roll(pair, narrow, axis=1)
            out_ref[at, 0:narrow, :] = jnp.where(lane < narrow, pair, 0.0)
            out_ref[at, narrow:radial, :] = jnp.zeros((radial - narrow, radial), jnp.float32)


VMEM = pl.BlockSpec(memory_space=pltpu.VMEM)
SMEM = pl.BlockSpec(memory_space=pltpu.SMEM)


def call(kernel, outs, ins, scratch=()):
    return pl.pallas_call(
        kernel,
        out_shape=outs,
        in_specs=ins,
        out_specs=jax.tree.map(lambda _: VMEM, outs),
        scratch_shapes=scratch,
        compiler_params=pltpu.CompilerParams(vmem_limit_bytes=16 << 20),
    )


def fast_device(plan, images, radial_counts, order, zeros_table, noise_var):
    both = ("batch", "freq")
    radial, total, quota, pairs = plan.radial, plan.total, plan.quota, plan.pairs
    shape = jax.ShapeDtypeStruct
    block = shape((plan.devices, plan.rows, radial), jnp.bfloat16)
    coef, table, cb, sb, wave, zero = call(
        functools.partial(analysis_kernel, plan),
        (
            block,
            shape((2 * total, plan.angles), jnp.bfloat16),
            shape((2 * total, radial), jnp.float32),
            shape((2 * total, radial), jnp.float32),
            shape((2 * radial, radial), jnp.bfloat16),
            shape((plan.all_pairs, radial), jnp.int32),
        ),
        [VMEM] * 4,
        [pltpu.VMEM((2 * plan.vecs * plan.all_pairs, radial), jnp.float32)],
    )(order.reshape(1, total), radial_counts.reshape(1, total), zeros_table, images)
    recv = lax.all_to_all(coef, both, split_axis=0, concat_axis=0, tiled=True)
    back, shrink = call(
        functools.partial(filter_kernel, plan),
        (block, shape((quota * radial + pairs * plan.narrow, radial), jnp.bfloat16)),
        [SMEM, SMEM, SMEM, VMEM, VMEM],
        [
            pltpu.VMEM((plan.devices * plan.low_rows, radial), jnp.float32),
            pltpu.VMEM((quota, radial, radial), jnp.float32),
            pltpu.VMEM((pairs, plan.narrow, radial), jnp.float32),
            pltpu.VMEM((quota, radial, radial), jnp.bfloat16),
            pltpu.VMEM((pairs, plan.devices * plan.vecs, radial), jnp.bfloat16),
        ],
    )(order, noise_var, radial_counts, zeros_table, recv)
    returned = lax.all_to_all(back, both, split_axis=0, concat_axis=0, tiled=True)
    other = lax.ppermute(shrink, "batch", [(0, 1), (1, 0)])
    wiener_blocks = call(
        functools.partial(wiener_kernel, plan),
        shape((plan.owned, radial, radial), jnp.float32),
        [VMEM] * 2,
    )(shrink, other)
    denoised = call(
        functools.partial(synthesis_kernel, plan),
        shape((plan.count_img, radial, plan.angles), jnp.bfloat16),
        [VMEM] * 6,
        [pltpu.VMEM((2 * plan.vecs * plan.all_pairs, radial), jnp.float32)],
    )(table, cb, sb, wave, zero, returned)
    return denoised, wiener_blocks


def solution(mesh):
    owners, batches = mesh.shape["freq"], mesh.shape["batch"]

    def body(images, radial_counts, order, zeros_table, noise_var):
        plan = Plan(images.shape, order.shape[0], owners, batches)
        device = functools.partial(fast_device, plan) if plan.fits else per_device
        return device(images, radial_counts, order, zeros_table, noise_var)

    return jax.shard_map(
        body,
        mesh=mesh,
        in_specs=(P(("batch", "freq"), None, None), P(), P(), P(), P()),
        out_specs=(P(("batch", "freq"), None, None), P("freq", None, None)),
        check_vma=False,
    )
```

```python
import functools
import math

import jax
import jax.numpy as jnp
from jax import lax
from jax.experimental import pallas as pl
from jax.experimental.pallas import tpu as pltpu
from jax.sharding import PartitionSpec as P


def make_table(freqs, angles):
    angle_index = jnp.arange(angles, dtype=jnp.int32)
    product = angle_index[:, None] * freqs[None, :] % angles
    phase = 2.0 * math.pi / angles * product.astype(jnp.float32)
    factor = math.sqrt(2.0 / angles)
    return jnp.concatenate([factor * jnp.cos(phase), factor * jnp.sin(phase)], axis=1).astype(
        jnp.bfloat16
    )


def make_basis(freqs, zero_rows, counts, radial):
    slots = zero_rows.shape[1]
    freq_float = freqs.astype(jnp.float32)[:, None, None]
    scaled = math.pi * (zero_rows.astype(jnp.float32)[:, :, None] + 0.5 * freq_float - 0.25)
    grid = (jnp.arange(radial, dtype=jnp.float32) + 0.5) / radial
    phase = scaled * grid[None, None, :] - 0.5 * math.pi * freq_float - 0.25 * math.pi
    keep = jnp.arange(slots, dtype=jnp.int32)[None, :, None] < counts[:, None, None]
    values = math.sqrt(2.0 / radial) * jnp.cos(phase)
    return jnp.where(keep, values, jnp.zeros_like(values)).astype(jnp.bfloat16)


def gram_of(blocks):
    return jnp.einsum("kvq,kvp->kqp", blocks, blocks, preferred_element_type=jnp.float32)


def shrink_from(gram, noise, vectors):
    width = gram.shape[1]
    eye = jnp.eye(width, dtype=jnp.float32)
    covariance = gram / vectors + noise[:, None, None] * eye
    lower = jnp.linalg.cholesky(covariance)
    inv_lower = jax.scipy.linalg.solve_triangular(
        lower, jnp.broadcast_to(eye, covariance.shape), lower=True
    )
    inverse = jnp.einsum("kmq,kmp->kqp", inv_lower, inv_lower, precision=lax.Precision.HIGHEST)
    return eye - noise[:, None, None] * inverse


def apply_shrink(shrinkage, blocks):
    return jnp.einsum(
        "kqp,kvp->kvq", shrinkage.astype(jnp.bfloat16), blocks, preferred_element_type=jnp.float32
    ).astype(jnp.bfloat16)


def per_device(images, radial_counts, order, zeros_table, noise_var):
    count_img, radial, angles = images.shape
    total_freq = order.shape[0]
    block = min(64, total_freq)
    nblocks = total_freq // block
    flat = images.reshape(count_img * radial, angles)
    slot_rows = jnp.take(zeros_table, order, axis=0)
    slot_counts = jnp.take(radial_counts, order)

    def block_tools(index):
        start = index * block
        freqs = lax.dynamic_slice_in_dim(order, start, block)
        table = make_table(freqs, angles)
        rows_here = lax.dynamic_slice_in_dim(slot_rows, start, block, 0)
        counts_here = lax.dynamic_slice_in_dim(slot_counts, start, block)
        return (table, make_basis(freqs, rows_here, counts_here, radial))

    def analyse(index):
        table, basis = block_tools(index)
        spectrum = jnp.dot(flat, table, preferred_element_type=jnp.float32)
        spectrum = spectrum.astype(jnp.bfloat16).reshape(count_img, radial, 2, block)
        return jnp.einsum(
            "ircj,jqr->jciq", spectrum, basis, preferred_element_type=jnp.float32
        ).astype(jnp.bfloat16)

    pieces = lax.map(analyse, jnp.arange(nblocks, dtype=jnp.int32))
    moved = pieces.reshape(total_freq, 2 * count_img, radial)
    owners = lax.axis_size("freq")
    owned = total_freq // owners
    batches = lax.axis_size("batch")
    mine = lax.dynamic_slice_in_dim(order, lax.axis_index("freq") * owned, owned)
    noise_mine = jnp.take(noise_var, mine)
    half_slots = owned // 2
    narrow = radial // 2
    grouped = moved.reshape(owners, owned, 2 * count_img, radial)
    lower_part = grouped[:, :half_slots].reshape(owners * half_slots, 2 * count_img, radial)
    upper_part = grouped[:, half_slots:, :, :narrow].reshape(
        owners * half_slots, 2 * count_img, narrow
    )
    low_recv, high_recv = (
        lax.all_to_all(lower_part, "freq", split_axis=0, concat_axis=1, tiled=True),
        lax.all_to_all(upper_part, "freq", split_axis=0, concat_axis=1, tiled=True),
    )
    gram_low, gram_high = lax.psum((gram_of(low_recv), gram_of(high_recv)), "batch")
    vectors = low_recv.shape[1] * batches
    shrink_lower = shrink_from(gram_low, noise_mine[:half_slots], vectors)
    shrink_upper = shrink_from(gram_high, noise_mine[half_slots:], vectors)
    low_back, high_back = (
        lax.all_to_all(
            apply_shrink(shrink_lower, low_recv), "freq", split_axis=1, concat_axis=0, tiled=True
        ),
        lax.all_to_all(
            apply_shrink(shrink_upper, high_recv), "freq", split_axis=1, concat_axis=0, tiled=True
        ),
    )
    high_wide = jnp.pad(high_back, ((0, 0), (0, 0), (0, radial - narrow)))
    returned = jnp.concatenate(
        [
            low_back.reshape(owners, half_slots, 2 * count_img, radial),
            high_wide.reshape(owners, half_slots, 2 * count_img, radial),
        ],
        axis=1,
    )
    returned = returned.reshape(total_freq, 2 * count_img, radial)
    upper_wide = jnp.pad(shrink_upper, ((0, 0), (0, radial - narrow), (0, radial - narrow)))
    wiener_blocks = jnp.concatenate([shrink_lower, upper_wide], axis=0)
    filtered_blocks = returned.reshape(nblocks, block, 2, count_img, radial)

    def synthesise(index, total):
        table, basis = block_tools(index)
        piece = lax.dynamic_index_in_dim(filtered_blocks, index, 0, keepdims=False)
        spectrum_out = jnp.einsum(
            "jciq,jqr->ircj", piece, basis, preferred_element_type=jnp.float32
        )
        spectrum_out = spectrum_out.astype(jnp.bfloat16).reshape(count_img * radial, 2 * block)
        return total + lax.dot_general(
            spectrum_out, table, (((1,), (1,)), ((), ())), preferred_element_type=jnp.float32
        )

    summed = lax.fori_loop(
        0, nblocks, synthesise, jnp.zeros((count_img * radial, angles), jnp.float32)
    )
    denoised = summed.astype(jnp.bfloat16).reshape(count_img, radial, angles)
    return (denoised, wiener_blocks)


COSINE = (
    -0.9999999889445799,
    4.934801116644238,
    -4.058694745523659,
    1.3351580223122241,
    -0.23502902263765682,
    0.025358285764913842,
    -0.0015936782168350142,
)


def cosine_of(turns, steps):
    x = ((turns & (steps - 1)) - steps // 2).astype(jnp.float32) * (2.0 / steps)
    y = x * x
    total = jnp.full_like(y, COSINE[-1])
    for term in COSINE[-2::-1]:
        total = total * y + term
    return total


def iota(shape, dim):
    return lax.broadcasted_iota(jnp.int32, shape, dim)


def nt(a, b):
    return lax.dot_general(a, b, (((1,), (1,)), ((), ())), preferred_element_type=jnp.float32)


def tn(a, b):
    return lax.dot_general(a, b, (((0,), (0,)), ((), ())), preferred_element_type=jnp.float32)


def nn(a, b):
    return jnp.dot(a, b, preferred_element_type=jnp.float32)


def low_bits(mask):
    return mask.astype(jnp.float32).astype(jnp.bfloat16)


class Plan:
    def __init__(self, images, order, owners, batches):
        self.count_img, self.radial, self.angles = images
        self.total = order
        self.owners, self.batches = owners, batches
        self.devices = owners * batches
        self.owned = order // owners
        self.half = self.owned // 2
        self.vecs = 2 * self.count_img
        self.quota = 4
        self.pairs = self.quota // 2
        self.narrow = self.radial // 2
        self.low_rows = self.vecs * self.quota
        self.rows = self.low_rows + self.vecs * self.pairs
        self.all_pairs = self.devices * self.pairs
        power = lambda n: n > 0 and n & (n - 1) == 0
        self.fits = (
            batches == 2
            and self.half == batches * self.quota
            and self.radial == 128
            and self.count_img == 4
            and all(power(n) for n in (self.angles, self.total, owners))
            and self.angles == 2 * self.total
        )

    def slot_of(self, device, place):
        batch, owner = device // self.owners, device & (self.owners - 1)
        return owner * self.owned + batch * self.quota + place


def analysis_kernel(
    plan, order_hbm, counts_hbm, noise_hbm, zeros_hbm, images_hbm,
    coef_ref, table_ref, cb_ref, sb_ref, wave_ref, zero_ref, info_ref,
    wide_ref, order_ref, counts_ref, noise_ref, zeros_ref, images_ref, sems,
):
    radial, angles, total = plan.radial, plan.angles, plan.total
    quota, pairs, narrow = plan.quota, plan.pairs, plan.narrow
    copies = [
        pltpu.make_async_copy(source, target, sems.at[at])
        for at, (source, target) in enumerate(
            (
                (order_hbm, order_ref),
                (counts_hbm, counts_ref),
                (noise_hbm, noise_ref),
                (zeros_hbm, zeros_ref),
                (images_hbm, images_ref),
            )
        )
    ]
    for copy in copies:
        copy.start()
    turns = (iota((radial, radial), 1) + 1) * (2 * iota((radial, radial), 0) + 1)
    factor = math.sqrt(2.0 / radial)
    wave_ref[0:radial, :] = (factor * cosine_of(turns, 4 * radial)).astype(jnp.bfloat16)
    wave_ref[radial : 2 * radial, :] = (-factor * cosine_of(turns - radial, 4 * radial)).astype(
        jnp.bfloat16
    )
    row = iota((2 * total, total), 0)
    high = row - total
    low_slot = plan.slot_of(row // (2 * quota), row & (quota - 1))
    pair = high & (plan.all_pairs - 1)
    side = high // (2 * plan.all_pairs)
    place = plan.half + 2 * (pair & (pairs - 1)) + side
    high_slot = plan.slot_of(pair // pairs, place)
    slot = jnp.where(row < total, low_slot, high_slot)
    pick = low_bits(slot == iota((2 * total, total), 1))
    spread = lambda ref: jnp.broadcast_to(ref[...].astype(jnp.float32), (128, total)).astype(jnp.bfloat16)
    copies[0].wait()
    held = spread(order_ref)
    freq = nt(pick, held).astype(jnp.int32)
    row = iota((2 * total, 128), 0)
    lane = iota((2 * total, 128), 1)
    sine_row = jnp.where(row < total, row // quota, row // plan.all_pairs) & 1
    lag = sine_row * (angles // 4)
    flip = (1 - 2 * (freq & 1)).astype(jnp.float32)
    factor = math.sqrt(2.0 / angles)
    for part in range(angles // 256):
        cosine = cosine_of((lane + part * 128) * freq - lag, angles) * factor
        table_ref[:, part * 128 : part * 128 + 128] = cosine.astype(jnp.bfloat16)
        start = angles // 2 + part * 128
        table_ref[:, start : start + 128] = (cosine * flip).astype(jnp.bfloat16)
    steps = 16 * radial
    turns = (2 * freq - 1) * (2 * lane + 1) - 4 * radial * freq - 2 * radial
    cb_ref[...] = cosine_of(turns, steps)
    sb_ref[...] = cosine_of(turns - steps // 4, steps)
    for copy in copies[1:4]:
        copy.wait()
    by_freq = low_bits(iota((total, total), 0) == iota((total, total), 1))
    counts = nt(by_freq, spread(counts_ref)).astype(jnp.int32)
    zeros = jnp.where(iota((total, radial), 1) < counts, zeros_ref[...], 0)
    zeros = zeros.astype(jnp.float32).astype(jnp.bfloat16)
    freq_lane = iota((plan.all_pairs, total), 1)
    sides = []
    for e in range(2):
        start = total + e * 2 * plan.all_pairs
        named = freq[start : start + plan.all_pairs]
        named = jnp.concatenate([named] * (total // 128), axis=1)
        sides.append(nn(low_bits(named == freq_lane), zeros))
    lane = iota((plan.all_pairs, radial), 1)
    zero_ref[...] = jnp.where(lane < narrow, sides[0], pltpu.roll(sides[1], narrow, axis=1)).astype(
        jnp.int32
    )
    place = iota((8, total), 0)
    device = lax.axis_index("batch") * plan.owners + lax.axis_index("freq")
    slot = plan.slot_of(device, (place // quota) * plan.half + (place & (quota - 1)))
    mine = nt(low_bits(slot == iota((8, total), 1)), held).astype(jnp.int32)
    mine = jnp.concatenate([mine] * (total // 128), axis=1) == iota((8, total), 1)
    info_ref[0:8, :] = nn(low_bits(mine), zeros)
    noise = jnp.sum(jnp.where(mine, noise_ref[...], 0.0), axis=1, keepdims=True)
    info_ref[8:16, :] = jnp.broadcast_to(noise, (8, 128))
    copies[4].wait()
    images = images_ref[...].reshape(plan.count_img * radial, angles)
    for two in range(plan.count_img // 2):
        spectrum = nt(table_ref[...], images[2 * two * radial : 2 * (two + 1) * radial])
        lows = []
        for i in range(2):
            part = spectrum[:, i * radial : (i + 1) * radial]
            turned = jnp.concatenate(
                [(part * cb_ref[...]).astype(jnp.bfloat16), (part * sb_ref[...]).astype(jnp.bfloat16)],
                axis=1,
            )
            coef = nn(turned, wave_ref[...])
            lows.append(coef[:total].reshape(plan.devices, 2 * quota, radial))
            span = 2 * plan.all_pairs
            for e in range(2):
                at = (e * plan.count_img + 2 * two + i) * span
                wide_ref[at : at + span, :] = coef[total + e * span : total + (e + 1) * span]
        size = 4 * quota
        coef_ref[:, size * two : size * (two + 1), :] = jnp.concatenate(lows, axis=1).astype(
            jnp.bfloat16
        )
    lane = iota((plan.vecs, radial), 1)
    zero_here = iota((radial, radial), 0) + 1
    for device in range(plan.devices):
        tiles = []
        for i in range(pairs):
            at = device * pairs + i
            vectors = wide_ref[pl.ds(at, 2 * plan.vecs, stride=plan.all_pairs), :]
            chosen = low_bits(zero_here == zero_ref[at : at + 1, :])
            both = nn(vectors.astype(jnp.bfloat16), chosen)
            tiles.append(jnp.where(lane < narrow, both[: plan.vecs], both[plan.vecs :]))
        coef_ref[device, plan.low_rows : plan.rows, :] = jnp.concatenate(tiles, axis=0).astype(
            jnp.bfloat16
        )


def thirds(x):
    first = x.astype(jnp.bfloat16)
    rest = x - first.astype(jnp.float32)
    second = rest.astype(jnp.bfloat16)
    third = (rest - second.astype(jnp.float32)).astype(jnp.bfloat16)
    return first, second, third


def outer(u, v):
    u1, u2, u3 = thirds(u)
    v1, v2, v3 = thirds(v)
    return lax.dot_general(
        jnp.concatenate([u1, u1, u1, u2, u2, u3], axis=0),
        jnp.concatenate([v1, v2, v3, v1, v2, v1], axis=0),
        (((0,), (0,)), ((), ())),
        preferred_element_type=jnp.float32,
    )


def first_lane(halved, lane, step):
    return (lane & 64 if halved else jnp.zeros_like(lane)) + step * 8


def pivot_panels(panels, halves, step):
    shape = (8, 128)
    sub, lane = iota(shape, 0), iota(shape, 1)
    blocks = [
        [
            jnp.take_along_axis(panel, first_lane(halved, lane, step) + j, axis=1)
            for j in range(8)
        ]
        for panel, halved in zip(panels, halves)
    ]
    for i in range(8):
        unit = (sub == i).astype(jnp.float32)
        for at, cols in enumerate(blocks):
            inverse = 1.0 / jnp.broadcast_to(cols[i][i : i + 1], shape)
            weight = (cols[i] - unit) * inverse
            blocks[at] = [
                unit - weight
                if j == i
                else cols[j] - weight * jnp.broadcast_to(cols[j][i : i + 1], shape)
                for j in range(8)
            ]
    solved = []
    for panel, halved, cols in zip(panels, halves, blocks):
        offset = lane - first_lane(halved, lane, step)
        unit = (sub == offset).astype(jnp.float32)
        lines = jnp.where((offset < 0) | (offset >= 8), panel, unit)
        total = cols[0] * jnp.broadcast_to(lines[0:1], shape)
        for j in range(1, 8):
            total = total + cols[j] * jnp.broadcast_to(lines[j : j + 1], shape)
        solved.append(total)
    return solved


def scales_of(matrix, halved):
    row, lane = iota(matrix.shape, 0), iota(matrix.shape, 1)
    diagonal = jnp.where(row == (lane & 63 if halved else lane), matrix, 0.0)
    across = lax.rsqrt(jnp.sum(diagonal, axis=0, keepdims=True))
    if not halved:
        return across * lax.rsqrt(jnp.sum(diagonal, axis=1, keepdims=True))
    left = lax.rsqrt(jnp.sum(jnp.where(lane < 64, diagonal, 0.0), axis=1, keepdims=True))
    right = lax.rsqrt(jnp.sum(jnp.where(lane < 64, 0.0, diagonal), axis=1, keepdims=True))
    return across * jnp.where(lane < 64, left, right)


def sweep(matrices, step, carry):
    start = pl.multiple_of(step * 8, 8)
    halves = [halved for _, _, halved in matrices]
    panels = [ref[m, pl.ds(start, 8), :] for ref, m, _ in matrices]
    solved = pivot_panels(panels, halves, step)
    sub, lane = iota((8, 128), 0), iota((8, 128), 1)
    for (ref, m, halved), panel, fresh in zip(matrices, panels, solved):
        height = ref.shape[1]
        done = (lane & 63 if halved else lane) < step * 8
        unit = (sub == lane - first_lane(halved, lane, step)).astype(jnp.float32)
        update = outer(jnp.where(done, -panel, panel), fresh + unit)
        if halved:
            update = jnp.where(iota((height, 128), 1) < 64, update[:height], update[height:])
        ref[m] = ref[m] - update
        ref[m, pl.ds(start, 8), :] = fresh
    return carry


def filter_kernel(
    plan, info_ref, recv_ref,
    back_ref, shrink_ref, wide_ref, full_ref, pair_ref, pick_ref, held_ref, full_scale_ref, pair_scale_ref,
):
    radial, quota, pairs, narrow = plan.radial, plan.quota, plan.pairs, plan.narrow
    low_rows = plan.low_rows
    rows = plan.devices * plan.vecs
    low_part = recv_ref[:, :low_rows, :].astype(jnp.float32)
    wide_ref[...] = low_part.reshape(plan.devices * low_rows, radial)
    square = (radial, radial)
    strip = (narrow, radial)
    eye = (iota(square, 0) == iota(square, 1)).astype(jnp.float32)
    twins = (iota(strip, 0) == (iota(strip, 1) & (narrow - 1))).astype(jnp.float32)
    first = iota(strip, 1) < narrow
    noises = []
    for s in range(quota):
        noises.append(info_ref[8 + s : 9 + s, :])
        zero = info_ref[s : s + 1, :].astype(jnp.int32)
        pick = low_bits(iota(square, 0) + 1 == zero)
        pick_ref[s] = pick
        vectors = wide_ref[pl.ds(s, rows, stride=quota), :].astype(jnp.bfloat16)
        coef = nn(vectors, pick).astype(jnp.bfloat16)
        covariance = tn(coef, coef) / float(rows) + noises[s] * eye
        scale = scales_of(covariance, False)
        full_scale_ref[s] = scale
        full_ref[s] = covariance * scale
    high_part = recv_ref[:, low_rows:, :].astype(jnp.float32)
    for i in range(pairs):
        coef = high_part[:, i * plan.vecs : (i + 1) * plan.vecs, :].reshape(rows, radial)
        coef = coef.astype(jnp.bfloat16)
        held_ref[i] = coef
        gram = tn(coef, coef)
        gram = jnp.where(first, gram[:narrow], gram[narrow:])
        at = 8 + quota + 2 * i
        noise = jnp.where(first, info_ref[at : at + 1, :], info_ref[at + 1 : at + 2, :])
        noises.append(noise)
        covariance = gram / float(rows) + noise * twins
        scale = scales_of(covariance, True)
        pair_scale_ref[i] = scale
        pair_ref[i] = covariance * scale
    lower = [(full_ref, m, False) for m in range(quota)]
    upper = [(pair_ref, m, True) for m in range(pairs)]
    lax.fori_loop(0, narrow // 8, functools.partial(sweep, lower + upper), 0)
    lax.fori_loop(narrow // 8, radial // 8, functools.partial(sweep, lower), 0)
    for s in range(quota):
        shrink = eye - noises[s] * (full_ref[s] * full_scale_ref[s])
        shrink_ref[s * radial : (s + 1) * radial, :] = shrink.astype(jnp.bfloat16)
        pick = pick_ref[s]
        moved = lax.dot_general(
            shrink.astype(jnp.bfloat16),
            pick,
            (((0,), (1,)), ((), ())),
            preferred_element_type=jnp.float32,
        ).astype(jnp.bfloat16)
        spread = nn(pick, moved).astype(jnp.bfloat16)
        vectors = wide_ref[pl.ds(s, rows, stride=quota), :].astype(jnp.bfloat16)
        wide_ref[pl.ds(s, rows, stride=quota), :] = nn(vectors, spread)
    shape = (plan.devices, low_rows, radial)
    back_ref[:, :low_rows, :] = wide_ref[...].reshape(shape).astype(jnp.bfloat16)
    tiles = []
    for i in range(pairs):
        shrink = twins - noises[quota + i] * (pair_ref[i] * pair_scale_ref[i])
        start = quota * radial + i * narrow
        shrink_ref[start : start + narrow, :] = shrink.astype(jnp.bfloat16)
        blocks = jnp.concatenate(
            [jnp.where(first, shrink, 0.0), jnp.where(first, 0.0, shrink)], axis=0
        )
        filtered = nt(held_ref[i], blocks.astype(jnp.bfloat16))
        tiles.append(filtered.reshape(plan.devices, plan.vecs, radial))
    back_ref[:, low_rows:, :] = jnp.concatenate(tiles, axis=1).astype(jnp.bfloat16)


def synthesis_kernel(plan, table_ref, cb_ref, sb_ref, wave_ref, zero_ref, recv_ref, out_ref, wide_ref, held_ref):
    radial, total, quota, pairs = plan.radial, plan.total, plan.quota, plan.pairs
    lane = iota((plan.vecs, radial), 1)
    zero_here = iota((radial, radial), 0) + 1
    for device in range(plan.devices):
        tile = recv_ref[device, plan.low_rows : plan.rows, :].astype(jnp.float32)
        for i in range(pairs):
            at = device * pairs + i
            packed = tile[i * plan.vecs : (i + 1) * plan.vecs]
            both = jnp.concatenate(
                [jnp.where(lane < plan.narrow, packed, 0.0), jnp.where(lane < plan.narrow, 0.0, packed)],
                axis=0,
            )
            chosen = low_bits(zero_here == zero_ref[at : at + 1, :])
            spread = nt(both.astype(jnp.bfloat16), chosen)
            wide_ref[pl.ds(at, 2 * plan.vecs, stride=plan.all_pairs), :] = spread
    span = 2 * plan.all_pairs
    for i in range(plan.count_img):
        low = recv_ref[:, 2 * quota * i : 2 * quota * (i + 1), :].astype(jnp.float32)
        at = [(e * plan.count_img + i) * span for e in range(2)]
        filtered = jnp.concatenate(
            [low.reshape(total, radial)] + [wide_ref[a : a + span, :] for a in at], axis=0
        )
        turned = nt(filtered.astype(jnp.bfloat16), wave_ref[...])
        spectrum = turned[:, :radial] * cb_ref[...] + turned[:, radial:] * sb_ref[...]
        held_ref[:, i * radial : (i + 1) * radial] = spectrum.astype(jnp.bfloat16)
    image = tn(held_ref[...], table_ref[...]).astype(jnp.bfloat16)
    out_ref[...] = image.reshape(out_ref.shape)


def wiener_kernel(plan, own_ref, other_ref, out_ref):
    radial, quota, narrow = plan.radial, plan.quota, plan.narrow
    batch_at = lax.axis_index("batch")
    lane = iota((narrow, radial), 1)
    for batch, ref in ((batch_at, own_ref), (1 - batch_at, other_ref)):
        for s in range(quota):
            out_ref[batch * quota + s] = ref[s * radial : (s + 1) * radial, :].astype(jnp.float32)
            at = plan.half + batch * quota + s
            start = quota * radial + (s // 2) * narrow
            pair = ref[start : start + narrow, :].astype(jnp.float32)
            if s % 2:
                pair = pltpu.roll(pair, narrow, axis=1)
            out_ref[at, 0:narrow, :] = jnp.where(lane < narrow, pair, 0.0)
            out_ref[at, narrow:radial, :] = jnp.zeros((radial - narrow, radial), jnp.float32)


VMEM = pl.BlockSpec(memory_space=pltpu.VMEM)
HBM = pl.BlockSpec(memory_space=pltpu.HBM)


def call(kernel, outs, ins, scratch=()):
    return pl.pallas_call(
        kernel,
        out_shape=outs,
        in_specs=ins,
        out_specs=jax.tree.map(lambda _: VMEM, outs),
        scratch_shapes=scratch,
        compiler_params=pltpu.CompilerParams(vmem_limit_bytes=16 << 20),
    )


def fast_device(plan, images, radial_counts, order, zeros_table, noise_var):
    both = ("batch", "freq")
    radial, total, quota, pairs = plan.radial, plan.total, plan.quota, plan.pairs
    shape = jax.ShapeDtypeStruct
    block = shape((plan.devices, plan.rows, radial), jnp.bfloat16)
    coef, table, cb, sb, wave, zero, info = call(
        functools.partial(analysis_kernel, plan),
        (
            block,
            shape((2 * total, plan.angles), jnp.bfloat16),
            shape((2 * total, radial), jnp.float32),
            shape((2 * total, radial), jnp.float32),
            shape((2 * radial, radial), jnp.bfloat16),
            shape((plan.all_pairs, radial), jnp.int32),
            shape((16, radial), jnp.float32),
        ),
        [HBM] * 5,
        [
            pltpu.VMEM((2 * plan.vecs * plan.all_pairs, radial), jnp.float32),
            pltpu.VMEM((1, total), jnp.int32),
            pltpu.VMEM((1, total), jnp.int32),
            pltpu.VMEM((1, total), jnp.float32),
            pltpu.VMEM(zeros_table.shape, jnp.int32),
            pltpu.VMEM(images.shape, jnp.bfloat16),
            pltpu.SemaphoreType.DMA((5,)),
        ],
    )(
        *(
            pltpu.with_memory_space_constraint(array, pltpu.HBM)
            for array in (
                order.reshape(1, total),
                radial_counts.reshape(1, total),
                noise_var.reshape(1, total),
                zeros_table,
                images,
            )
        )
    )
    recv = lax.all_to_all(coef, both, split_axis=0, concat_axis=0, tiled=True)
    back, shrink = call(
        functools.partial(filter_kernel, plan),
        (block, shape((quota * radial + pairs * plan.narrow, radial), jnp.bfloat16)),
        [VMEM, VMEM],
        [
            pltpu.VMEM((plan.devices * plan.low_rows, radial), jnp.float32),
            pltpu.VMEM((quota, radial, radial), jnp.float32),
            pltpu.VMEM((pairs, plan.narrow, radial), jnp.float32),
            pltpu.VMEM((quota, radial, radial), jnp.bfloat16),
            pltpu.VMEM((pairs, plan.devices * plan.vecs, radial), jnp.bfloat16),
            pltpu.VMEM((quota, radial, radial), jnp.float32),
            pltpu.VMEM((pairs, plan.narrow, radial), jnp.float32),
        ],
    )(info, recv)
    returned = lax.all_to_all(back, both, split_axis=0, concat_axis=0, tiled=True)
    other = lax.ppermute(shrink, "batch", [(0, 1), (1, 0)])
    wiener_blocks = call(
        functools.partial(wiener_kernel, plan),
        shape((plan.owned, radial, radial), jnp.float32),
        [VMEM] * 2,
    )(shrink, other)
    denoised = call(
        functools.partial(synthesis_kernel, plan),
        shape((plan.count_img, radial, plan.angles), jnp.bfloat16),
        [VMEM] * 6,
        [
            pltpu.VMEM((2 * plan.vecs * plan.all_pairs, radial), jnp.float32),
            pltpu.VMEM((2 * total, plan.count_img * radial), jnp.bfloat16),
        ],
    )(table, cb, sb, wave, zero, returned)
    return denoised, wiener_blocks


def solution(mesh):
    owners, batches = mesh.shape["freq"], mesh.shape["batch"]

    def body(images, radial_counts, order, zeros_table, noise_var):
        plan = Plan(images.shape, order.shape[0], owners, batches)
        device = functools.partial(fast_device, plan) if plan.fits else per_device
        return device(images, radial_counts, order, zeros_table, noise_var)

    return jax.shard_map(
        body,
        mesh=mesh,
        in_specs=(P(("batch", "freq"), None, None), P(), P(), P(), P()),
        out_specs=(P(("batch", "freq"), None, None), P("freq", None, None)),
        check_vma=False,
    )
```

```python
import functools
import math

import jax
import jax.numpy as jnp
from jax import lax
from jax.experimental import pallas as pl
from jax.experimental.pallas import tpu as pltpu
from jax.sharding import PartitionSpec as P


def make_table(freqs, angles):
    angle_index = jnp.arange(angles, dtype=jnp.int32)
    product = angle_index[:, None] * freqs[None, :] % angles
    phase = 2.0 * math.pi / angles * product.astype(jnp.float32)
    factor = math.sqrt(2.0 / angles)
    return jnp.concatenate([factor * jnp.cos(phase), factor * jnp.sin(phase)], axis=1).astype(
        jnp.bfloat16
    )


def make_basis(freqs, zero_rows, counts, radial):
    slots = zero_rows.shape[1]
    freq_float = freqs.astype(jnp.float32)[:, None, None]
    scaled = math.pi * (zero_rows.astype(jnp.float32)[:, :, None] + 0.5 * freq_float - 0.25)
    grid = (jnp.arange(radial, dtype=jnp.float32) + 0.5) / radial
    phase = scaled * grid[None, None, :] - 0.5 * math.pi * freq_float - 0.25 * math.pi
    keep = jnp.arange(slots, dtype=jnp.int32)[None, :, None] < counts[:, None, None]
    values = math.sqrt(2.0 / radial) * jnp.cos(phase)
    return jnp.where(keep, values, jnp.zeros_like(values)).astype(jnp.bfloat16)


def gram_of(blocks):
    return jnp.einsum("kvq,kvp->kqp", blocks, blocks, preferred_element_type=jnp.float32)


def shrink_from(gram, noise, vectors):
    width = gram.shape[1]
    eye = jnp.eye(width, dtype=jnp.float32)
    covariance = gram / vectors + noise[:, None, None] * eye
    lower = jnp.linalg.cholesky(covariance)
    inv_lower = jax.scipy.linalg.solve_triangular(
        lower, jnp.broadcast_to(eye, covariance.shape), lower=True
    )
    inverse = jnp.einsum("kmq,kmp->kqp", inv_lower, inv_lower, precision=lax.Precision.HIGHEST)
    return eye - noise[:, None, None] * inverse


def apply_shrink(shrinkage, blocks):
    return jnp.einsum(
        "kqp,kvp->kvq", shrinkage.astype(jnp.bfloat16), blocks, preferred_element_type=jnp.float32
    ).astype(jnp.bfloat16)


def per_device(images, radial_counts, order, zeros_table, noise_var):
    count_img, radial, angles = images.shape
    total_freq = order.shape[0]
    block = min(64, total_freq)
    nblocks = total_freq // block
    flat = images.reshape(count_img * radial, angles)
    slot_rows = jnp.take(zeros_table, order, axis=0)
    slot_counts = jnp.take(radial_counts, order)

    def block_tools(index):
        start = index * block
        freqs = lax.dynamic_slice_in_dim(order, start, block)
        table = make_table(freqs, angles)
        rows_here = lax.dynamic_slice_in_dim(slot_rows, start, block, 0)
        counts_here = lax.dynamic_slice_in_dim(slot_counts, start, block)
        return (table, make_basis(freqs, rows_here, counts_here, radial))

    def analyse(index):
        table, basis = block_tools(index)
        spectrum = jnp.dot(flat, table, preferred_element_type=jnp.float32)
        spectrum = spectrum.astype(jnp.bfloat16).reshape(count_img, radial, 2, block)
        return jnp.einsum(
            "ircj,jqr->jciq", spectrum, basis, preferred_element_type=jnp.float32
        ).astype(jnp.bfloat16)

    pieces = lax.map(analyse, jnp.arange(nblocks, dtype=jnp.int32))
    moved = pieces.reshape(total_freq, 2 * count_img, radial)
    owners = lax.axis_size("freq")
    owned = total_freq // owners
    batches = lax.axis_size("batch")
    mine = lax.dynamic_slice_in_dim(order, lax.axis_index("freq") * owned, owned)
    noise_mine = jnp.take(noise_var, mine)
    half_slots = owned // 2
    narrow = radial // 2
    grouped = moved.reshape(owners, owned, 2 * count_img, radial)
    lower_part = grouped[:, :half_slots].reshape(owners * half_slots, 2 * count_img, radial)
    upper_part = grouped[:, half_slots:, :, :narrow].reshape(
        owners * half_slots, 2 * count_img, narrow
    )
    low_recv, high_recv = (
        lax.all_to_all(lower_part, "freq", split_axis=0, concat_axis=1, tiled=True),
        lax.all_to_all(upper_part, "freq", split_axis=0, concat_axis=1, tiled=True),
    )
    gram_low, gram_high = lax.psum((gram_of(low_recv), gram_of(high_recv)), "batch")
    vectors = low_recv.shape[1] * batches
    shrink_lower = shrink_from(gram_low, noise_mine[:half_slots], vectors)
    shrink_upper = shrink_from(gram_high, noise_mine[half_slots:], vectors)
    low_back, high_back = (
        lax.all_to_all(
            apply_shrink(shrink_lower, low_recv), "freq", split_axis=1, concat_axis=0, tiled=True
        ),
        lax.all_to_all(
            apply_shrink(shrink_upper, high_recv), "freq", split_axis=1, concat_axis=0, tiled=True
        ),
    )
    high_wide = jnp.pad(high_back, ((0, 0), (0, 0), (0, radial - narrow)))
    returned = jnp.concatenate(
        [
            low_back.reshape(owners, half_slots, 2 * count_img, radial),
            high_wide.reshape(owners, half_slots, 2 * count_img, radial),
        ],
        axis=1,
    )
    returned = returned.reshape(total_freq, 2 * count_img, radial)
    upper_wide = jnp.pad(shrink_upper, ((0, 0), (0, radial - narrow), (0, radial - narrow)))
    wiener_blocks = jnp.concatenate([shrink_lower, upper_wide], axis=0)
    filtered_blocks = returned.reshape(nblocks, block, 2, count_img, radial)

    def synthesise(index, total):
        table, basis = block_tools(index)
        piece = lax.dynamic_index_in_dim(filtered_blocks, index, 0, keepdims=False)
        spectrum_out = jnp.einsum(
            "jciq,jqr->ircj", piece, basis, preferred_element_type=jnp.float32
        )
        spectrum_out = spectrum_out.astype(jnp.bfloat16).reshape(count_img * radial, 2 * block)
        return total + lax.dot_general(
            spectrum_out, table, (((1,), (1,)), ((), ())), preferred_element_type=jnp.float32
        )

    summed = lax.fori_loop(
        0, nblocks, synthesise, jnp.zeros((count_img * radial, angles), jnp.float32)
    )
    denoised = summed.astype(jnp.bfloat16).reshape(count_img, radial, angles)
    return (denoised, wiener_blocks)


COSINE = (
    -0.9999999889445799,
    4.934801116644238,
    -4.058694745523659,
    1.3351580223122241,
    -0.23502902263765682,
    0.025358285764913842,
    -0.0015936782168350142,
)


def cosine_of(turns, steps):
    x = ((turns & (steps - 1)) - steps // 2).astype(jnp.float32) * (2.0 / steps)
    y = x * x
    total = jnp.full_like(y, COSINE[-1])
    for term in COSINE[-2::-1]:
        total = total * y + term
    return total


def iota(shape, dim):
    return lax.broadcasted_iota(jnp.int32, shape, dim)


def nt(a, b):
    return lax.dot_general(a, b, (((1,), (1,)), ((), ())), preferred_element_type=jnp.float32)


def tn(a, b):
    return lax.dot_general(a, b, (((0,), (0,)), ((), ())), preferred_element_type=jnp.float32)


def nn(a, b):
    return jnp.dot(a, b, preferred_element_type=jnp.float32)


def low_bits(mask):
    return mask.astype(jnp.float32).astype(jnp.bfloat16)


class Plan:
    def __init__(self, images, order, owners, batches):
        self.count_img, self.radial, self.angles = images
        self.total = order
        self.owners, self.batches = owners, batches
        self.devices = owners * batches
        self.owned = order // owners
        self.half = self.owned // 2
        self.vecs = 2 * self.count_img
        self.quota = 4
        self.pairs = self.quota // 2
        self.narrow = self.radial // 2
        self.low_rows = self.vecs * self.quota
        self.rows = self.low_rows + self.vecs * self.pairs
        self.all_pairs = self.devices * self.pairs
        power = lambda n: n > 0 and n & (n - 1) == 0
        self.fits = (
            batches == 2
            and self.half == batches * self.quota
            and self.radial == 128
            and self.count_img == 4
            and all(power(n) for n in (self.angles, self.total, owners))
            and self.angles == 2 * self.total
        )

    def slot_of(self, device, place):
        batch, owner = device // self.owners, device & (self.owners - 1)
        return owner * self.owned + batch * self.quota + place


def analysis_kernel(
    plan, order_hbm, counts_hbm, noise_hbm, zeros_hbm, images_hbm,
    coef_ref, table_ref, cb_ref, sb_ref, wave_ref, zero_ref, info_ref,
    wide_ref, order_ref, counts_ref, noise_ref, zeros_ref, images_ref, sems,
):
    radial, angles, total = plan.radial, plan.angles, plan.total
    quota, pairs, narrow = plan.quota, plan.pairs, plan.narrow
    copies = [
        pltpu.make_async_copy(source, target, sems.at[at])
        for at, (source, target) in enumerate(
            (
                (order_hbm, order_ref),
                (counts_hbm, counts_ref),
                (noise_hbm, noise_ref),
                (zeros_hbm, zeros_ref),
                (images_hbm, images_ref),
            )
        )
    ]
    for copy in copies:
        copy.start()
    turns = (iota((radial, radial), 1) + 1) * (2 * iota((radial, radial), 0) + 1)
    factor = math.sqrt(2.0 / radial)
    wave_ref[0:radial, :] = (factor * cosine_of(turns, 4 * radial)).astype(jnp.bfloat16)
    wave_ref[radial : 2 * radial, :] = (-factor * cosine_of(turns - radial, 4 * radial)).astype(
        jnp.bfloat16
    )
    sub, lane = iota((8, total), 0), iota((8, total), 1)
    place = sub & (quota - 1)
    jump = (place // pairs) * plan.owned + 2 * (place & (pairs - 1))
    slots = [place + plan.slot_of(device, 0) for device in range(plan.devices)]
    slots += [
        jump + (plan.slot_of(2 * four, 0) + plan.half + e)
        for e in range(2)
        for four in range(plan.all_pairs // 4)
    ]
    jump = (sub // pairs) * plan.owned + 2 * (sub & (pairs - 1))
    slots += [
        jump + (plan.slot_of(4 * eight, 0) + plan.half + e)
        for e in range(2)
        for eight in range(plan.all_pairs // 8)
    ]
    device = lax.axis_index("batch") * plan.owners + lax.axis_index("freq")
    slots.append(plan.slot_of(device, (sub // quota) * plan.half + place))
    slots.append(slots[-1])
    pick = jnp.concatenate([(slot == lane).astype(jnp.float32) for slot in slots], axis=0)
    pick = pick.astype(jnp.bfloat16)
    copies[0].wait()
    spread = lambda ref: jnp.broadcast_to(ref[...].astype(jnp.float32), (128, total)).astype(jnp.bfloat16)
    every_freq = nt(pick, spread(order_ref)).astype(jnp.int32)
    freq = every_freq[: 2 * total]
    lane = iota((2 * total, 128), 1)
    sine_row = (iota((2 * total, 128), 0) // quota) & 1
    lag = sine_row * (angles // 4)
    flip = (1 - 2 * (freq & 1)).astype(jnp.float32)
    factor = math.sqrt(2.0 / angles)
    for part in range(angles // 256):
        cosine = cosine_of((lane + part * 128) * freq - lag, angles) * factor
        table_ref[:, part * 128 : part * 128 + 128] = cosine.astype(jnp.bfloat16)
        start = angles // 2 + part * 128
        table_ref[:, start : start + 128] = (cosine * flip).astype(jnp.bfloat16)
    steps = 16 * radial
    turns = (2 * freq - 1) * (2 * lane + 1) - 4 * radial * freq - 2 * radial
    cb_ref[...] = cosine_of(turns, steps)
    sb_ref[...] = cosine_of(turns - steps // 4, steps)
    for copy in copies[1:4]:
        copy.wait()
    named = every_freq[2 * total :]
    named = jnp.concatenate([named] * (total // 128), axis=1) == iota((named.shape[0], total), 1)
    pick = low_bits(named)
    zeros = nn(pick, zeros_ref[...].astype(jnp.float32).astype(jnp.bfloat16))
    counts = nt(pick, spread(counts_ref)).astype(jnp.int32)
    zeros = jnp.where(iota(zeros.shape, 1) < counts, zeros, 0.0)
    first, second = zeros[: plan.all_pairs], zeros[plan.all_pairs : 2 * plan.all_pairs]
    lane = iota((plan.all_pairs, radial), 1)
    zero_ref[...] = jnp.where(lane < narrow, first, pltpu.roll(second, narrow, axis=1)).astype(
        jnp.int32
    )
    info_ref[0:8, :] = zeros[2 * plan.all_pairs : 2 * plan.all_pairs + 8]
    mine = named[2 * plan.all_pairs : 2 * plan.all_pairs + 8]
    noise = jnp.sum(jnp.where(mine, noise_ref[...], 0.0), axis=1, keepdims=True)
    info_ref[8:16, :] = jnp.broadcast_to(noise, (8, 128))
    copies[4].wait()
    images = images_ref[...].reshape(plan.count_img * radial, angles)
    for two in range(plan.count_img // 2):
        spectrum = nt(table_ref[...], images[2 * two * radial : 2 * (two + 1) * radial])
        lows = []
        for i in range(2):
            part = spectrum[:, i * radial : (i + 1) * radial]
            turned = jnp.concatenate(
                [(part * cb_ref[...]).astype(jnp.bfloat16), (part * sb_ref[...]).astype(jnp.bfloat16)],
                axis=1,
            )
            coef = nn(turned, wave_ref[...])
            lows.append(coef[:total].reshape(plan.devices, 2 * quota, radial))
            span = 2 * plan.all_pairs
            for e in range(2):
                at = 8 * (e * plan.count_img + 2 * two + i)
                part = coef[total + e * span : total + (e + 1) * span]
                wide_ref[:, at : at + 8, :] = part.reshape(span // 8, 8, radial)
        size = 4 * quota
        coef_ref[:, size * two : size * (two + 1), :] = jnp.concatenate(lows, axis=1).astype(
            jnp.bfloat16
        )
    lane = iota((plan.vecs, radial), 1)
    zero_here = iota((radial, radial), 0) + 1
    for device in range(plan.devices):
        rows, chosen = [], []
        for i in range(pairs):
            at = device * pairs + i
            rows.append(wide_ref[at // 4, pl.ds(at % 4, 2 * plan.vecs, stride=4), :])
            chosen.append(low_bits(zero_here == zero_ref[at : at + 1, :]))
        rows = jnp.concatenate(rows, axis=0).astype(jnp.bfloat16)
        packed = nn(rows, jnp.concatenate(chosen, axis=1))
        tiles = []
        for i in range(pairs):
            start = 2 * i * plan.vecs
            both = packed[start : start + 2 * plan.vecs, i * radial : (i + 1) * radial]
            tiles.append(jnp.where(lane < narrow, both[: plan.vecs], both[plan.vecs :]))
        coef_ref[device, plan.low_rows : plan.rows, :] = jnp.concatenate(tiles, axis=0).astype(
            jnp.bfloat16
        )


def thirds(x):
    first = x.astype(jnp.bfloat16)
    rest = x - first.astype(jnp.float32)
    second = rest.astype(jnp.bfloat16)
    third = (rest - second.astype(jnp.float32)).astype(jnp.bfloat16)
    return first, second, third


def outer(u, v):
    u1, u2, u3 = thirds(u)
    v1, v2, v3 = thirds(v)
    return lax.dot_general(
        jnp.concatenate([u1, u1, u1, u2, u2, u3], axis=0),
        jnp.concatenate([v1, v2, v3, v1, v2, v1], axis=0),
        (((0,), (0,)), ((), ())),
        preferred_element_type=jnp.float32,
    )


def first_lane(halved, lane, step):
    return (lane & 64 if halved else jnp.zeros_like(lane)) + step * 8


def pivot_panels(panels, halves, step):
    shape = (8, 128)
    sub, lane = iota(shape, 0), iota(shape, 1)
    blocks = [
        [
            jnp.take_along_axis(panel, first_lane(halved, lane, step) + j, axis=1)
            for j in range(8)
        ]
        for panel, halved in zip(panels, halves)
    ]
    for i in range(8):
        unit = (sub == i).astype(jnp.float32)
        for at, cols in enumerate(blocks):
            inverse = 1.0 / jnp.broadcast_to(cols[i][i : i + 1], shape)
            weight = (cols[i] - unit) * inverse
            blocks[at] = [
                unit - weight
                if j == i
                else cols[j] - weight * jnp.broadcast_to(cols[j][i : i + 1], shape)
                for j in range(8)
            ]
    solved = []
    for panel, halved, cols in zip(panels, halves, blocks):
        offset = lane - first_lane(halved, lane, step)
        unit = (sub == offset).astype(jnp.float32)
        lines = jnp.where((offset < 0) | (offset >= 8), panel, unit)
        total = cols[0] * jnp.broadcast_to(lines[0:1], shape)
        for j in range(1, 8):
            total = total + cols[j] * jnp.broadcast_to(lines[j : j + 1], shape)
        solved.append(total)
    return solved


def scales_of(matrix, halved):
    row, lane = iota(matrix.shape, 0), iota(matrix.shape, 1)
    diagonal = jnp.where(row == (lane & 63 if halved else lane), matrix, 0.0)
    across = lax.rsqrt(jnp.sum(diagonal, axis=0, keepdims=True))
    if not halved:
        return across * lax.rsqrt(jnp.sum(diagonal, axis=1, keepdims=True))
    left = lax.rsqrt(jnp.sum(jnp.where(lane < 64, diagonal, 0.0), axis=1, keepdims=True))
    right = lax.rsqrt(jnp.sum(jnp.where(lane < 64, 0.0, diagonal), axis=1, keepdims=True))
    return across * jnp.where(lane < 64, left, right)


def sweep(matrices, step, carry):
    start = pl.multiple_of(step * 8, 8)
    halves = [halved for _, _, halved in matrices]
    panels = [ref[m, pl.ds(start, 8), :] for ref, m, _ in matrices]
    solved = pivot_panels(panels, halves, step)
    sub, lane = iota((8, 128), 0), iota((8, 128), 1)
    for (ref, m, halved), panel, fresh in zip(matrices, panels, solved):
        height = ref.shape[1]
        done = (lane & 63 if halved else lane) < step * 8
        unit = (sub == lane - first_lane(halved, lane, step)).astype(jnp.float32)
        update = outer(jnp.where(done, -panel, panel), fresh + unit)
        if halved:
            update = jnp.where(iota((height, 128), 1) < 64, update[:height], update[height:])
        ref[m] = ref[m] - update
        ref[m, pl.ds(start, 8), :] = fresh
    return carry


def filter_kernel(
    plan, info_ref, recv_ref,
    back_ref, shrink_ref, wide_ref, full_ref, pair_ref, pick_ref, held_ref, full_scale_ref, pair_scale_ref,
):
    radial, quota, pairs, narrow = plan.radial, plan.quota, plan.pairs, plan.narrow
    low_rows = plan.low_rows
    rows = plan.devices * plan.vecs
    low_part = recv_ref[:, :low_rows, :].astype(jnp.float32)
    wide_ref[...] = low_part.reshape(plan.devices * low_rows, radial)
    square = (radial, radial)
    strip = (narrow, radial)
    eye = (iota(square, 0) == iota(square, 1)).astype(jnp.float32)
    twins = (iota(strip, 0) == (iota(strip, 1) & (narrow - 1))).astype(jnp.float32)
    first = iota(strip, 1) < narrow
    noises = []
    for s in range(quota):
        noises.append(info_ref[8 + s : 9 + s, :])
        zero = info_ref[s : s + 1, :].astype(jnp.int32)
        pick = low_bits(iota(square, 0) + 1 == zero)
        pick_ref[s] = pick
        vectors = wide_ref[pl.ds(s, rows, stride=quota), :].astype(jnp.bfloat16)
        coef = nn(vectors, pick).astype(jnp.bfloat16)
        covariance = tn(coef, coef) / float(rows) + noises[s] * eye
        scale = scales_of(covariance, False)
        full_scale_ref[s] = scale
        full_ref[s] = covariance * scale
    high_part = recv_ref[:, low_rows:, :].astype(jnp.float32)
    for i in range(pairs):
        coef = high_part[:, i * plan.vecs : (i + 1) * plan.vecs, :].reshape(rows, radial)
        coef = coef.astype(jnp.bfloat16)
        held_ref[i] = coef
        gram = tn(coef, coef)
        gram = jnp.where(first, gram[:narrow], gram[narrow:])
        at = 8 + quota + 2 * i
        noise = jnp.where(first, info_ref[at : at + 1, :], info_ref[at + 1 : at + 2, :])
        noises.append(noise)
        covariance = gram / float(rows) + noise * twins
        scale = scales_of(covariance, True)
        pair_scale_ref[i] = scale
        pair_ref[i] = covariance * scale
    lower = [(full_ref, m, False) for m in range(quota)]
    upper = [(pair_ref, m, True) for m in range(pairs)]
    lax.fori_loop(0, narrow // 8, functools.partial(sweep, lower + upper), 0)
    lax.fori_loop(narrow // 8, radial // 8, functools.partial(sweep, lower), 0)
    for s in range(quota):
        shrink = eye - noises[s] * (full_ref[s] * full_scale_ref[s])
        shrink_ref[s * radial : (s + 1) * radial, :] = shrink.astype(jnp.bfloat16)
        pick = pick_ref[s]
        moved = lax.dot_general(
            shrink.astype(jnp.bfloat16),
            pick,
            (((0,), (1,)), ((), ())),
            preferred_element_type=jnp.float32,
        ).astype(jnp.bfloat16)
        spread = nn(pick, moved).astype(jnp.bfloat16)
        vectors = wide_ref[pl.ds(s, rows, stride=quota), :].astype(jnp.bfloat16)
        wide_ref[pl.ds(s, rows, stride=quota), :] = nn(vectors, spread)
    shape = (plan.devices, low_rows, radial)
    back_ref[:, :low_rows, :] = wide_ref[...].reshape(shape).astype(jnp.bfloat16)
    tiles = []
    for i in range(pairs):
        shrink = twins - noises[quota + i] * (pair_ref[i] * pair_scale_ref[i])
        start = quota * radial + i * narrow
        shrink_ref[start : start + narrow, :] = shrink.astype(jnp.bfloat16)
        blocks = jnp.concatenate(
            [jnp.where(first, shrink, 0.0), jnp.where(first, 0.0, shrink)], axis=0
        )
        filtered = nt(held_ref[i], blocks.astype(jnp.bfloat16))
        tiles.append(filtered.reshape(plan.devices, plan.vecs, radial))
    back_ref[:, low_rows:, :] = jnp.concatenate(tiles, axis=1).astype(jnp.bfloat16)


def synthesis_kernel(plan, table_ref, cb_ref, sb_ref, wave_ref, zero_ref, recv_ref, out_ref, wide_ref, held_ref):
    radial, total, quota, pairs = plan.radial, plan.total, plan.quota, plan.pairs
    lane = iota((plan.vecs, radial), 1)
    zero_here = iota((radial, radial), 0) + 1
    for device in range(plan.devices):
        tile = recv_ref[device, plan.low_rows : plan.rows, :].astype(jnp.float32)
        rows, chosen = [], []
        for i in range(pairs):
            at = device * pairs + i
            packed = tile[i * plan.vecs : (i + 1) * plan.vecs]
            rows += [jnp.where(lane < plan.narrow, packed, 0.0), jnp.where(lane < plan.narrow, 0.0, packed)]
            chosen.append(low_bits(zero_here == zero_ref[at : at + 1, :]))
        rows = jnp.concatenate(rows, axis=0).astype(jnp.bfloat16)
        spread = nt(rows, jnp.concatenate(chosen, axis=0))
        for i in range(pairs):
            at = device * pairs + i
            start = 2 * i * plan.vecs
            wide_ref[at // 4, pl.ds(at % 4, 2 * plan.vecs, stride=4), :] = spread[
                start : start + 2 * plan.vecs, i * radial : (i + 1) * radial
            ]
    span = 2 * plan.all_pairs
    for i in range(plan.count_img):
        low = recv_ref[:, 2 * quota * i : 2 * quota * (i + 1), :].astype(jnp.float32)
        at = [8 * (e * plan.count_img + i) for e in range(2)]
        high = [wide_ref[:, a : a + 8, :].reshape(span, radial) for a in at]
        filtered = jnp.concatenate([low.reshape(total, radial)] + high, axis=0)
        turned = nt(filtered.astype(jnp.bfloat16), wave_ref[...])
        spectrum = turned[:, :radial] * cb_ref[...] + turned[:, radial:] * sb_ref[...]
        held_ref[:, i * radial : (i + 1) * radial] = spectrum.astype(jnp.bfloat16)
    image = tn(held_ref[...], table_ref[...]).astype(jnp.bfloat16)
    out_ref[...] = image.reshape(out_ref.shape)


def wiener_kernel(plan, own_ref, other_ref, out_ref):
    radial, quota, narrow = plan.radial, plan.quota, plan.narrow
    batch_at = lax.axis_index("batch")
    lane = iota((narrow, radial), 1)
    for batch, ref in ((batch_at, own_ref), (1 - batch_at, other_ref)):
        for s in range(quota):
            out_ref[batch * quota + s] = ref[s * radial : (s + 1) * radial, :].astype(jnp.float32)
            at = plan.half + batch * quota + s
            start = quota * radial + (s // 2) * narrow
            pair = ref[start : start + narrow, :].astype(jnp.float32)
            if s % 2:
                pair = pltpu.roll(pair, narrow, axis=1)
            out_ref[at, 0:narrow, :] = jnp.where(lane < narrow, pair, 0.0)
            out_ref[at, narrow:radial, :] = jnp.zeros((radial - narrow, radial), jnp.float32)


VMEM = pl.BlockSpec(memory_space=pltpu.VMEM)
HBM = pl.BlockSpec(memory_space=pltpu.HBM)


def call(kernel, outs, ins, scratch=()):
    return pl.pallas_call(
        kernel,
        out_shape=outs,
        in_specs=ins,
        out_specs=jax.tree.map(lambda _: VMEM, outs),
        scratch_shapes=scratch,
        compiler_params=pltpu.CompilerParams(vmem_limit_bytes=16 << 20),
    )


def fast_device(plan, images, radial_counts, order, zeros_table, noise_var):
    both = ("batch", "freq")
    radial, total, quota, pairs = plan.radial, plan.total, plan.quota, plan.pairs
    shape = jax.ShapeDtypeStruct
    block = shape((plan.devices, plan.rows, radial), jnp.bfloat16)
    coef, table, cb, sb, wave, zero, info = call(
        functools.partial(analysis_kernel, plan),
        (
            block,
            shape((2 * total, plan.angles), jnp.bfloat16),
            shape((2 * total, radial), jnp.float32),
            shape((2 * total, radial), jnp.float32),
            shape((2 * radial, radial), jnp.bfloat16),
            shape((plan.all_pairs, radial), jnp.int32),
            shape((16, radial), jnp.float32),
        ),
        [HBM] * 5,
        [
            pltpu.VMEM((plan.all_pairs // 4, 8 * plan.vecs, radial), jnp.float32),
            pltpu.VMEM((1, total), jnp.int32),
            pltpu.VMEM((1, total), jnp.int32),
            pltpu.VMEM((1, total), jnp.float32),
            pltpu.VMEM(zeros_table.shape, jnp.int32),
            pltpu.VMEM(images.shape, jnp.bfloat16),
            pltpu.SemaphoreType.DMA((5,)),
        ],
    )(
        *(
            pltpu.with_memory_space_constraint(array, pltpu.HBM)
            for array in (
                order.reshape(1, total),
                radial_counts.reshape(1, total),
                noise_var.reshape(1, total),
                zeros_table,
                images,
            )
        )
    )
    recv = lax.all_to_all(coef, both, split_axis=0, concat_axis=0, tiled=True)
    back, shrink = call(
        functools.partial(filter_kernel, plan),
        (block, shape((quota * radial + pairs * plan.narrow, radial), jnp.bfloat16)),
        [VMEM, VMEM],
        [
            pltpu.VMEM((plan.devices * plan.low_rows, radial), jnp.float32),
            pltpu.VMEM((quota, radial, radial), jnp.float32),
            pltpu.VMEM((pairs, plan.narrow, radial), jnp.float32),
            pltpu.VMEM((quota, radial, radial), jnp.bfloat16),
            pltpu.VMEM((pairs, plan.devices * plan.vecs, radial), jnp.bfloat16),
            pltpu.VMEM((quota, radial, radial), jnp.float32),
            pltpu.VMEM((pairs, plan.narrow, radial), jnp.float32),
        ],
    )(info, recv)
    returned = lax.all_to_all(back, both, split_axis=0, concat_axis=0, tiled=True)
    other = lax.ppermute(shrink, "batch", [(0, 1), (1, 0)])
    wiener_blocks = call(
        functools.partial(wiener_kernel, plan),
        shape((plan.owned, radial, radial), jnp.float32),
        [VMEM] * 2,
    )(shrink, other)
    denoised = call(
        functools.partial(synthesis_kernel, plan),
        shape((plan.count_img, radial, plan.angles), jnp.bfloat16),
        [VMEM] * 6,
        [
            pltpu.VMEM((plan.all_pairs // 4, 8 * plan.vecs, radial), jnp.float32),
            pltpu.VMEM((2 * total, plan.count_img * radial), jnp.bfloat16),
        ],
    )(table, cb, sb, wave, zero, returned)
    return denoised, wiener_blocks


def solution(mesh):
    owners, batches = mesh.shape["freq"], mesh.shape["batch"]

    def body(images, radial_counts, order, zeros_table, noise_var):
        plan = Plan(images.shape, order.shape[0], owners, batches)
        device = functools.partial(fast_device, plan) if plan.fits else per_device
        return device(images, radial_counts, order, zeros_table, noise_var)

    return jax.shard_map(
        body,
        mesh=mesh,
        in_specs=(P(("batch", "freq"), None, None), P(), P(), P(), P()),
        out_specs=(P(("batch", "freq"), None, None), P("freq", None, None)),
        check_vma=False,
    )
```

```python
import functools
import math

import jax
import jax.numpy as jnp
from jax import lax
from jax.experimental import pallas as pl
from jax.experimental.pallas import tpu as pltpu
from jax.sharding import PartitionSpec as P


def make_table(freqs, angles):
    angle_index = jnp.arange(angles, dtype=jnp.int32)
    product = angle_index[:, None] * freqs[None, :] % angles
    phase = 2.0 * math.pi / angles * product.astype(jnp.float32)
    factor = math.sqrt(2.0 / angles)
    return jnp.concatenate([factor * jnp.cos(phase), factor * jnp.sin(phase)], axis=1).astype(
        jnp.bfloat16
    )


def make_basis(freqs, zero_rows, counts, radial):
    slots = zero_rows.shape[1]
    freq_float = freqs.astype(jnp.float32)[:, None, None]
    scaled = math.pi * (zero_rows.astype(jnp.float32)[:, :, None] + 0.5 * freq_float - 0.25)
    grid = (jnp.arange(radial, dtype=jnp.float32) + 0.5) / radial
    phase = scaled * grid[None, None, :] - 0.5 * math.pi * freq_float - 0.25 * math.pi
    keep = jnp.arange(slots, dtype=jnp.int32)[None, :, None] < counts[:, None, None]
    values = math.sqrt(2.0 / radial) * jnp.cos(phase)
    return jnp.where(keep, values, jnp.zeros_like(values)).astype(jnp.bfloat16)


def gram_of(blocks):
    return jnp.einsum("kvq,kvp->kqp", blocks, blocks, preferred_element_type=jnp.float32)


def shrink_from(gram, noise, vectors):
    width = gram.shape[1]
    eye = jnp.eye(width, dtype=jnp.float32)
    covariance = gram / vectors + noise[:, None, None] * eye
    lower = jnp.linalg.cholesky(covariance)
    inv_lower = jax.scipy.linalg.solve_triangular(
        lower, jnp.broadcast_to(eye, covariance.shape), lower=True
    )
    inverse = jnp.einsum("kmq,kmp->kqp", inv_lower, inv_lower, precision=lax.Precision.HIGHEST)
    return eye - noise[:, None, None] * inverse


def apply_shrink(shrinkage, blocks):
    return jnp.einsum(
        "kqp,kvp->kvq", shrinkage.astype(jnp.bfloat16), blocks, preferred_element_type=jnp.float32
    ).astype(jnp.bfloat16)


def per_device(images, radial_counts, order, zeros_table, noise_var):
    count_img, radial, angles = images.shape
    total_freq = order.shape[0]
    block = min(64, total_freq)
    nblocks = total_freq // block
    flat = images.reshape(count_img * radial, angles)
    slot_rows = jnp.take(zeros_table, order, axis=0)
    slot_counts = jnp.take(radial_counts, order)

    def block_tools(index):
        start = index * block
        freqs = lax.dynamic_slice_in_dim(order, start, block)
        table = make_table(freqs, angles)
        rows_here = lax.dynamic_slice_in_dim(slot_rows, start, block, 0)
        counts_here = lax.dynamic_slice_in_dim(slot_counts, start, block)
        return (table, make_basis(freqs, rows_here, counts_here, radial))

    def analyse(index):
        table, basis = block_tools(index)
        spectrum = jnp.dot(flat, table, preferred_element_type=jnp.float32)
        spectrum = spectrum.astype(jnp.bfloat16).reshape(count_img, radial, 2, block)
        return jnp.einsum(
            "ircj,jqr->jciq", spectrum, basis, preferred_element_type=jnp.float32
        ).astype(jnp.bfloat16)

    pieces = lax.map(analyse, jnp.arange(nblocks, dtype=jnp.int32))
    moved = pieces.reshape(total_freq, 2 * count_img, radial)
    owners = lax.axis_size("freq")
    owned = total_freq // owners
    batches = lax.axis_size("batch")
    mine = lax.dynamic_slice_in_dim(order, lax.axis_index("freq") * owned, owned)
    noise_mine = jnp.take(noise_var, mine)
    half_slots = owned // 2
    narrow = radial // 2
    grouped = moved.reshape(owners, owned, 2 * count_img, radial)
    lower_part = grouped[:, :half_slots].reshape(owners * half_slots, 2 * count_img, radial)
    upper_part = grouped[:, half_slots:, :, :narrow].reshape(
        owners * half_slots, 2 * count_img, narrow
    )
    low_recv, high_recv = (
        lax.all_to_all(lower_part, "freq", split_axis=0, concat_axis=1, tiled=True),
        lax.all_to_all(upper_part, "freq", split_axis=0, concat_axis=1, tiled=True),
    )
    gram_low, gram_high = lax.psum((gram_of(low_recv), gram_of(high_recv)), "batch")
    vectors = low_recv.shape[1] * batches
    shrink_lower = shrink_from(gram_low, noise_mine[:half_slots], vectors)
    shrink_upper = shrink_from(gram_high, noise_mine[half_slots:], vectors)
    low_back, high_back = (
        lax.all_to_all(
            apply_shrink(shrink_lower, low_recv), "freq", split_axis=1, concat_axis=0, tiled=True
        ),
        lax.all_to_all(
            apply_shrink(shrink_upper, high_recv), "freq", split_axis=1, concat_axis=0, tiled=True
        ),
    )
    high_wide = jnp.pad(high_back, ((0, 0), (0, 0), (0, radial - narrow)))
    returned = jnp.concatenate(
        [
            low_back.reshape(owners, half_slots, 2 * count_img, radial),
            high_wide.reshape(owners, half_slots, 2 * count_img, radial),
        ],
        axis=1,
    )
    returned = returned.reshape(total_freq, 2 * count_img, radial)
    upper_wide = jnp.pad(shrink_upper, ((0, 0), (0, radial - narrow), (0, radial - narrow)))
    wiener_blocks = jnp.concatenate([shrink_lower, upper_wide], axis=0)
    filtered_blocks = returned.reshape(nblocks, block, 2, count_img, radial)

    def synthesise(index, total):
        table, basis = block_tools(index)
        piece = lax.dynamic_index_in_dim(filtered_blocks, index, 0, keepdims=False)
        spectrum_out = jnp.einsum(
            "jciq,jqr->ircj", piece, basis, preferred_element_type=jnp.float32
        )
        spectrum_out = spectrum_out.astype(jnp.bfloat16).reshape(count_img * radial, 2 * block)
        return total + lax.dot_general(
            spectrum_out, table, (((1,), (1,)), ((), ())), preferred_element_type=jnp.float32
        )

    summed = lax.fori_loop(
        0, nblocks, synthesise, jnp.zeros((count_img * radial, angles), jnp.float32)
    )
    denoised = summed.astype(jnp.bfloat16).reshape(count_img, radial, angles)
    return (denoised, wiener_blocks)


COSINE = (
    -0.9999999889445799,
    4.934801116644238,
    -4.058694745523659,
    1.3351580223122241,
    -0.23502902263765682,
    0.025358285764913842,
    -0.0015936782168350142,
)


def cosine_of(turns, steps):
    x = ((turns & (steps - 1)) - steps // 2).astype(jnp.float32) * (2.0 / steps)
    y = x * x
    total = jnp.full_like(y, COSINE[-1])
    for term in COSINE[-2::-1]:
        total = total * y + term
    return total


def iota(shape, dim):
    return lax.broadcasted_iota(jnp.int32, shape, dim)


def nt(a, b):
    return lax.dot_general(a, b, (((1,), (1,)), ((), ())), preferred_element_type=jnp.float32)


def tn(a, b):
    return lax.dot_general(a, b, (((0,), (0,)), ((), ())), preferred_element_type=jnp.float32)


def nn(a, b):
    return jnp.dot(a, b, preferred_element_type=jnp.float32)


def low_bits(mask):
    return mask.astype(jnp.float32).astype(jnp.bfloat16)


class Plan:
    def __init__(self, images, order, owners, batches):
        self.count_img, self.radial, self.angles = images
        self.total = order
        self.owners, self.batches = owners, batches
        self.devices = owners * batches
        self.owned = order // owners
        self.half = self.owned // 2
        self.vecs = 2 * self.count_img
        self.quota = 4
        self.pairs = self.quota // 2
        self.narrow = self.radial // 2
        self.low_rows = self.vecs * self.quota
        self.rows = self.low_rows + self.vecs * self.pairs
        self.all_pairs = self.devices * self.pairs
        power = lambda n: n > 0 and n & (n - 1) == 0
        self.fits = (
            batches == 2
            and self.half == batches * self.quota
            and self.radial == 128
            and self.count_img == 4
            and all(power(n) for n in (self.angles, self.total, owners))
            and self.angles == 2 * self.total
        )

    def slot_of(self, device, place):
        batch, owner = device // self.owners, device & (self.owners - 1)
        return owner * self.owned + batch * self.quota + place


def analysis_kernel(
    plan, order_hbm, counts_hbm, noise_hbm, zeros_hbm, images_hbm,
    coef_ref, table_ref, cb_ref, sb_ref, wave_ref, zero_ref, info_ref,
    wide_ref, order_ref, counts_ref, noise_ref, zeros_ref, images_ref, sems,
):
    radial, angles, total = plan.radial, plan.angles, plan.total
    quota, pairs, narrow = plan.quota, plan.pairs, plan.narrow
    copies = [
        pltpu.make_async_copy(source, target, sems.at[at])
        for at, (source, target) in enumerate(
            (
                (order_hbm, order_ref),
                (counts_hbm, counts_ref),
                (noise_hbm, noise_ref),
                (zeros_hbm, zeros_ref),
                (images_hbm, images_ref),
            )
        )
    ]
    for copy in copies:
        copy.start()
    turns = (iota((radial, radial), 1) + 1) * (2 * iota((radial, radial), 0) + 1)
    factor = math.sqrt(2.0 / radial)
    wave_ref[0:radial, :] = (factor * cosine_of(turns, 4 * radial)).astype(jnp.bfloat16)
    wave_ref[radial : 2 * radial, :] = (-factor * cosine_of(turns - radial, 4 * radial)).astype(
        jnp.bfloat16
    )
    sub, lane = iota((8, total), 0), iota((8, total), 1)
    place = sub & (quota - 1)
    jump = (place // pairs) * plan.owned + 2 * (place & (pairs - 1))
    slots = [place + plan.slot_of(device, 0) for device in range(plan.devices)]
    slots += [
        jump + (plan.slot_of(2 * four, 0) + plan.half + e)
        for e in range(2)
        for four in range(plan.all_pairs // 4)
    ]
    jump = (sub // pairs) * plan.owned + 2 * (sub & (pairs - 1))
    slots += [
        jump + (plan.slot_of(4 * eight, 0) + plan.half + e)
        for e in range(2)
        for eight in range(plan.all_pairs // 8)
    ]
    device = lax.axis_index("batch") * plan.owners + lax.axis_index("freq")
    slots.append(plan.slot_of(device, (sub // quota) * plan.half + place))
    slots.append(slots[-1])
    pick = jnp.concatenate([(slot == lane).astype(jnp.float32) for slot in slots], axis=0)
    pick = pick.astype(jnp.bfloat16)
    copies[0].wait()
    spread = lambda ref: jnp.broadcast_to(ref[...].astype(jnp.float32), (128, total)).astype(jnp.bfloat16)
    every_freq = nt(pick, spread(order_ref)).astype(jnp.int32)
    freq = every_freq[: 2 * total]
    lane = iota((2 * total, 128), 1)
    sine_row = (iota((2 * total, 128), 0) // quota) & 1
    lag = sine_row * (angles // 4)
    flip = (1 - 2 * (freq & 1)).astype(jnp.float32)
    factor = math.sqrt(2.0 / angles)
    for part in range(angles // 256):
        cosine = cosine_of((lane + part * 128) * freq - lag, angles) * factor
        table_ref[:, part * 128 : part * 128 + 128] = cosine.astype(jnp.bfloat16)
        start = angles // 2 + part * 128
        table_ref[:, start : start + 128] = (cosine * flip).astype(jnp.bfloat16)
    steps = 16 * radial
    turns = (2 * freq - 1) * (2 * lane + 1) - 4 * radial * freq - 2 * radial
    cb_ref[...] = cosine_of(turns, steps)
    sb_ref[...] = cosine_of(turns - steps // 4, steps)
    for copy in copies[1:4]:
        copy.wait()
    named = every_freq[2 * total :]
    named = jnp.concatenate([named] * (total // 128), axis=1) == iota((named.shape[0], total), 1)
    pick = low_bits(named)
    zeros = nn(pick, zeros_ref[...].astype(jnp.float32).astype(jnp.bfloat16))
    counts = nt(pick, spread(counts_ref)).astype(jnp.int32)
    zeros = jnp.where(iota(zeros.shape, 1) < counts, zeros, 0.0)
    first, second = zeros[: plan.all_pairs], zeros[plan.all_pairs : 2 * plan.all_pairs]
    lane = iota((plan.all_pairs, radial), 1)
    zero_ref[...] = jnp.where(lane < narrow, first, pltpu.roll(second, narrow, axis=1)).astype(
        jnp.int32
    )
    info_ref[0:8, :] = zeros[2 * plan.all_pairs : 2 * plan.all_pairs + 8]
    mine = named[2 * plan.all_pairs : 2 * plan.all_pairs + 8]
    noise = jnp.sum(jnp.where(mine, noise_ref[...], 0.0), axis=1, keepdims=True)
    info_ref[8:16, :] = jnp.broadcast_to(noise, (8, 128))
    copies[4].wait()
    images = images_ref[...].reshape(plan.count_img * radial, angles)
    for two in range(plan.count_img // 2):
        spectrum = nt(table_ref[...], images[2 * two * radial : 2 * (two + 1) * radial])
        lows = []
        for i in range(2):
            part = spectrum[:, i * radial : (i + 1) * radial]
            turned = jnp.concatenate(
                [(part * cb_ref[...]).astype(jnp.bfloat16), (part * sb_ref[...]).astype(jnp.bfloat16)],
                axis=1,
            )
            coef = nn(turned, wave_ref[...])
            lows.append(coef[:total].reshape(plan.devices, 2 * quota, radial))
            span = 2 * plan.all_pairs
            for e in range(2):
                at = 8 * (e * plan.count_img + 2 * two + i)
                part = coef[total + e * span : total + (e + 1) * span]
                wide_ref[:, at : at + 8, :] = part.reshape(span // 8, 8, radial)
        size = 4 * quota
        coef_ref[:, size * two : size * (two + 1), :] = jnp.concatenate(lows, axis=1).astype(
            jnp.bfloat16
        )
    lane = iota((plan.vecs, radial), 1)
    zero_here = iota((radial, radial), 0) + 1
    for device in range(plan.devices):
        rows, chosen = [], []
        for i in range(pairs):
            at = device * pairs + i
            rows.append(wide_ref[at // 4, pl.ds(at % 4, 2 * plan.vecs, stride=4), :])
            chosen.append(low_bits(zero_here == zero_ref[at : at + 1, :]))
        rows = jnp.concatenate(rows, axis=0).astype(jnp.bfloat16)
        packed = nn(rows, jnp.concatenate(chosen, axis=1))
        tiles = []
        for i in range(pairs):
            start = 2 * i * plan.vecs
            both = packed[start : start + 2 * plan.vecs, i * radial : (i + 1) * radial]
            tiles.append(jnp.where(lane < narrow, both[: plan.vecs], both[plan.vecs :]))
        coef_ref[device, plan.low_rows : plan.rows, :] = jnp.concatenate(tiles, axis=0).astype(
            jnp.bfloat16
        )


def thirds(x):
    first = x.astype(jnp.bfloat16)
    rest = x - first.astype(jnp.float32)
    second = rest.astype(jnp.bfloat16)
    third = (rest - second.astype(jnp.float32)).astype(jnp.bfloat16)
    return first, second, third


def outer(u, v):
    u1, u2, u3 = thirds(u)
    v1, v2, v3 = thirds(v)
    return lax.dot_general(
        jnp.concatenate([u1, u1, u1, u2, u2, u3], axis=0),
        jnp.concatenate([v1, v2, v3, v1, v2, v1], axis=0),
        (((0,), (0,)), ((), ())),
        preferred_element_type=jnp.float32,
    )


def columns(panel, halved, first):
    lane = iota(panel.shape, 1)
    base = (lane & 64 if halved else jnp.zeros_like(lane)) + first
    return [jnp.take_along_axis(panel, base + j, axis=1) for j in range(8)]


def offset_of(shape, halved, first):
    lane = iota(shape, 1)
    return (lane & 63 if halved else lane) - first


def spread_row(panel, j):
    return jnp.broadcast_to(panel[j : j + 1], panel.shape)


def invert_blocks(blocks):
    sub = iota((8, 128), 0)
    for i in range(8):
        unit = (sub == i).astype(jnp.float32)
        for at, cols in enumerate(blocks):
            weight = (cols[i] - unit) * (1.0 / spread_row(cols[i], i))
            blocks[at] = [
                unit - weight if j == i else cols[j] - weight * spread_row(cols[j], i)
                for j in range(8)
            ]
    return blocks


def solve_panel(panel, cols, halved, first):
    offset = offset_of(panel.shape, halved, first)
    unit = (iota(panel.shape, 0) == offset).astype(jnp.float32)
    lines = jnp.where((offset < 0) | (offset >= 8), panel, unit)
    total = cols[0] * spread_row(lines, 0)
    for j in range(1, 8):
        total = total + cols[j] * spread_row(lines, j)
    return total


def take_away(panel, factors, solved, halved, first):
    offset = offset_of(panel.shape, halved, first)
    total = jnp.where((offset >= 0) & (offset < 8), 0.0, panel)
    other = factors[1] * spread_row(solved, 1)
    for j in range(0, 8, 2):
        total = total - factors[j] * spread_row(solved, j)
        if j:
            other = other + factors[j + 1] * spread_row(solved, j + 1)
    return total - other


def scales_of(matrix, halved):
    row, lane = iota(matrix.shape, 0), iota(matrix.shape, 1)
    diagonal = jnp.where(row == (lane & 63 if halved else lane), matrix, 0.0)
    across = lax.rsqrt(jnp.sum(diagonal, axis=0, keepdims=True))
    if not halved:
        return across * lax.rsqrt(jnp.sum(diagonal, axis=1, keepdims=True))
    left = lax.rsqrt(jnp.sum(jnp.where(lane < 64, diagonal, 0.0), axis=1, keepdims=True))
    right = lax.rsqrt(jnp.sum(jnp.where(lane < 64, 0.0, diagonal), axis=1, keepdims=True))
    return across * jnp.where(lane < 64, left, right)


def sweep(matrices):
    upper, lower, starts = [], [], []
    for ref, m, _, first in matrices:
        start = pl.multiple_of(first, 16)
        starts.append(start)
        upper.append(ref[m, pl.ds(start, 8), :])
        lower.append(ref[m, pl.ds(start + 8, 8), :])
    kinds = [(halved, first) for _, _, halved, first in matrices]
    blocks = invert_blocks([columns(p, h, f) for p, (h, f) in zip(upper, kinds)])
    factors = [columns(p, h, f) for p, (h, f) in zip(lower, kinds)]
    tops = [solve_panel(p, c, h, f) for p, c, (h, f) in zip(upper, blocks, kinds)]
    rests = [take_away(p, c, t, h, f) for p, c, t, (h, f) in zip(lower, factors, tops, kinds)]
    factors = [columns(t, h, f + 8) for t, (h, f) in zip(tops, kinds)]
    blocks = invert_blocks([columns(r, h, f + 8) for r, (h, f) in zip(rests, kinds)])
    bottoms = [solve_panel(r, c, h, f + 8) for r, c, (h, f) in zip(rests, blocks, kinds)]
    tops = [take_away(t, c, b, h, f + 8) for t, c, b, (h, f) in zip(tops, factors, bottoms, kinds)]
    shape = (16, 128)
    for at, (ref, m, halved, first) in enumerate(matrices):
        height = ref.shape[1]
        panel = jnp.concatenate([upper[at], lower[at]], axis=0)
        fresh = jnp.concatenate([tops[at], bottoms[at]], axis=0)
        offset = offset_of(shape, halved, first)
        unit = (iota(shape, 0) == offset).astype(jnp.float32)
        update = outer(jnp.where(offset < 0, -panel, panel), fresh + unit)
        if halved:
            update = jnp.where(iota((height, 128), 1) < 64, update[:height], update[height:])
        ref[m] = ref[m] - update
        ref[m, pl.ds(starts[at], 16), :] = fresh


def filter_kernel(
    plan, info_ref, recv_ref,
    back_ref, shrink_ref, wide_ref, full_ref, pair_ref, pick_ref, held_ref, full_scale_ref, pair_scale_ref,
):
    radial, quota, pairs, narrow = plan.radial, plan.quota, plan.pairs, plan.narrow
    low_rows = plan.low_rows
    rows = plan.devices * plan.vecs
    low_part = recv_ref[:, :low_rows, :].astype(jnp.float32)
    wide_ref[...] = low_part.reshape(plan.devices * low_rows, radial)
    square = (radial, radial)
    strip = (narrow, radial)
    eye = (iota(square, 0) == iota(square, 1)).astype(jnp.float32)
    twins = (iota(strip, 0) == (iota(strip, 1) & (narrow - 1))).astype(jnp.float32)
    first = iota(strip, 1) < narrow
    noises = []
    for s in range(quota):
        noises.append(info_ref[8 + s : 9 + s, :])
        zero = info_ref[s : s + 1, :].astype(jnp.int32)
        pick = low_bits(iota(square, 0) + 1 == zero)
        pick_ref[s] = pick
        vectors = wide_ref[pl.ds(s, rows, stride=quota), :].astype(jnp.bfloat16)
        coef = nn(vectors, pick).astype(jnp.bfloat16)
        covariance = tn(coef, coef) / float(rows) + noises[s] * eye
        scale = scales_of(covariance, False)
        full_scale_ref[s] = scale
        full_ref[s] = covariance * scale
    high_part = recv_ref[:, low_rows:, :].astype(jnp.float32)
    for i in range(pairs):
        coef = high_part[:, i * plan.vecs : (i + 1) * plan.vecs, :].reshape(rows, radial)
        coef = coef.astype(jnp.bfloat16)
        held_ref[i] = coef
        gram = tn(coef, coef)
        gram = jnp.where(first, gram[:narrow], gram[narrow:])
        at = 8 + quota + 2 * i
        noise = jnp.where(first, info_ref[at : at + 1, :], info_ref[at + 1 : at + 2, :])
        noises.append(noise)
        covariance = gram / float(rows) + noise * twins
        scale = scales_of(covariance, True)
        pair_scale_ref[i] = scale
        pair_ref[i] = covariance * scale
    steps, half_steps = radial // 16, narrow // 16

    def body(step, carry):
        matrices = [(full_ref, m, False, 16 * step) for m in range(quota)]
        part = 16 * (step % half_steps)
        sweep(matrices + [(pair_ref, step // half_steps, True, part)])
        return carry

    lax.fori_loop(0, steps, body, 0)
    for s in range(quota):
        shrink = eye - noises[s] * (full_ref[s] * full_scale_ref[s])
        shrink_ref[s * radial : (s + 1) * radial, :] = shrink.astype(jnp.bfloat16)
        pick = pick_ref[s]
        moved = lax.dot_general(
            shrink.astype(jnp.bfloat16),
            pick,
            (((0,), (1,)), ((), ())),
            preferred_element_type=jnp.float32,
        ).astype(jnp.bfloat16)
        spread = nn(pick, moved).astype(jnp.bfloat16)
        vectors = wide_ref[pl.ds(s, rows, stride=quota), :].astype(jnp.bfloat16)
        wide_ref[pl.ds(s, rows, stride=quota), :] = nn(vectors, spread)
    shape = (plan.devices, low_rows, radial)
    back_ref[:, :low_rows, :] = wide_ref[...].reshape(shape).astype(jnp.bfloat16)
    tiles = []
    for i in range(pairs):
        shrink = twins - noises[quota + i] * (pair_ref[i] * pair_scale_ref[i])
        start = quota * radial + i * narrow
        shrink_ref[start : start + narrow, :] = shrink.astype(jnp.bfloat16)
        blocks = jnp.concatenate(
            [jnp.where(first, shrink, 0.0), jnp.where(first, 0.0, shrink)], axis=0
        )
        filtered = nt(held_ref[i], blocks.astype(jnp.bfloat16))
        tiles.append(filtered.reshape(plan.devices, plan.vecs, radial))
    back_ref[:, low_rows:, :] = jnp.concatenate(tiles, axis=1).astype(jnp.bfloat16)


def synthesis_kernel(plan, table_ref, cb_ref, sb_ref, wave_ref, zero_ref, recv_ref, out_ref, wide_ref, held_ref):
    radial, total, quota, pairs = plan.radial, plan.total, plan.quota, plan.pairs
    lane = iota((plan.vecs, radial), 1)
    zero_here = iota((radial, radial), 0) + 1
    for device in range(plan.devices):
        tile = recv_ref[device, plan.low_rows : plan.rows, :].astype(jnp.float32)
        rows, chosen = [], []
        for i in range(pairs):
            at = device * pairs + i
            packed = tile[i * plan.vecs : (i + 1) * plan.vecs]
            rows += [jnp.where(lane < plan.narrow, packed, 0.0), jnp.where(lane < plan.narrow, 0.0, packed)]
            chosen.append(low_bits(zero_here == zero_ref[at : at + 1, :]))
        rows = jnp.concatenate(rows, axis=0).astype(jnp.bfloat16)
        spread = nt(rows, jnp.concatenate(chosen, axis=0))
        for i in range(pairs):
            at = device * pairs + i
            start = 2 * i * plan.vecs
            wide_ref[at // 4, pl.ds(at % 4, 2 * plan.vecs, stride=4), :] = spread[
                start : start + 2 * plan.vecs, i * radial : (i + 1) * radial
            ]
    span = 2 * plan.all_pairs
    for i in range(plan.count_img):
        low = recv_ref[:, 2 * quota * i : 2 * quota * (i + 1), :].astype(jnp.float32)
        at = [8 * (e * plan.count_img + i) for e in range(2)]
        high = [wide_ref[:, a : a + 8, :].reshape(span, radial) for a in at]
        filtered = jnp.concatenate([low.reshape(total, radial)] + high, axis=0)
        turned = nt(filtered.astype(jnp.bfloat16), wave_ref[...])
        spectrum = turned[:, :radial] * cb_ref[...] + turned[:, radial:] * sb_ref[...]
        held_ref[:, i * radial : (i + 1) * radial] = spectrum.astype(jnp.bfloat16)
    image = tn(held_ref[...], table_ref[...]).astype(jnp.bfloat16)
    out_ref[...] = image.reshape(out_ref.shape)


def wiener_kernel(plan, own_ref, other_ref, out_ref):
    radial, quota, narrow = plan.radial, plan.quota, plan.narrow
    batch_at = lax.axis_index("batch")
    lane = iota((narrow, radial), 1)
    for batch, ref in ((batch_at, own_ref), (1 - batch_at, other_ref)):
        for s in range(quota):
            out_ref[batch * quota + s] = ref[s * radial : (s + 1) * radial, :].astype(jnp.float32)
            at = plan.half + batch * quota + s
            start = quota * radial + (s // 2) * narrow
            pair = ref[start : start + narrow, :].astype(jnp.float32)
            if s % 2:
                pair = pltpu.roll(pair, narrow, axis=1)
            out_ref[at, 0:narrow, :] = jnp.where(lane < narrow, pair, 0.0)
            out_ref[at, narrow:radial, :] = jnp.zeros((radial - narrow, radial), jnp.float32)


VMEM = pl.BlockSpec(memory_space=pltpu.VMEM)
HBM = pl.BlockSpec(memory_space=pltpu.HBM)


def call(kernel, outs, ins, scratch=()):
    return pl.pallas_call(
        kernel,
        out_shape=outs,
        in_specs=ins,
        out_specs=jax.tree.map(lambda _: VMEM, outs),
        scratch_shapes=scratch,
        compiler_params=pltpu.CompilerParams(vmem_limit_bytes=16 << 20),
    )


def fast_device(plan, images, radial_counts, order, zeros_table, noise_var):
    both = ("batch", "freq")
    radial, total, quota, pairs = plan.radial, plan.total, plan.quota, plan.pairs
    shape = jax.ShapeDtypeStruct
    block = shape((plan.devices, plan.rows, radial), jnp.bfloat16)
    coef, table, cb, sb, wave, zero, info = call(
        functools.partial(analysis_kernel, plan),
        (
            block,
            shape((2 * total, plan.angles), jnp.bfloat16),
            shape((2 * total, radial), jnp.float32),
            shape((2 * total, radial), jnp.float32),
            shape((2 * radial, radial), jnp.bfloat16),
            shape((plan.all_pairs, radial), jnp.int32),
            shape((16, radial), jnp.float32),
        ),
        [HBM] * 5,
        [
            pltpu.VMEM((plan.all_pairs // 4, 8 * plan.vecs, radial), jnp.float32),
            pltpu.VMEM((1, total), jnp.int32),
            pltpu.VMEM((1, total), jnp.int32),
            pltpu.VMEM((1, total), jnp.float32),
            pltpu.VMEM(zeros_table.shape, jnp.int32),
            pltpu.VMEM(images.shape, jnp.bfloat16),
            pltpu.SemaphoreType.DMA((5,)),
        ],
    )(
        *(
            pltpu.with_memory_space_constraint(array, pltpu.HBM)
            for array in (
                order.reshape(1, total),
                radial_counts.reshape(1, total),
                noise_var.reshape(1, total),
                zeros_table,
                images,
            )
        )
    )
    recv = lax.all_to_all(coef, both, split_axis=0, concat_axis=0, tiled=True)
    back, shrink = call(
        functools.partial(filter_kernel, plan),
        (block, shape((quota * radial + pairs * plan.narrow, radial), jnp.bfloat16)),
        [VMEM, VMEM],
        [
            pltpu.VMEM((plan.devices * plan.low_rows, radial), jnp.float32),
            pltpu.VMEM((quota, radial, radial), jnp.float32),
            pltpu.VMEM((pairs, plan.narrow, radial), jnp.float32),
            pltpu.VMEM((quota, radial, radial), jnp.bfloat16),
            pltpu.VMEM((pairs, plan.devices * plan.vecs, radial), jnp.bfloat16),
            pltpu.VMEM((quota, radial, radial), jnp.float32),
            pltpu.VMEM((pairs, plan.narrow, radial), jnp.float32),
        ],
    )(info, recv)
    returned = lax.all_to_all(back, both, split_axis=0, concat_axis=0, tiled=True)
    other = lax.ppermute(shrink, "batch", [(0, 1), (1, 0)])
    wiener_blocks = call(
        functools.partial(wiener_kernel, plan),
        shape((plan.owned, radial, radial), jnp.float32),
        [VMEM] * 2,
    )(shrink, other)
    denoised = call(
        functools.partial(synthesis_kernel, plan),
        shape((plan.count_img, radial, plan.angles), jnp.bfloat16),
        [VMEM] * 6,
        [
            pltpu.VMEM((plan.all_pairs // 4, 8 * plan.vecs, radial), jnp.float32),
            pltpu.VMEM((2 * total, plan.count_img * radial), jnp.bfloat16),
        ],
    )(table, cb, sb, wave, zero, returned)
    return denoised, wiener_blocks


def solution(mesh):
    owners, batches = mesh.shape["freq"], mesh.shape["batch"]

    def body(images, radial_counts, order, zeros_table, noise_var):
        plan = Plan(images.shape, order.shape[0], owners, batches)
        device = functools.partial(fast_device, plan) if plan.fits else per_device
        return device(images, radial_counts, order, zeros_table, noise_var)

    return jax.shard_map(
        body,
        mesh=mesh,
        in_specs=(P(("batch", "freq"), None, None), P(), P(), P(), P()),
        out_specs=(P(("batch", "freq"), None, None), P("freq", None, None)),
        check_vma=False,
    )
```

```python
import functools
import math

import jax
import jax.numpy as jnp
from jax import lax
from jax.experimental import pallas as pl
from jax.experimental.pallas import tpu as pltpu
from jax.sharding import PartitionSpec as P


def make_table(freqs, angles):
    angle_index = jnp.arange(angles, dtype=jnp.int32)
    product = angle_index[:, None] * freqs[None, :] % angles
    phase = 2.0 * math.pi / angles * product.astype(jnp.float32)
    factor = math.sqrt(2.0 / angles)
    return jnp.concatenate([factor * jnp.cos(phase), factor * jnp.sin(phase)], axis=1).astype(
        jnp.bfloat16
    )


def make_basis(freqs, zero_rows, counts, radial):
    slots = zero_rows.shape[1]
    freq_float = freqs.astype(jnp.float32)[:, None, None]
    scaled = math.pi * (zero_rows.astype(jnp.float32)[:, :, None] + 0.5 * freq_float - 0.25)
    grid = (jnp.arange(radial, dtype=jnp.float32) + 0.5) / radial
    phase = scaled * grid[None, None, :] - 0.5 * math.pi * freq_float - 0.25 * math.pi
    keep = jnp.arange(slots, dtype=jnp.int32)[None, :, None] < counts[:, None, None]
    values = math.sqrt(2.0 / radial) * jnp.cos(phase)
    return jnp.where(keep, values, jnp.zeros_like(values)).astype(jnp.bfloat16)


def gram_of(blocks):
    return jnp.einsum("kvq,kvp->kqp", blocks, blocks, preferred_element_type=jnp.float32)


def shrink_from(gram, noise, vectors):
    width = gram.shape[1]
    eye = jnp.eye(width, dtype=jnp.float32)
    covariance = gram / vectors + noise[:, None, None] * eye
    lower = jnp.linalg.cholesky(covariance)
    inv_lower = jax.scipy.linalg.solve_triangular(
        lower, jnp.broadcast_to(eye, covariance.shape), lower=True
    )
    inverse = jnp.einsum("kmq,kmp->kqp", inv_lower, inv_lower, precision=lax.Precision.HIGHEST)
    return eye - noise[:, None, None] * inverse


def apply_shrink(shrinkage, blocks):
    return jnp.einsum(
        "kqp,kvp->kvq", shrinkage.astype(jnp.bfloat16), blocks, preferred_element_type=jnp.float32
    ).astype(jnp.bfloat16)


def per_device(images, radial_counts, order, zeros_table, noise_var):
    count_img, radial, angles = images.shape
    total_freq = order.shape[0]
    block = min(64, total_freq)
    nblocks = total_freq // block
    flat = images.reshape(count_img * radial, angles)
    slot_rows = jnp.take(zeros_table, order, axis=0)
    slot_counts = jnp.take(radial_counts, order)

    def block_tools(index):
        start = index * block
        freqs = lax.dynamic_slice_in_dim(order, start, block)
        table = make_table(freqs, angles)
        rows_here = lax.dynamic_slice_in_dim(slot_rows, start, block, 0)
        counts_here = lax.dynamic_slice_in_dim(slot_counts, start, block)
        return (table, make_basis(freqs, rows_here, counts_here, radial))

    def analyse(index):
        table, basis = block_tools(index)
        spectrum = jnp.dot(flat, table, preferred_element_type=jnp.float32)
        spectrum = spectrum.astype(jnp.bfloat16).reshape(count_img, radial, 2, block)
        return jnp.einsum(
            "ircj,jqr->jciq", spectrum, basis, preferred_element_type=jnp.float32
        ).astype(jnp.bfloat16)

    pieces = lax.map(analyse, jnp.arange(nblocks, dtype=jnp.int32))
    moved = pieces.reshape(total_freq, 2 * count_img, radial)
    owners = lax.axis_size("freq")
    owned = total_freq // owners
    batches = lax.axis_size("batch")
    mine = lax.dynamic_slice_in_dim(order, lax.axis_index("freq") * owned, owned)
    noise_mine = jnp.take(noise_var, mine)
    half_slots = owned // 2
    narrow = radial // 2
    grouped = moved.reshape(owners, owned, 2 * count_img, radial)
    lower_part = grouped[:, :half_slots].reshape(owners * half_slots, 2 * count_img, radial)
    upper_part = grouped[:, half_slots:, :, :narrow].reshape(
        owners * half_slots, 2 * count_img, narrow
    )
    low_recv, high_recv = (
        lax.all_to_all(lower_part, "freq", split_axis=0, concat_axis=1, tiled=True),
        lax.all_to_all(upper_part, "freq", split_axis=0, concat_axis=1, tiled=True),
    )
    gram_low, gram_high = lax.psum((gram_of(low_recv), gram_of(high_recv)), "batch")
    vectors = low_recv.shape[1] * batches
    shrink_lower = shrink_from(gram_low, noise_mine[:half_slots], vectors)
    shrink_upper = shrink_from(gram_high, noise_mine[half_slots:], vectors)
    low_back, high_back = (
        lax.all_to_all(
            apply_shrink(shrink_lower, low_recv), "freq", split_axis=1, concat_axis=0, tiled=True
        ),
        lax.all_to_all(
            apply_shrink(shrink_upper, high_recv), "freq", split_axis=1, concat_axis=0, tiled=True
        ),
    )
    high_wide = jnp.pad(high_back, ((0, 0), (0, 0), (0, radial - narrow)))
    returned = jnp.concatenate(
        [
            low_back.reshape(owners, half_slots, 2 * count_img, radial),
            high_wide.reshape(owners, half_slots, 2 * count_img, radial),
        ],
        axis=1,
    )
    returned = returned.reshape(total_freq, 2 * count_img, radial)
    upper_wide = jnp.pad(shrink_upper, ((0, 0), (0, radial - narrow), (0, radial - narrow)))
    wiener_blocks = jnp.concatenate([shrink_lower, upper_wide], axis=0)
    filtered_blocks = returned.reshape(nblocks, block, 2, count_img, radial)

    def synthesise(index, total):
        table, basis = block_tools(index)
        piece = lax.dynamic_index_in_dim(filtered_blocks, index, 0, keepdims=False)
        spectrum_out = jnp.einsum(
            "jciq,jqr->ircj", piece, basis, preferred_element_type=jnp.float32
        )
        spectrum_out = spectrum_out.astype(jnp.bfloat16).reshape(count_img * radial, 2 * block)
        return total + lax.dot_general(
            spectrum_out, table, (((1,), (1,)), ((), ())), preferred_element_type=jnp.float32
        )

    summed = lax.fori_loop(
        0, nblocks, synthesise, jnp.zeros((count_img * radial, angles), jnp.float32)
    )
    denoised = summed.astype(jnp.bfloat16).reshape(count_img, radial, angles)
    return (denoised, wiener_blocks)


COSINE = (
    -0.9999999889445799,
    4.934801116644238,
    -4.058694745523659,
    1.3351580223122241,
    -0.23502902263765682,
    0.025358285764913842,
    -0.0015936782168350142,
)


def cosine_of(turns, steps):
    x = ((turns & (steps - 1)) - steps // 2).astype(jnp.float32) * (2.0 / steps)
    y = x * x
    total = jnp.full_like(y, COSINE[-1])
    for term in COSINE[-2::-1]:
        total = total * y + term
    return total


def iota(shape, dim):
    return lax.broadcasted_iota(jnp.int32, shape, dim)


def nt(a, b):
    return lax.dot_general(a, b, (((1,), (1,)), ((), ())), preferred_element_type=jnp.float32)


def tn(a, b):
    return lax.dot_general(a, b, (((0,), (0,)), ((), ())), preferred_element_type=jnp.float32)


def nn(a, b):
    return jnp.dot(a, b, preferred_element_type=jnp.float32)


def low_bits(mask):
    return mask.astype(jnp.float32).astype(jnp.bfloat16)


class Plan:
    def __init__(self, images, order, owners, batches):
        self.count_img, self.radial, self.angles = images
        self.total = order
        self.owners, self.batches = owners, batches
        self.devices = owners * batches
        self.owned = order // owners
        self.half = self.owned // 2
        self.vecs = 2 * self.count_img
        self.quota = 4
        self.pairs = self.quota // 2
        self.narrow = self.radial // 2
        self.low_rows = self.vecs * self.quota
        self.rows = self.low_rows + self.vecs * self.pairs
        self.all_pairs = self.devices * self.pairs
        power = lambda n: n > 0 and n & (n - 1) == 0
        self.fits = (
            batches == 2
            and self.half == batches * self.quota
            and self.radial == 128
            and self.count_img == 4
            and all(power(n) for n in (self.angles, self.total, owners))
            and self.angles == 2 * self.total == 4 * self.radial
        )

    def slot_of(self, device, place):
        batch, owner = device // self.owners, device & (self.owners - 1)
        return owner * self.owned + batch * self.quota + place


def row_pairs(x, y):
    blocks, width = x.shape[0] // 8, x.shape[1]
    x, y = x.reshape(blocks, 8, width), y.reshape(blocks, 8, width)
    front = iota(x.shape, 1) < 4
    first = jnp.where(front, x, pltpu.roll(y, 4, axis=1))
    second = jnp.where(front, pltpu.roll(x, 4, axis=1), y)
    return jnp.concatenate([first, second], axis=1).reshape(16 * blocks, width)


def analysis_kernel(
    plan, order_hbm, counts_hbm, noise_hbm, zeros_hbm, images_hbm,
    coef_ref, table_ref, cb_ref, sb_ref, wave_ref, zero_ref, info_ref,
    wide_ref, order_ref, counts_ref, noise_ref, zeros_ref, images_ref, sems,
):
    radial, angles, total = plan.radial, plan.angles, plan.total
    quota, pairs, narrow = plan.quota, plan.pairs, plan.narrow
    copies = [
        pltpu.make_async_copy(source, target, sems.at[at])
        for at, (source, target) in enumerate(
            (
                (order_hbm, order_ref),
                (counts_hbm, counts_ref),
                (noise_hbm, noise_ref),
                (zeros_hbm, zeros_ref),
                (images_hbm, images_ref),
            )
        )
    ]
    for copy in copies:
        copy.start()
    turns = (iota((radial, radial), 1) + 1) * (2 * iota((radial, radial), 0) + 1)
    factor = math.sqrt(2.0 / radial)
    wave_ref[0:radial, :] = (factor * cosine_of(turns, 4 * radial)).astype(jnp.bfloat16)
    wave_ref[radial : 2 * radial, :] = (-factor * cosine_of(turns - radial, 4 * radial)).astype(
        jnp.bfloat16
    )
    sub, lane = iota((8, total), 0), iota((8, total), 1)
    place = sub & (quota - 1)
    jump = (sub // quota) * plan.owned + place
    slots = [jump + plan.slot_of(2 * two, 0) for two in range(plan.devices // 2)]
    jump = (sub // pairs) * plan.owned + 2 * (sub & (pairs - 1))
    slots += [
        jump + (plan.slot_of(4 * eight, 0) + plan.half + e)
        for e in range(2)
        for eight in range(plan.all_pairs // 8)
    ]
    device = lax.axis_index("batch") * plan.owners + lax.axis_index("freq")
    partner = (1 - lax.axis_index("batch")) * plan.owners + lax.axis_index("freq")
    slots += [plan.slot_of(d, (sub // quota) * plan.half + place) for d in (device, partner)]
    pick = jnp.concatenate([(slot == lane).astype(jnp.float32) for slot in slots], axis=0)
    pick = pick.astype(jnp.bfloat16)
    copies[0].wait()
    spread = lambda ref: jnp.broadcast_to(ref[...].astype(jnp.float32), (128, total)).astype(jnp.bfloat16)
    every_freq = nt(pick, spread(order_ref)).astype(jnp.int32)
    freq = every_freq[:total]
    lane = iota((total, 128), 1)
    factor = math.sqrt(2.0 / angles)
    turns = lane * freq
    cosine = cosine_of(turns, angles) * factor
    sine = cosine_of(turns - angles // 4, angles) * factor
    odd, flip = freq & 1, (1 - (freq & 2)).astype(jnp.float32)
    even_part, odd_part = (1 - odd).astype(jnp.float32) * flip, odd.astype(jnp.float32) * flip
    mirror = (1 - 2 * odd).astype(jnp.float32)
    turned_cosine = even_part * cosine - odd_part * sine
    turned_sine = even_part * sine + odd_part * cosine
    parts = [
        (cosine, sine),
        (turned_cosine, turned_sine),
        (mirror * cosine, mirror * sine),
        (mirror * turned_cosine, mirror * turned_sine),
    ]
    for part, (x, y) in enumerate(parts):
        table_ref[:, part * 128 : part * 128 + 128] = row_pairs(x, y).astype(jnp.bfloat16)
    steps = 16 * radial
    turns = (2 * freq - 1) * (2 * lane + 1) - 4 * radial * freq - 2 * radial
    cosine, sine = cosine_of(turns, steps), cosine_of(turns - steps // 4, steps)
    cb_ref[...] = row_pairs(cosine, cosine)
    sb_ref[...] = row_pairs(sine, sine)
    for copy in copies[1:4]:
        copy.wait()
    named = every_freq[total - 2 * plan.all_pairs :]
    named = jnp.concatenate([named] * (total // 128), axis=1) == iota((named.shape[0], total), 1)
    pick = low_bits(named)
    zeros = nn(pick, zeros_ref[...].astype(jnp.float32).astype(jnp.bfloat16))
    counts = nt(pick, spread(counts_ref)).astype(jnp.int32)
    zeros = jnp.where(iota(zeros.shape, 1) < counts, zeros, 0.0)
    first, second = zeros[: plan.all_pairs], zeros[plan.all_pairs : 2 * plan.all_pairs]
    lane = iota((plan.all_pairs, radial), 1)
    zero_ref[...] = jnp.where(lane < narrow, first, pltpu.roll(second, narrow, axis=1)).astype(
        jnp.int32
    )
    square = (radial, radial)
    ones = jnp.ones((8, radial), jnp.bfloat16)
    for s in range(quota):
        at = 2 * plan.all_pairs + s
        chosen = low_bits(iota(square, 0) + 1 == zeros[at : at + 1].astype(jnp.int32))
        info_ref[s : s + 1, :] = nt(ones, chosen)[0:1]
    mine = named[2 * plan.all_pairs : 2 * plan.all_pairs + 8]
    noise = jnp.sum(jnp.where(mine, noise_ref[...], 0.0), axis=1, keepdims=True)
    info_ref[8:16, :] = jnp.broadcast_to(noise, (8, 128))
    info_ref[16:32, :] = zeros[2 * plan.all_pairs :]
    copies[4].wait()
    images = images_ref[...].reshape(plan.count_img * radial, angles)
    for two in range(plan.count_img // 2):
        spectrum = nt(table_ref[...], images[2 * two * radial : 2 * (two + 1) * radial])
        lows = []
        for i in range(2):
            part = spectrum[:, i * radial : (i + 1) * radial]
            turned = jnp.concatenate(
                [(part * cb_ref[...]).astype(jnp.bfloat16), (part * sb_ref[...]).astype(jnp.bfloat16)],
                axis=1,
            )
            coef = nn(turned, wave_ref[...])
            lows.append(coef[:total].reshape(plan.devices, 2 * quota, radial))
            span = 2 * plan.all_pairs
            for e in range(2):
                at = 8 * (e * plan.count_img + 2 * two + i)
                part = coef[total + e * span : total + (e + 1) * span]
                wide_ref[:, at : at + 8, :] = part.reshape(span // 8, 8, radial)
        size = 4 * quota
        coef_ref[:, size * two : size * (two + 1), :] = jnp.concatenate(lows, axis=1).astype(
            jnp.bfloat16
        )
    lane = iota((plan.vecs, radial), 1)
    zero_here = iota((radial, radial), 0) + 1
    for device in range(plan.devices):
        rows, chosen = [], []
        for i in range(pairs):
            at = device * pairs + i
            rows.append(wide_ref[at // 4, pl.ds(at % 4, 2 * plan.vecs, stride=4), :])
            chosen.append(low_bits(zero_here == zero_ref[at : at + 1, :]))
        rows = jnp.concatenate(rows, axis=0).astype(jnp.bfloat16)
        packed = nn(rows, jnp.concatenate(chosen, axis=1))
        tiles = []
        for i in range(pairs):
            start = 2 * i * plan.vecs
            both = packed[start : start + 2 * plan.vecs, i * radial : (i + 1) * radial]
            tiles.append(jnp.where(lane < narrow, both[: plan.vecs], both[plan.vecs :]))
        coef_ref[device, plan.low_rows : plan.rows, :] = jnp.concatenate(tiles, axis=0).astype(
            jnp.bfloat16
        )


def thirds(x):
    first = x.astype(jnp.bfloat16)
    rest = x - first.astype(jnp.float32)
    second = rest.astype(jnp.bfloat16)
    third = (rest - second.astype(jnp.float32)).astype(jnp.bfloat16)
    return first, second, third


def outer(u, v):
    u1, u2, u3 = thirds(u)
    v1, v2, v3 = thirds(v)
    return lax.dot_general(
        jnp.concatenate([u1, u1, u1, u2, u2, u3], axis=0),
        jnp.concatenate([v1, v2, v3, v1, v2, v1], axis=0),
        (((0,), (0,)), ((), ())),
        preferred_element_type=jnp.float32,
    )


def columns(panel, halved, first):
    lane = iota(panel.shape, 1)
    base = (lane & 64 if halved else jnp.zeros_like(lane)) + first
    return [jnp.take_along_axis(panel, base + j, axis=1) for j in range(8)]


def offset_of(shape, halved, first):
    lane = iota(shape, 1)
    return (lane & 63 if halved else lane) - first


def spread_row(panel, j):
    return jnp.broadcast_to(panel[j : j + 1], panel.shape)


def invert_blocks(blocks):
    sub = iota((8, 128), 0)
    for i in range(8):
        unit = (sub == i).astype(jnp.float32)
        for at, cols in enumerate(blocks):
            weight = (cols[i] - unit) * (1.0 / spread_row(cols[i], i))
            blocks[at] = [
                unit - weight if j == i else cols[j] - weight * spread_row(cols[j], i)
                for j in range(8)
            ]
    return blocks


def solve_panel(panel, cols, halved, first):
    offset = offset_of(panel.shape, halved, first)
    unit = (iota(panel.shape, 0) == offset).astype(jnp.float32)
    lines = jnp.where((offset < 0) | (offset >= 8), panel, unit)
    total = cols[0] * spread_row(lines, 0)
    for j in range(1, 8):
        total = total + cols[j] * spread_row(lines, j)
    return total


def take_away(panel, factors, solved, halved, first):
    offset = offset_of(panel.shape, halved, first)
    total = jnp.where((offset >= 0) & (offset < 8), 0.0, panel)
    other = factors[1] * spread_row(solved, 1)
    for j in range(0, 8, 2):
        total = total - factors[j] * spread_row(solved, j)
        if j:
            other = other + factors[j + 1] * spread_row(solved, j + 1)
    return total - other


def scales_of(matrix, halved):
    row, lane = iota(matrix.shape, 0), iota(matrix.shape, 1)
    diagonal = jnp.where(row == (lane & 63 if halved else lane), matrix, 0.0)
    across = lax.rsqrt(jnp.sum(diagonal, axis=0, keepdims=True))
    if not halved:
        return across * lax.rsqrt(jnp.sum(diagonal, axis=1, keepdims=True))
    left = lax.rsqrt(jnp.sum(jnp.where(lane < 64, diagonal, 0.0), axis=1, keepdims=True))
    right = lax.rsqrt(jnp.sum(jnp.where(lane < 64, 0.0, diagonal), axis=1, keepdims=True))
    return across * jnp.where(lane < 64, left, right)


def sweep(matrices):
    upper, lower, starts = [], [], []
    for ref, m, _, first in matrices:
        start = pl.multiple_of(first, 16)
        starts.append(start)
        upper.append(ref[m, pl.ds(start, 8), :])
        lower.append(ref[m, pl.ds(start + 8, 8), :])
    kinds = [(halved, first) for _, _, halved, first in matrices]
    blocks = invert_blocks([columns(p, h, f) for p, (h, f) in zip(upper, kinds)])
    factors = [columns(p, h, f) for p, (h, f) in zip(lower, kinds)]
    tops = [solve_panel(p, c, h, f) for p, c, (h, f) in zip(upper, blocks, kinds)]
    rests = [take_away(p, c, t, h, f) for p, c, t, (h, f) in zip(lower, factors, tops, kinds)]
    factors = [columns(t, h, f + 8) for t, (h, f) in zip(tops, kinds)]
    blocks = invert_blocks([columns(r, h, f + 8) for r, (h, f) in zip(rests, kinds)])
    bottoms = [solve_panel(r, c, h, f + 8) for r, c, (h, f) in zip(rests, blocks, kinds)]
    tops = [take_away(t, c, b, h, f + 8) for t, c, b, (h, f) in zip(tops, factors, bottoms, kinds)]
    shape = (16, 128)
    for at, (ref, m, halved, first) in enumerate(matrices):
        height = ref.shape[1]
        panel = jnp.concatenate([upper[at], lower[at]], axis=0)
        fresh = jnp.concatenate([tops[at], bottoms[at]], axis=0)
        offset = offset_of(shape, halved, first)
        unit = (iota(shape, 0) == offset).astype(jnp.float32)
        update = outer(jnp.where(offset < 0, -panel, panel), fresh + unit)
        if halved:
            update = jnp.where(iota((height, 128), 1) < 64, update[:height], update[height:])
        ref[m] = ref[m] - update
        ref[m, pl.ds(starts[at], 16), :] = fresh


def filter_kernel(
    plan, info_ref, recv_ref,
    back_ref, shrink_ref, wide_ref, full_ref, pair_ref, kept_ref, held_ref, full_scale_ref, pair_scale_ref,
):
    radial, quota, pairs, narrow = plan.radial, plan.quota, plan.pairs, plan.narrow
    low_rows = plan.low_rows
    rows = plan.devices * plan.vecs
    low_part = recv_ref[:, :low_rows, :].astype(jnp.float32)
    wide_ref[...] = low_part.reshape(plan.devices * low_rows, radial)
    square = (radial, radial)
    strip = (narrow, radial)
    eye = (iota(square, 0) == iota(square, 1)).astype(jnp.float32)
    twins = (iota(strip, 0) == (iota(strip, 1) & (narrow - 1))).astype(jnp.float32)
    first = iota(strip, 1) < narrow
    noises = []
    for s in range(quota):
        noises.append(info_ref[8 + s : 9 + s, :])
        coef = wide_ref[pl.ds(s, rows, stride=quota), :] * info_ref[s : s + 1, :]
        coef = coef.astype(jnp.bfloat16)
        kept_ref[s] = coef
        covariance = tn(coef, coef) / float(rows) + noises[s] * eye
        scale = scales_of(covariance, False)
        full_scale_ref[s] = scale
        full_ref[s] = covariance * scale
    high_part = recv_ref[:, low_rows:, :].astype(jnp.float32)
    for i in range(pairs):
        coef = high_part[:, i * plan.vecs : (i + 1) * plan.vecs, :].reshape(rows, radial)
        coef = coef.astype(jnp.bfloat16)
        held_ref[i] = coef
        gram = tn(coef, coef)
        gram = jnp.where(first, gram[:narrow], gram[narrow:])
        at = 8 + quota + 2 * i
        noise = jnp.where(first, info_ref[at : at + 1, :], info_ref[at + 1 : at + 2, :])
        noises.append(noise)
        covariance = gram / float(rows) + noise * twins
        scale = scales_of(covariance, True)
        pair_scale_ref[i] = scale
        pair_ref[i] = covariance * scale
    steps, half_steps = radial // 16, narrow // 16

    def body(step, carry):
        matrices = [(full_ref, m, False, 16 * step) for m in range(quota)]
        part = 16 * (step % half_steps)
        sweep(matrices + [(pair_ref, step // half_steps, True, part)])
        return carry

    lax.fori_loop(0, steps, body, 0)
    for s in range(quota):
        shrink = eye - noises[s] * (full_ref[s] * full_scale_ref[s])
        shrink_ref[s * radial : (s + 1) * radial, :] = shrink.astype(jnp.bfloat16)
        wide_ref[pl.ds(s, rows, stride=quota), :] = nt(kept_ref[s], shrink.astype(jnp.bfloat16))
    shape = (plan.devices, low_rows, radial)
    back_ref[:, :low_rows, :] = wide_ref[...].reshape(shape).astype(jnp.bfloat16)
    tiles = []
    for i in range(pairs):
        shrink = twins - noises[quota + i] * (pair_ref[i] * pair_scale_ref[i])
        start = quota * radial + i * narrow
        shrink_ref[start : start + narrow, :] = shrink.astype(jnp.bfloat16)
        blocks = jnp.concatenate(
            [jnp.where(first, shrink, 0.0), jnp.where(first, 0.0, shrink)], axis=0
        )
        filtered = nt(held_ref[i], blocks.astype(jnp.bfloat16))
        tiles.append(filtered.reshape(plan.devices, plan.vecs, radial))
    back_ref[:, low_rows:, :] = jnp.concatenate(tiles, axis=1).astype(jnp.bfloat16)


def synthesis_kernel(plan, table_ref, cb_ref, sb_ref, wave_ref, zero_ref, recv_ref, out_ref, wide_ref, held_ref):
    radial, total, quota, pairs = plan.radial, plan.total, plan.quota, plan.pairs
    lane = iota((plan.vecs, radial), 1)
    zero_here = iota((radial, radial), 0) + 1
    for device in range(plan.devices):
        tile = recv_ref[device, plan.low_rows : plan.rows, :].astype(jnp.float32)
        rows, chosen = [], []
        for i in range(pairs):
            at = device * pairs + i
            packed = tile[i * plan.vecs : (i + 1) * plan.vecs]
            rows += [jnp.where(lane < plan.narrow, packed, 0.0), jnp.where(lane < plan.narrow, 0.0, packed)]
            chosen.append(low_bits(zero_here == zero_ref[at : at + 1, :]))
        rows = jnp.concatenate(rows, axis=0).astype(jnp.bfloat16)
        spread = nt(rows, jnp.concatenate(chosen, axis=0))
        for i in range(pairs):
            at = device * pairs + i
            start = 2 * i * plan.vecs
            wide_ref[at // 4, pl.ds(at % 4, 2 * plan.vecs, stride=4), :] = spread[
                start : start + 2 * plan.vecs, i * radial : (i + 1) * radial
            ]
    span = 2 * plan.all_pairs
    for i in range(plan.count_img):
        low = recv_ref[:, 2 * quota * i : 2 * quota * (i + 1), :].astype(jnp.float32)
        at = [8 * (e * plan.count_img + i) for e in range(2)]
        high = [wide_ref[:, a : a + 8, :].reshape(span, radial) for a in at]
        filtered = jnp.concatenate([low.reshape(total, radial)] + high, axis=0)
        turned = nt(filtered.astype(jnp.bfloat16), wave_ref[...])
        spectrum = turned[:, :radial] * cb_ref[...] + turned[:, radial:] * sb_ref[...]
        held_ref[:, i * radial : (i + 1) * radial] = spectrum.astype(jnp.bfloat16)
    image = tn(held_ref[...], table_ref[...]).astype(jnp.bfloat16)
    out_ref[...] = image.reshape(out_ref.shape)


def wiener_kernel(plan, own_ref, other_ref, info_ref, out_ref):
    radial, quota, narrow = plan.radial, plan.quota, plan.narrow
    batch_at = lax.axis_index("batch")
    lane = iota((narrow, radial), 1)
    zero_here = iota((radial, radial), 0) + 1
    for batch, ref, start in ((batch_at, own_ref, 16), (1 - batch_at, other_ref, 24)):
        for s in range(quota):
            zero = info_ref[start + s : start + s + 1, :].astype(jnp.int32)
            chosen = low_bits(zero_here == zero)
            half_way = nn(ref[s * radial : (s + 1) * radial, :], chosen).astype(jnp.bfloat16)
            out_ref[batch * quota + s] = tn(chosen, half_way)
            at = plan.half + batch * quota + s
            first = quota * radial + (s // 2) * narrow
            pair = ref[first : first + narrow, :].astype(jnp.float32)
            if s % 2:
                pair = pltpu.roll(pair, narrow, axis=1)
            out_ref[at, 0:narrow, :] = jnp.where(lane < narrow, pair, 0.0)
            out_ref[at, narrow:radial, :] = jnp.zeros((radial - narrow, radial), jnp.float32)


VMEM = pl.BlockSpec(memory_space=pltpu.VMEM)
HBM = pl.BlockSpec(memory_space=pltpu.HBM)


def call(kernel, outs, ins, scratch=()):
    return pl.pallas_call(
        kernel,
        out_shape=outs,
        in_specs=ins,
        out_specs=jax.tree.map(lambda _: VMEM, outs),
        scratch_shapes=scratch,
        compiler_params=pltpu.CompilerParams(vmem_limit_bytes=16 << 20),
    )


def fast_device(plan, images, radial_counts, order, zeros_table, noise_var):
    both = ("batch", "freq")
    radial, total, quota, pairs = plan.radial, plan.total, plan.quota, plan.pairs
    shape = jax.ShapeDtypeStruct
    block = shape((plan.devices, plan.rows, radial), jnp.bfloat16)
    coef, table, cb, sb, wave, zero, info = call(
        functools.partial(analysis_kernel, plan),
        (
            block,
            shape((2 * total, plan.angles), jnp.bfloat16),
            shape((2 * total, radial), jnp.float32),
            shape((2 * total, radial), jnp.float32),
            shape((2 * radial, radial), jnp.bfloat16),
            shape((plan.all_pairs, radial), jnp.int32),
            shape((32, radial), jnp.float32),
        ),
        [HBM] * 5,
        [
            pltpu.VMEM((plan.all_pairs // 4, 8 * plan.vecs, radial), jnp.float32),
            pltpu.VMEM((1, total), jnp.int32),
            pltpu.VMEM((1, total), jnp.int32),
            pltpu.VMEM((1, total), jnp.float32),
            pltpu.VMEM(zeros_table.shape, jnp.int32),
            pltpu.VMEM(images.shape, jnp.bfloat16),
            pltpu.SemaphoreType.DMA((5,)),
        ],
    )(
        *(
            pltpu.with_memory_space_constraint(array, pltpu.HBM)
            for array in (
                order.reshape(1, total),
                radial_counts.reshape(1, total),
                noise_var.reshape(1, total),
                zeros_table,
                images,
            )
        )
    )
    recv = lax.all_to_all(coef, both, split_axis=0, concat_axis=0, tiled=True)
    back, shrink = call(
        functools.partial(filter_kernel, plan),
        (block, shape((quota * radial + pairs * plan.narrow, radial), jnp.bfloat16)),
        [VMEM, VMEM],
        [
            pltpu.VMEM((plan.devices * plan.low_rows, radial), jnp.float32),
            pltpu.VMEM((quota, radial, radial), jnp.float32),
            pltpu.VMEM((pairs, plan.narrow, radial), jnp.float32),
            pltpu.VMEM((quota, plan.devices * plan.vecs, radial), jnp.bfloat16),
            pltpu.VMEM((pairs, plan.devices * plan.vecs, radial), jnp.bfloat16),
            pltpu.VMEM((quota, radial, radial), jnp.float32),
            pltpu.VMEM((pairs, plan.narrow, radial), jnp.float32),
        ],
    )(info, recv)
    returned = lax.all_to_all(back, both, split_axis=0, concat_axis=0, tiled=True)
    other = lax.ppermute(shrink, "batch", [(0, 1), (1, 0)])
    wiener_blocks = call(
        functools.partial(wiener_kernel, plan),
        shape((plan.owned, radial, radial), jnp.float32),
        [VMEM] * 3,
    )(shrink, other, info)
    denoised = call(
        functools.partial(synthesis_kernel, plan),
        shape((plan.count_img, radial, plan.angles), jnp.bfloat16),
        [VMEM] * 6,
        [
            pltpu.VMEM((plan.all_pairs // 4, 8 * plan.vecs, radial), jnp.float32),
            pltpu.VMEM((2 * total, plan.count_img * radial), jnp.bfloat16),
        ],
    )(table, cb, sb, wave, zero, returned)
    return denoised, wiener_blocks


def solution(mesh):
    owners, batches = mesh.shape["freq"], mesh.shape["batch"]

    def body(images, radial_counts, order, zeros_table, noise_var):
        plan = Plan(images.shape, order.shape[0], owners, batches)
        device = functools.partial(fast_device, plan) if plan.fits else per_device
        return device(images, radial_counts, order, zeros_table, noise_var)

    return jax.shard_map(
        body,
        mesh=mesh,
        in_specs=(P(("batch", "freq"), None, None), P(), P(), P(), P()),
        out_specs=(P(("batch", "freq"), None, None), P("freq", None, None)),
        check_vma=False,
    )
```

```python
import functools
import math

import jax
import jax.numpy as jnp
from jax import lax
from jax.experimental import pallas as pl
from jax.experimental.pallas import tpu as pltpu
from jax.sharding import PartitionSpec as P


def make_table(freqs, angles):
    angle_index = jnp.arange(angles, dtype=jnp.int32)
    product = angle_index[:, None] * freqs[None, :] % angles
    phase = 2.0 * math.pi / angles * product.astype(jnp.float32)
    factor = math.sqrt(2.0 / angles)
    return jnp.concatenate([factor * jnp.cos(phase), factor * jnp.sin(phase)], axis=1).astype(
        jnp.bfloat16
    )


def make_basis(freqs, zero_rows, counts, radial):
    slots = zero_rows.shape[1]
    freq_float = freqs.astype(jnp.float32)[:, None, None]
    scaled = math.pi * (zero_rows.astype(jnp.float32)[:, :, None] + 0.5 * freq_float - 0.25)
    grid = (jnp.arange(radial, dtype=jnp.float32) + 0.5) / radial
    phase = scaled * grid[None, None, :] - 0.5 * math.pi * freq_float - 0.25 * math.pi
    keep = jnp.arange(slots, dtype=jnp.int32)[None, :, None] < counts[:, None, None]
    values = math.sqrt(2.0 / radial) * jnp.cos(phase)
    return jnp.where(keep, values, jnp.zeros_like(values)).astype(jnp.bfloat16)


def gram_of(blocks):
    return jnp.einsum("kvq,kvp->kqp", blocks, blocks, preferred_element_type=jnp.float32)


def shrink_from(gram, noise, vectors):
    width = gram.shape[1]
    eye = jnp.eye(width, dtype=jnp.float32)
    covariance = gram / vectors + noise[:, None, None] * eye
    lower = jnp.linalg.cholesky(covariance)
    inv_lower = jax.scipy.linalg.solve_triangular(
        lower, jnp.broadcast_to(eye, covariance.shape), lower=True
    )
    inverse = jnp.einsum("kmq,kmp->kqp", inv_lower, inv_lower, precision=lax.Precision.HIGHEST)
    return eye - noise[:, None, None] * inverse


def apply_shrink(shrinkage, blocks):
    return jnp.einsum(
        "kqp,kvp->kvq", shrinkage.astype(jnp.bfloat16), blocks, preferred_element_type=jnp.float32
    ).astype(jnp.bfloat16)


def per_device(images, radial_counts, order, zeros_table, noise_var):
    count_img, radial, angles = images.shape
    total_freq = order.shape[0]
    block = min(64, total_freq)
    nblocks = total_freq // block
    flat = images.reshape(count_img * radial, angles)
    slot_rows = jnp.take(zeros_table, order, axis=0)
    slot_counts = jnp.take(radial_counts, order)

    def block_tools(index):
        start = index * block
        freqs = lax.dynamic_slice_in_dim(order, start, block)
        table = make_table(freqs, angles)
        rows_here = lax.dynamic_slice_in_dim(slot_rows, start, block, 0)
        counts_here = lax.dynamic_slice_in_dim(slot_counts, start, block)
        return (table, make_basis(freqs, rows_here, counts_here, radial))

    def analyse(index):
        table, basis = block_tools(index)
        spectrum = jnp.dot(flat, table, preferred_element_type=jnp.float32)
        spectrum = spectrum.astype(jnp.bfloat16).reshape(count_img, radial, 2, block)
        return jnp.einsum(
            "ircj,jqr->jciq", spectrum, basis, preferred_element_type=jnp.float32
        ).astype(jnp.bfloat16)

    pieces = lax.map(analyse, jnp.arange(nblocks, dtype=jnp.int32))
    moved = pieces.reshape(total_freq, 2 * count_img, radial)
    owners = lax.axis_size("freq")
    owned = total_freq // owners
    batches = lax.axis_size("batch")
    mine = lax.dynamic_slice_in_dim(order, lax.axis_index("freq") * owned, owned)
    noise_mine = jnp.take(noise_var, mine)
    half_slots = owned // 2
    narrow = radial // 2
    grouped = moved.reshape(owners, owned, 2 * count_img, radial)
    lower_part = grouped[:, :half_slots].reshape(owners * half_slots, 2 * count_img, radial)
    upper_part = grouped[:, half_slots:, :, :narrow].reshape(
        owners * half_slots, 2 * count_img, narrow
    )
    low_recv, high_recv = (
        lax.all_to_all(lower_part, "freq", split_axis=0, concat_axis=1, tiled=True),
        lax.all_to_all(upper_part, "freq", split_axis=0, concat_axis=1, tiled=True),
    )
    gram_low, gram_high = lax.psum((gram_of(low_recv), gram_of(high_recv)), "batch")
    vectors = low_recv.shape[1] * batches
    shrink_lower = shrink_from(gram_low, noise_mine[:half_slots], vectors)
    shrink_upper = shrink_from(gram_high, noise_mine[half_slots:], vectors)
    low_back, high_back = (
        lax.all_to_all(
            apply_shrink(shrink_lower, low_recv), "freq", split_axis=1, concat_axis=0, tiled=True
        ),
        lax.all_to_all(
            apply_shrink(shrink_upper, high_recv), "freq", split_axis=1, concat_axis=0, tiled=True
        ),
    )
    high_wide = jnp.pad(high_back, ((0, 0), (0, 0), (0, radial - narrow)))
    returned = jnp.concatenate(
        [
            low_back.reshape(owners, half_slots, 2 * count_img, radial),
            high_wide.reshape(owners, half_slots, 2 * count_img, radial),
        ],
        axis=1,
    )
    returned = returned.reshape(total_freq, 2 * count_img, radial)
    upper_wide = jnp.pad(shrink_upper, ((0, 0), (0, radial - narrow), (0, radial - narrow)))
    wiener_blocks = jnp.concatenate([shrink_lower, upper_wide], axis=0)
    filtered_blocks = returned.reshape(nblocks, block, 2, count_img, radial)

    def synthesise(index, total):
        table, basis = block_tools(index)
        piece = lax.dynamic_index_in_dim(filtered_blocks, index, 0, keepdims=False)
        spectrum_out = jnp.einsum(
            "jciq,jqr->ircj", piece, basis, preferred_element_type=jnp.float32
        )
        spectrum_out = spectrum_out.astype(jnp.bfloat16).reshape(count_img * radial, 2 * block)
        return total + lax.dot_general(
            spectrum_out, table, (((1,), (1,)), ((), ())), preferred_element_type=jnp.float32
        )

    summed = lax.fori_loop(
        0, nblocks, synthesise, jnp.zeros((count_img * radial, angles), jnp.float32)
    )
    denoised = summed.astype(jnp.bfloat16).reshape(count_img, radial, angles)
    return (denoised, wiener_blocks)


COSINE = (
    -0.9999999889445799,
    4.934801116644238,
    -4.058694745523659,
    1.3351580223122241,
    -0.23502902263765682,
    0.025358285764913842,
    -0.0015936782168350142,
)


def cosine_of(turns, steps):
    x = ((turns & (steps - 1)) - steps // 2).astype(jnp.float32) * (2.0 / steps)
    y = x * x
    total = jnp.full_like(y, COSINE[-1])
    for term in COSINE[-2::-1]:
        total = total * y + term
    return total


def iota(shape, dim):
    return lax.broadcasted_iota(jnp.int32, shape, dim)


def nt(a, b):
    return lax.dot_general(a, b, (((1,), (1,)), ((), ())), preferred_element_type=jnp.float32)


def tn(a, b):
    return lax.dot_general(a, b, (((0,), (0,)), ((), ())), preferred_element_type=jnp.float32)


def nn(a, b):
    return jnp.dot(a, b, preferred_element_type=jnp.float32)


def low_bits(mask):
    return mask.astype(jnp.float32).astype(jnp.bfloat16)


class Plan:
    def __init__(self, images, order, owners, batches):
        self.count_img, self.radial, self.angles = images
        self.total = order
        self.owners, self.batches = owners, batches
        self.devices = owners * batches
        self.owned = order // owners
        self.half = self.owned // 2
        self.vecs = 2 * self.count_img
        self.quota = 4
        self.pairs = self.quota // 2
        self.narrow = self.radial // 2
        self.low_rows = self.vecs * self.quota
        self.rows = self.low_rows + self.vecs * self.pairs
        self.all_pairs = self.devices * self.pairs
        power = lambda n: n > 0 and n & (n - 1) == 0
        self.fits = (
            batches == 2
            and self.half == batches * self.quota
            and self.radial == 128
            and self.count_img == 4
            and all(power(n) for n in (self.angles, self.total, owners))
            and self.angles == 2 * self.total == 4 * self.radial
        )

    def slot_of(self, device, place):
        batch, owner = device // self.owners, device & (self.owners - 1)
        return owner * self.owned + batch * self.quota + place


def row_pairs(x, y):
    blocks, width = x.shape[0] // 8, x.shape[1]
    x, y = x.reshape(blocks, 8, width), y.reshape(blocks, 8, width)
    front = iota(x.shape, 1) < 4
    first = jnp.where(front, x, pltpu.roll(y, 4, axis=1))
    second = jnp.where(front, pltpu.roll(x, 4, axis=1), y)
    return jnp.concatenate([first, second], axis=1).reshape(16 * blocks, width)


def analysis_kernel(
    plan, order_hbm, counts_hbm, noise_hbm, zeros_hbm, images_hbm,
    coef_ref, table_ref, cb_ref, sb_ref, wave_ref, zero_ref, info_ref,
    wide_ref, order_ref, counts_ref, noise_ref, zeros_ref, images_ref, sems,
):
    radial, angles, total = plan.radial, plan.angles, plan.total
    quota, pairs, narrow = plan.quota, plan.pairs, plan.narrow
    copies = [
        pltpu.make_async_copy(source, target, sems.at[at])
        for at, (source, target) in enumerate(
            (
                (order_hbm, order_ref),
                (counts_hbm, counts_ref),
                (noise_hbm, noise_ref),
                (zeros_hbm, zeros_ref),
                (images_hbm, images_ref),
            )
        )
    ]
    for copy in copies:
        copy.start()
    turns = (iota((radial, radial), 1) + 1) * (2 * iota((radial, radial), 0) + 1)
    factor = math.sqrt(2.0 / radial)
    wave_ref[0:radial, :] = (factor * cosine_of(turns, 4 * radial)).astype(jnp.bfloat16)
    wave_ref[radial : 2 * radial, :] = (-factor * cosine_of(turns - radial, 4 * radial)).astype(
        jnp.bfloat16
    )
    sub, lane = iota((8, total), 0), iota((8, total), 1)
    place = sub & (quota - 1)
    jump = (sub // quota) * plan.owned + place
    slots = [jump + plan.slot_of(2 * two, 0) for two in range(plan.devices // 2)]
    jump = (sub // pairs) * plan.owned + 2 * (sub & (pairs - 1))
    slots += [
        jump + (plan.slot_of(4 * eight, 0) + plan.half + e)
        for e in range(2)
        for eight in range(plan.all_pairs // 8)
    ]
    device = lax.axis_index("batch") * plan.owners + lax.axis_index("freq")
    partner = (1 - lax.axis_index("batch")) * plan.owners + lax.axis_index("freq")
    slots += [plan.slot_of(d, (sub // quota) * plan.half + place) for d in (device, partner)]
    pick = jnp.concatenate([(slot == lane).astype(jnp.float32) for slot in slots], axis=0)
    pick = pick.astype(jnp.bfloat16)
    copies[0].wait()
    spread = lambda ref: jnp.broadcast_to(ref[...].astype(jnp.float32), (128, total)).astype(jnp.bfloat16)
    every_freq = nt(pick, spread(order_ref)).astype(jnp.int32)
    freq = every_freq[:total]
    lane = iota((total, 128), 1)
    factor = math.sqrt(2.0 / angles)
    turns = lane * freq
    cosine = cosine_of(turns, angles) * factor
    sine = cosine_of(turns - angles // 4, angles) * factor
    odd, flip = freq & 1, (1 - (freq & 2)).astype(jnp.float32)
    even_part, odd_part = (1 - odd).astype(jnp.float32) * flip, odd.astype(jnp.float32) * flip
    mirror = (1 - 2 * odd).astype(jnp.float32)
    turned_cosine = even_part * cosine - odd_part * sine
    turned_sine = even_part * sine + odd_part * cosine
    parts = [
        (cosine, sine),
        (turned_cosine, turned_sine),
        (mirror * cosine, mirror * sine),
        (mirror * turned_cosine, mirror * turned_sine),
    ]
    for part, (x, y) in enumerate(parts):
        table_ref[:, part * 128 : part * 128 + 128] = row_pairs(x, y).astype(jnp.bfloat16)
    steps = 16 * radial
    turns = (2 * freq - 1) * (2 * lane + 1) - 4 * radial * freq - 2 * radial
    cosine, sine = cosine_of(turns, steps), cosine_of(turns - steps // 4, steps)
    cb_ref[...] = row_pairs(cosine, cosine)
    sb_ref[...] = row_pairs(sine, sine)
    for copy in copies[1:4]:
        copy.wait()
    named = every_freq[total - 2 * plan.all_pairs :]
    named = jnp.concatenate([named] * (total // 128), axis=1) == iota((named.shape[0], total), 1)
    pick = low_bits(named)
    zeros = nn(pick, zeros_ref[...].astype(jnp.float32).astype(jnp.bfloat16))
    counts = nt(pick, spread(counts_ref)).astype(jnp.int32)
    zeros = jnp.where(iota(zeros.shape, 1) < counts, zeros, 0.0)
    first, second = zeros[: plan.all_pairs], zeros[plan.all_pairs : 2 * plan.all_pairs]
    lane = iota((plan.all_pairs, radial), 1)
    zero_ref[...] = jnp.where(lane < narrow, first, pltpu.roll(second, narrow, axis=1)).astype(
        jnp.int32
    )
    square = (radial, radial)
    ones = jnp.ones((8, radial), jnp.bfloat16)
    for s in range(quota):
        at = 2 * plan.all_pairs + s
        chosen = low_bits(iota(square, 0) + 1 == zeros[at : at + 1].astype(jnp.int32))
        info_ref[s : s + 1, :] = nt(ones, chosen)[0:1]
    mine = named[2 * plan.all_pairs : 2 * plan.all_pairs + 8]
    noise = jnp.sum(jnp.where(mine, noise_ref[...], 0.0), axis=1, keepdims=True)
    info_ref[8:16, :] = jnp.broadcast_to(noise, (8, 128))
    info_ref[16:32, :] = zeros[2 * plan.all_pairs :]
    copies[4].wait()
    images = images_ref[...].reshape(plan.count_img * radial, angles)
    for two in range(plan.count_img // 2):
        spectrum = nt(table_ref[...], images[2 * two * radial : 2 * (two + 1) * radial])
        lows = []
        for i in range(2):
            part = spectrum[:, i * radial : (i + 1) * radial]
            turned = jnp.concatenate(
                [(part * cb_ref[...]).astype(jnp.bfloat16), (part * sb_ref[...]).astype(jnp.bfloat16)],
                axis=1,
            )
            coef = nn(turned, wave_ref[...])
            lows.append(coef[:total].reshape(plan.devices, 2 * quota, radial))
            span = 2 * plan.all_pairs
            for e in range(2):
                at = 8 * (e * plan.count_img + 2 * two + i)
                part = coef[total + e * span : total + (e + 1) * span]
                wide_ref[:, at : at + 8, :] = part.reshape(span // 8, 8, radial)
        size = 4 * quota
        coef_ref[:, size * two : size * (two + 1), :] = jnp.concatenate(lows, axis=1).astype(
            jnp.bfloat16
        )
    lane = iota((plan.vecs, radial), 1)
    zero_here = iota((radial, radial), 0) + 1
    for device in range(plan.devices):
        rows, chosen = [], []
        for i in range(pairs):
            at = device * pairs + i
            rows.append(wide_ref[at // 4, pl.ds(at % 4, 2 * plan.vecs, stride=4), :])
            chosen.append(low_bits(zero_here == zero_ref[at : at + 1, :]))
        rows = jnp.concatenate(rows, axis=0).astype(jnp.bfloat16)
        packed = nn(rows, jnp.concatenate(chosen, axis=1))
        tiles = []
        for i in range(pairs):
            start = 2 * i * plan.vecs
            both = packed[start : start + 2 * plan.vecs, i * radial : (i + 1) * radial]
            tiles.append(jnp.where(lane < narrow, both[: plan.vecs], both[plan.vecs :]))
        coef_ref[device, plan.low_rows : plan.rows, :] = jnp.concatenate(tiles, axis=0).astype(
            jnp.bfloat16
        )


def thirds(x):
    first = x.astype(jnp.bfloat16)
    rest = x - first.astype(jnp.float32)
    second = rest.astype(jnp.bfloat16)
    third = (rest - second.astype(jnp.float32)).astype(jnp.bfloat16)
    return first, second, third


def outer(u, v):
    u1, u2, u3 = thirds(u)
    v1, v2, v3 = thirds(v)
    return lax.dot_general(
        jnp.concatenate([u1, u1, u1, u2, u2, u3], axis=0),
        jnp.concatenate([v1, v2, v3, v1, v2, v1], axis=0),
        (((0,), (0,)), ((), ())),
        preferred_element_type=jnp.float32,
    )


def columns(panel, halved, first):
    lane = iota(panel.shape, 1)
    base = (lane & 64 if halved else jnp.zeros_like(lane)) + first
    return [jnp.take_along_axis(panel, base + j, axis=1) for j in range(8)]


def offset_of(shape, halved, first):
    lane = iota(shape, 1)
    return (lane & 63 if halved else lane) - first


def spread_row(panel, j):
    return jnp.broadcast_to(panel[j : j + 1], panel.shape)


def eliminate(panels, kinds):
    sub = iota((8, 128), 0)
    blocks, lines = [], []
    for panel, (halved, first) in zip(panels, kinds):
        offset = offset_of(panel.shape, halved, first)
        unit = (sub == offset).astype(jnp.float32)
        blocks.append(columns(panel, halved, first))
        lines.append(jnp.where((offset < 0) | (offset >= 8), panel, unit))
    for i in range(8):
        unit = (sub == i).astype(jnp.float32)
        for at, cols in enumerate(blocks):
            weight = (cols[i] - unit) * (1.0 / spread_row(cols[i], i))
            for j in range(i + 1, 8):
                cols[j] = cols[j] - weight * spread_row(cols[j], i)
            lines[at] = lines[at] - weight * spread_row(lines[at], i)
    return lines


def take_away(panel, factors, solved, halved, first):
    offset = offset_of(panel.shape, halved, first)
    total = jnp.where((offset >= 0) & (offset < 8), 0.0, panel)
    other = factors[1] * spread_row(solved, 1)
    for j in range(0, 8, 2):
        total = total - factors[j] * spread_row(solved, j)
        if j:
            other = other + factors[j + 1] * spread_row(solved, j + 1)
    return total - other


def scales_of(matrix, halved):
    row, lane = iota(matrix.shape, 0), iota(matrix.shape, 1)
    diagonal = jnp.where(row == (lane & 63 if halved else lane), matrix, 0.0)
    across = lax.rsqrt(jnp.sum(diagonal, axis=0, keepdims=True))
    if not halved:
        return across * lax.rsqrt(jnp.sum(diagonal, axis=1, keepdims=True))
    left = lax.rsqrt(jnp.sum(jnp.where(lane < 64, diagonal, 0.0), axis=1, keepdims=True))
    right = lax.rsqrt(jnp.sum(jnp.where(lane < 64, 0.0, diagonal), axis=1, keepdims=True))
    return across * jnp.where(lane < 64, left, right)


def sweep(matrices):
    upper, lower, starts = [], [], []
    for ref, m, _, first in matrices:
        start = pl.multiple_of(first, 16)
        starts.append(start)
        upper.append(ref[m, pl.ds(start, 8), :])
        lower.append(ref[m, pl.ds(start + 8, 8), :])
    kinds = [(halved, first) for _, _, halved, first in matrices]
    factors = [columns(p, h, f) for p, (h, f) in zip(lower, kinds)]
    tops = eliminate(upper, kinds)
    rests = [take_away(p, c, t, h, f) for p, c, t, (h, f) in zip(lower, factors, tops, kinds)]
    factors = [columns(t, h, f + 8) for t, (h, f) in zip(tops, kinds)]
    bottoms = eliminate(rests, [(h, f + 8) for h, f in kinds])
    tops = [take_away(t, c, b, h, f + 8) for t, c, b, (h, f) in zip(tops, factors, bottoms, kinds)]
    shape = (16, 128)
    for at, (ref, m, halved, first) in enumerate(matrices):
        height = ref.shape[1]
        panel = jnp.concatenate([upper[at], lower[at]], axis=0)
        fresh = jnp.concatenate([tops[at], bottoms[at]], axis=0)
        offset = offset_of(shape, halved, first)
        unit = (iota(shape, 0) == offset).astype(jnp.float32)
        update = outer(jnp.where(offset < 0, -panel, panel), fresh + unit)
        if halved:
            update = jnp.where(iota((height, 128), 1) < 64, update[:height], update[height:])
        ref[m] = ref[m] - update
        ref[m, pl.ds(starts[at], 16), :] = fresh


def filter_kernel(
    plan, info_ref, recv_ref,
    back_ref, shrink_ref, wide_ref, full_ref, pair_ref, kept_ref, held_ref, full_scale_ref, pair_scale_ref,
):
    radial, quota, pairs, narrow = plan.radial, plan.quota, plan.pairs, plan.narrow
    low_rows = plan.low_rows
    rows = plan.devices * plan.vecs
    low_part = recv_ref[:, :low_rows, :].astype(jnp.float32)
    wide_ref[...] = low_part.reshape(plan.devices * low_rows, radial)
    square = (radial, radial)
    strip = (narrow, radial)
    eye = (iota(square, 0) == iota(square, 1)).astype(jnp.float32)
    twins = (iota(strip, 0) == (iota(strip, 1) & (narrow - 1))).astype(jnp.float32)
    first = iota(strip, 1) < narrow
    noises = []
    for s in range(quota):
        noises.append(info_ref[8 + s : 9 + s, :])
        coef = wide_ref[pl.ds(s, rows, stride=quota), :] * info_ref[s : s + 1, :]
        coef = coef.astype(jnp.bfloat16)
        kept_ref[s] = coef
        covariance = tn(coef, coef) / float(rows) + noises[s] * eye
        scale = scales_of(covariance, False)
        full_scale_ref[s] = scale
        full_ref[s] = covariance * scale
    high_part = recv_ref[:, low_rows:, :].astype(jnp.float32)
    for i in range(pairs):
        coef = high_part[:, i * plan.vecs : (i + 1) * plan.vecs, :].reshape(rows, radial)
        coef = coef.astype(jnp.bfloat16)
        held_ref[i] = coef
        gram = tn(coef, coef)
        gram = jnp.where(first, gram[:narrow], gram[narrow:])
        at = 8 + quota + 2 * i
        noise = jnp.where(first, info_ref[at : at + 1, :], info_ref[at + 1 : at + 2, :])
        noises.append(noise)
        covariance = gram / float(rows) + noise * twins
        scale = scales_of(covariance, True)
        pair_scale_ref[i] = scale
        pair_ref[i] = covariance * scale
    steps, half_steps = radial // 16, narrow // 16

    def body(step, carry):
        matrices = [(full_ref, m, False, 16 * step) for m in range(quota)]
        part = 16 * (step % half_steps)
        sweep(matrices + [(pair_ref, step // half_steps, True, part)])
        return carry

    lax.fori_loop(0, steps, body, 0)
    for s in range(quota):
        shrink = eye - noises[s] * (full_ref[s] * full_scale_ref[s])
        shrink_ref[s * radial : (s + 1) * radial, :] = shrink.astype(jnp.bfloat16)
        wide_ref[pl.ds(s, rows, stride=quota), :] = nt(kept_ref[s], shrink.astype(jnp.bfloat16))
    shape = (plan.devices, low_rows, radial)
    back_ref[:, :low_rows, :] = wide_ref[...].reshape(shape).astype(jnp.bfloat16)
    tiles = []
    for i in range(pairs):
        shrink = twins - noises[quota + i] * (pair_ref[i] * pair_scale_ref[i])
        start = quota * radial + i * narrow
        shrink_ref[start : start + narrow, :] = shrink.astype(jnp.bfloat16)
        blocks = jnp.concatenate(
            [jnp.where(first, shrink, 0.0), jnp.where(first, 0.0, shrink)], axis=0
        )
        filtered = nt(held_ref[i], blocks.astype(jnp.bfloat16))
        tiles.append(filtered.reshape(plan.devices, plan.vecs, radial))
    back_ref[:, low_rows:, :] = jnp.concatenate(tiles, axis=1).astype(jnp.bfloat16)


def synthesis_kernel(plan, table_ref, cb_ref, sb_ref, wave_ref, zero_ref, recv_ref, out_ref, wide_ref, held_ref):
    radial, total, quota, pairs = plan.radial, plan.total, plan.quota, plan.pairs
    lane = iota((plan.vecs, radial), 1)
    zero_here = iota((radial, radial), 0) + 1
    for device in range(plan.devices):
        tile = recv_ref[device, plan.low_rows : plan.rows, :].astype(jnp.float32)
        rows, chosen = [], []
        for i in range(pairs):
            at = device * pairs + i
            packed = tile[i * plan.vecs : (i + 1) * plan.vecs]
            rows += [jnp.where(lane < plan.narrow, packed, 0.0), jnp.where(lane < plan.narrow, 0.0, packed)]
            chosen.append(low_bits(zero_here == zero_ref[at : at + 1, :]))
        rows = jnp.concatenate(rows, axis=0).astype(jnp.bfloat16)
        spread = nt(rows, jnp.concatenate(chosen, axis=0))
        for i in range(pairs):
            at = device * pairs + i
            start = 2 * i * plan.vecs
            wide_ref[at // 4, pl.ds(at % 4, 2 * plan.vecs, stride=4), :] = spread[
                start : start + 2 * plan.vecs, i * radial : (i + 1) * radial
            ]
    span = 2 * plan.all_pairs
    for i in range(plan.count_img):
        low = recv_ref[:, 2 * quota * i : 2 * quota * (i + 1), :].astype(jnp.float32)
        at = [8 * (e * plan.count_img + i) for e in range(2)]
        high = [wide_ref[:, a : a + 8, :].reshape(span, radial) for a in at]
        filtered = jnp.concatenate([low.reshape(total, radial)] + high, axis=0)
        turned = nt(filtered.astype(jnp.bfloat16), wave_ref[...])
        spectrum = turned[:, :radial] * cb_ref[...] + turned[:, radial:] * sb_ref[...]
        held_ref[:, i * radial : (i + 1) * radial] = spectrum.astype(jnp.bfloat16)
    image = tn(held_ref[...], table_ref[...]).astype(jnp.bfloat16)
    out_ref[...] = image.reshape(out_ref.shape)


def wiener_kernel(plan, own_ref, other_ref, info_ref, out_ref):
    radial, quota, narrow = plan.radial, plan.quota, plan.narrow
    batch_at = lax.axis_index("batch")
    lane = iota((narrow, radial), 1)
    zero_here = iota((radial, radial), 0) + 1
    for batch, ref, start in ((batch_at, own_ref, 16), (1 - batch_at, other_ref, 24)):
        for s in range(quota):
            zero = info_ref[start + s : start + s + 1, :].astype(jnp.int32)
            chosen = low_bits(zero_here == zero)
            half_way = nn(ref[s * radial : (s + 1) * radial, :], chosen).astype(jnp.bfloat16)
            out_ref[batch * quota + s] = tn(chosen, half_way)
            at = plan.half + batch * quota + s
            first = quota * radial + (s // 2) * narrow
            pair = ref[first : first + narrow, :].astype(jnp.float32)
            if s % 2:
                pair = pltpu.roll(pair, narrow, axis=1)
            out_ref[at, 0:narrow, :] = jnp.where(lane < narrow, pair, 0.0)
            out_ref[at, narrow:radial, :] = jnp.zeros((radial - narrow, radial), jnp.float32)


VMEM = pl.BlockSpec(memory_space=pltpu.VMEM)
HBM = pl.BlockSpec(memory_space=pltpu.HBM)


def call(kernel, outs, ins, scratch=()):
    return pl.pallas_call(
        kernel,
        out_shape=outs,
        in_specs=ins,
        out_specs=jax.tree.map(lambda _: VMEM, outs),
        scratch_shapes=scratch,
        compiler_params=pltpu.CompilerParams(vmem_limit_bytes=16 << 20),
    )


def fast_device(plan, images, radial_counts, order, zeros_table, noise_var):
    both = ("batch", "freq")
    radial, total, quota, pairs = plan.radial, plan.total, plan.quota, plan.pairs
    shape = jax.ShapeDtypeStruct
    block = shape((plan.devices, plan.rows, radial), jnp.bfloat16)
    coef, table, cb, sb, wave, zero, info = call(
        functools.partial(analysis_kernel, plan),
        (
            block,
            shape((2 * total, plan.angles), jnp.bfloat16),
            shape((2 * total, radial), jnp.float32),
            shape((2 * total, radial), jnp.float32),
            shape((2 * radial, radial), jnp.bfloat16),
            shape((plan.all_pairs, radial), jnp.int32),
            shape((32, radial), jnp.float32),
        ),
        [HBM] * 5,
        [
            pltpu.VMEM((plan.all_pairs // 4, 8 * plan.vecs, radial), jnp.float32),
            pltpu.VMEM((1, total), jnp.int32),
            pltpu.VMEM((1, total), jnp.int32),
            pltpu.VMEM((1, total), jnp.float32),
            pltpu.VMEM(zeros_table.shape, jnp.int32),
            pltpu.VMEM(images.shape, jnp.bfloat16),
            pltpu.SemaphoreType.DMA((5,)),
        ],
    )(
        *(
            pltpu.with_memory_space_constraint(array, pltpu.HBM)
            for array in (
                order.reshape(1, total),
                radial_counts.reshape(1, total),
                noise_var.reshape(1, total),
                zeros_table,
                images,
            )
        )
    )
    recv = lax.all_to_all(coef, both, split_axis=0, concat_axis=0, tiled=True)
    back, shrink = call(
        functools.partial(filter_kernel, plan),
        (block, shape((quota * radial + pairs * plan.narrow, radial), jnp.bfloat16)),
        [VMEM, VMEM],
        [
            pltpu.VMEM((plan.devices * plan.low_rows, radial), jnp.float32),
            pltpu.VMEM((quota, radial, radial), jnp.float32),
            pltpu.VMEM((pairs, plan.narrow, radial), jnp.float32),
            pltpu.VMEM((quota, plan.devices * plan.vecs, radial), jnp.bfloat16),
            pltpu.VMEM((pairs, plan.devices * plan.vecs, radial), jnp.bfloat16),
            pltpu.VMEM((quota, radial, radial), jnp.float32),
            pltpu.VMEM((pairs, plan.narrow, radial), jnp.float32),
        ],
    )(info, recv)
    returned = lax.all_to_all(back, both, split_axis=0, concat_axis=0, tiled=True)
    other = lax.ppermute(shrink, "batch", [(0, 1), (1, 0)])
    wiener_blocks = call(
        functools.partial(wiener_kernel, plan),
        shape((plan.owned, radial, radial), jnp.float32),
        [VMEM] * 3,
    )(shrink, other, info)
    denoised = call(
        functools.partial(synthesis_kernel, plan),
        shape((plan.count_img, radial, plan.angles), jnp.bfloat16),
        [VMEM] * 6,
        [
            pltpu.VMEM((plan.all_pairs // 4, 8 * plan.vecs, radial), jnp.float32),
            pltpu.VMEM((2 * total, plan.count_img * radial), jnp.bfloat16),
        ],
    )(table, cb, sb, wave, zero, returned)
    return denoised, wiener_blocks


def solution(mesh):
    owners, batches = mesh.shape["freq"], mesh.shape["batch"]

    def body(images, radial_counts, order, zeros_table, noise_var):
        plan = Plan(images.shape, order.shape[0], owners, batches)
        device = functools.partial(fast_device, plan) if plan.fits else per_device
        return device(images, radial_counts, order, zeros_table, noise_var)

    return jax.shard_map(
        body,
        mesh=mesh,
        in_specs=(P(("batch", "freq"), None, None), P(), P(), P(), P()),
        out_specs=(P(("batch", "freq"), None, None), P("freq", None, None)),
        check_vma=False,
    )
```

```python
import functools
import math

import jax
import jax.numpy as jnp
from jax import lax
from jax.experimental import pallas as pl
from jax.experimental.pallas import tpu as pltpu
from jax.sharding import PartitionSpec as P


def make_table(freqs, angles):
    angle_index = jnp.arange(angles, dtype=jnp.int32)
    product = angle_index[:, None] * freqs[None, :] % angles
    phase = 2.0 * math.pi / angles * product.astype(jnp.float32)
    factor = math.sqrt(2.0 / angles)
    return jnp.concatenate([factor * jnp.cos(phase), factor * jnp.sin(phase)], axis=1).astype(
        jnp.bfloat16
    )


def make_basis(freqs, zero_rows, counts, radial):
    slots = zero_rows.shape[1]
    freq_float = freqs.astype(jnp.float32)[:, None, None]
    scaled = math.pi * (zero_rows.astype(jnp.float32)[:, :, None] + 0.5 * freq_float - 0.25)
    grid = (jnp.arange(radial, dtype=jnp.float32) + 0.5) / radial
    phase = scaled * grid[None, None, :] - 0.5 * math.pi * freq_float - 0.25 * math.pi
    keep = jnp.arange(slots, dtype=jnp.int32)[None, :, None] < counts[:, None, None]
    values = math.sqrt(2.0 / radial) * jnp.cos(phase)
    return jnp.where(keep, values, jnp.zeros_like(values)).astype(jnp.bfloat16)


def gram_of(blocks):
    return jnp.einsum("kvq,kvp->kqp", blocks, blocks, preferred_element_type=jnp.float32)


def shrink_from(gram, noise, vectors):
    width = gram.shape[1]
    eye = jnp.eye(width, dtype=jnp.float32)
    covariance = gram / vectors + noise[:, None, None] * eye
    lower = jnp.linalg.cholesky(covariance)
    inv_lower = jax.scipy.linalg.solve_triangular(
        lower, jnp.broadcast_to(eye, covariance.shape), lower=True
    )
    inverse = jnp.einsum("kmq,kmp->kqp", inv_lower, inv_lower, precision=lax.Precision.HIGHEST)
    return eye - noise[:, None, None] * inverse


def apply_shrink(shrinkage, blocks):
    return jnp.einsum(
        "kqp,kvp->kvq", shrinkage.astype(jnp.bfloat16), blocks, preferred_element_type=jnp.float32
    ).astype(jnp.bfloat16)


def per_device(images, radial_counts, order, zeros_table, noise_var):
    count_img, radial, angles = images.shape
    total_freq = order.shape[0]
    block = min(64, total_freq)
    nblocks = total_freq // block
    flat = images.reshape(count_img * radial, angles)
    slot_rows = jnp.take(zeros_table, order, axis=0)
    slot_counts = jnp.take(radial_counts, order)

    def block_tools(index):
        start = index * block
        freqs = lax.dynamic_slice_in_dim(order, start, block)
        table = make_table(freqs, angles)
        rows_here = lax.dynamic_slice_in_dim(slot_rows, start, block, 0)
        counts_here = lax.dynamic_slice_in_dim(slot_counts, start, block)
        return (table, make_basis(freqs, rows_here, counts_here, radial))

    def analyse(index):
        table, basis = block_tools(index)
        spectrum = jnp.dot(flat, table, preferred_element_type=jnp.float32)
        spectrum = spectrum.astype(jnp.bfloat16).reshape(count_img, radial, 2, block)
        return jnp.einsum(
            "ircj,jqr->jciq", spectrum, basis, preferred_element_type=jnp.float32
        ).astype(jnp.bfloat16)

    pieces = lax.map(analyse, jnp.arange(nblocks, dtype=jnp.int32))
    moved = pieces.reshape(total_freq, 2 * count_img, radial)
    owners = lax.axis_size("freq")
    owned = total_freq // owners
    batches = lax.axis_size("batch")
    mine = lax.dynamic_slice_in_dim(order, lax.axis_index("freq") * owned, owned)
    noise_mine = jnp.take(noise_var, mine)
    half_slots = owned // 2
    narrow = radial // 2
    grouped = moved.reshape(owners, owned, 2 * count_img, radial)
    lower_part = grouped[:, :half_slots].reshape(owners * half_slots, 2 * count_img, radial)
    upper_part = grouped[:, half_slots:, :, :narrow].reshape(
        owners * half_slots, 2 * count_img, narrow
    )
    low_recv, high_recv = (
        lax.all_to_all(lower_part, "freq", split_axis=0, concat_axis=1, tiled=True),
        lax.all_to_all(upper_part, "freq", split_axis=0, concat_axis=1, tiled=True),
    )
    gram_low, gram_high = lax.psum((gram_of(low_recv), gram_of(high_recv)), "batch")
    vectors = low_recv.shape[1] * batches
    shrink_lower = shrink_from(gram_low, noise_mine[:half_slots], vectors)
    shrink_upper = shrink_from(gram_high, noise_mine[half_slots:], vectors)
    low_back, high_back = (
        lax.all_to_all(
            apply_shrink(shrink_lower, low_recv), "freq", split_axis=1, concat_axis=0, tiled=True
        ),
        lax.all_to_all(
            apply_shrink(shrink_upper, high_recv), "freq", split_axis=1, concat_axis=0, tiled=True
        ),
    )
    high_wide = jnp.pad(high_back, ((0, 0), (0, 0), (0, radial - narrow)))
    returned = jnp.concatenate(
        [
            low_back.reshape(owners, half_slots, 2 * count_img, radial),
            high_wide.reshape(owners, half_slots, 2 * count_img, radial),
        ],
        axis=1,
    )
    returned = returned.reshape(total_freq, 2 * count_img, radial)
    upper_wide = jnp.pad(shrink_upper, ((0, 0), (0, radial - narrow), (0, radial - narrow)))
    wiener_blocks = jnp.concatenate([shrink_lower, upper_wide], axis=0)
    filtered_blocks = returned.reshape(nblocks, block, 2, count_img, radial)

    def synthesise(index, total):
        table, basis = block_tools(index)
        piece = lax.dynamic_index_in_dim(filtered_blocks, index, 0, keepdims=False)
        spectrum_out = jnp.einsum(
            "jciq,jqr->ircj", piece, basis, preferred_element_type=jnp.float32
        )
        spectrum_out = spectrum_out.astype(jnp.bfloat16).reshape(count_img * radial, 2 * block)
        return total + lax.dot_general(
            spectrum_out, table, (((1,), (1,)), ((), ())), preferred_element_type=jnp.float32
        )

    summed = lax.fori_loop(
        0, nblocks, synthesise, jnp.zeros((count_img * radial, angles), jnp.float32)
    )
    denoised = summed.astype(jnp.bfloat16).reshape(count_img, radial, angles)
    return (denoised, wiener_blocks)


COSINE = (
    -0.9999999889445799,
    4.934801116644238,
    -4.058694745523659,
    1.3351580223122241,
    -0.23502902263765682,
    0.025358285764913842,
    -0.0015936782168350142,
)


def cosine_of(turns, steps):
    x = ((turns & (steps - 1)) - steps // 2).astype(jnp.float32) * (2.0 / steps)
    y = x * x
    total = jnp.full_like(y, COSINE[-1])
    for term in COSINE[-2::-1]:
        total = total * y + term
    return total


def iota(shape, dim):
    return lax.broadcasted_iota(jnp.int32, shape, dim)


def nt(a, b):
    return lax.dot_general(a, b, (((1,), (1,)), ((), ())), preferred_element_type=jnp.float32)


def tn(a, b):
    return lax.dot_general(a, b, (((0,), (0,)), ((), ())), preferred_element_type=jnp.float32)


def nn(a, b):
    return jnp.dot(a, b, preferred_element_type=jnp.float32)


def low_bits(mask):
    return mask.astype(jnp.float32).astype(jnp.bfloat16)


class Plan:
    def __init__(self, images, order, owners, batches):
        self.count_img, self.radial, self.angles = images
        self.total = order
        self.owners, self.batches = owners, batches
        self.devices = owners * batches
        self.owned = order // owners
        self.half = self.owned // 2
        self.vecs = 2 * self.count_img
        self.quota = 4
        self.pairs = self.quota // 2
        self.narrow = self.radial // 2
        self.low_rows = self.vecs * self.quota
        self.rows = self.low_rows + self.vecs * self.pairs
        self.all_pairs = self.devices * self.pairs
        power = lambda n: n > 0 and n & (n - 1) == 0
        self.fits = (
            batches == 2
            and self.half == batches * self.quota
            and self.radial == 128
            and self.count_img == 4
            and all(power(n) for n in (self.angles, self.total, owners))
            and self.angles == 2 * self.total == 4 * self.radial
        )

    def slot_of(self, device, place):
        batch, owner = device // self.owners, device & (self.owners - 1)
        return owner * self.owned + batch * self.quota + place


def row_pairs(x, y):
    blocks, width = x.shape[0] // 8, x.shape[1]
    x, y = x.reshape(blocks, 8, width), y.reshape(blocks, 8, width)
    front = iota(x.shape, 1) < 4
    first = jnp.where(front, x, pltpu.roll(y, 4, axis=1))
    second = jnp.where(front, pltpu.roll(x, 4, axis=1), y)
    return jnp.concatenate([first, second], axis=1).reshape(16 * blocks, width)


def analysis_kernel(
    plan, order_hbm, counts_hbm, noise_hbm, zeros_hbm, images_hbm,
    coef_ref, table_ref, cb_ref, sb_ref, wave_ref, zero_ref, info_ref,
    wide_ref, order_ref, counts_ref, noise_ref, zeros_ref, images_ref, sems,
):
    radial, angles, total = plan.radial, plan.angles, plan.total
    quota, pairs, narrow = plan.quota, plan.pairs, plan.narrow
    copies = [
        pltpu.make_async_copy(source, target, sems.at[at])
        for at, (source, target) in enumerate(
            (
                (order_hbm, order_ref),
                (counts_hbm, counts_ref),
                (noise_hbm, noise_ref),
                (zeros_hbm, zeros_ref),
                (images_hbm, images_ref),
            )
        )
    ]
    for copy in copies:
        copy.start()
    turns = (iota((radial, radial), 1) + 1) * (2 * iota((radial, radial), 0) + 1)
    factor = math.sqrt(2.0 / radial)
    wave_ref[0:radial, :] = (factor * cosine_of(turns, 4 * radial)).astype(jnp.bfloat16)
    wave_ref[radial : 2 * radial, :] = (-factor * cosine_of(turns - radial, 4 * radial)).astype(
        jnp.bfloat16
    )
    sub, lane = iota((8, total), 0), iota((8, total), 1)
    place = sub & (quota - 1)
    jump = (sub // quota) * plan.owned + place
    slots = [jump + plan.slot_of(2 * two, 0) for two in range(plan.devices // 2)]
    jump = (sub // pairs) * plan.owned + 2 * (sub & (pairs - 1))
    slots += [
        jump + (plan.slot_of(4 * eight, 0) + plan.half + e)
        for e in range(2)
        for eight in range(plan.all_pairs // 8)
    ]
    device = lax.axis_index("batch") * plan.owners + lax.axis_index("freq")
    partner = (1 - lax.axis_index("batch")) * plan.owners + lax.axis_index("freq")
    slots += [plan.slot_of(d, (sub // quota) * plan.half + place) for d in (device, partner)]
    pick = jnp.concatenate([(slot == lane).astype(jnp.float32) for slot in slots], axis=0)
    pick = pick.astype(jnp.bfloat16)
    copies[0].wait()
    spread = lambda ref: jnp.broadcast_to(ref[...].astype(jnp.float32), (128, total)).astype(jnp.bfloat16)
    every_freq = nt(pick, spread(order_ref)).astype(jnp.int32)
    freq = every_freq[:total]
    lane = iota((total, 128), 1)
    factor = math.sqrt(2.0 / angles)
    turns = lane * freq
    cosine = cosine_of(turns, angles) * factor
    sine = cosine_of(turns - angles // 4, angles) * factor
    odd, flip = freq & 1, (1 - (freq & 2)).astype(jnp.float32)
    even_part, odd_part = (1 - odd).astype(jnp.float32) * flip, odd.astype(jnp.float32) * flip
    mirror = (1 - 2 * odd).astype(jnp.float32)
    turned_cosine = even_part * cosine - odd_part * sine
    turned_sine = even_part * sine + odd_part * cosine
    parts = [
        (cosine, sine),
        (turned_cosine, turned_sine),
        (mirror * cosine, mirror * sine),
        (mirror * turned_cosine, mirror * turned_sine),
    ]
    for part, (x, y) in enumerate(parts):
        table_ref[:, part * 128 : part * 128 + 128] = row_pairs(x, y).astype(jnp.bfloat16)
    steps = 16 * radial
    turns = (2 * freq - 1) * (2 * lane + 1) - 4 * radial * freq - 2 * radial
    cosine, sine = cosine_of(turns, steps), cosine_of(turns - steps // 4, steps)
    cb_ref[...] = row_pairs(cosine, cosine)
    sb_ref[...] = row_pairs(sine, sine)
    for copy in copies[1:]:
        copy.wait()
    named = every_freq[total - 2 * plan.all_pairs :]
    named = jnp.concatenate([named] * (total // 128), axis=1) == iota((named.shape[0], total), 1)
    pick = low_bits(named)
    zeros = nn(pick, zeros_ref[...].astype(jnp.float32).astype(jnp.bfloat16))
    counts = nt(pick, spread(counts_ref)).astype(jnp.int32)
    zeros = jnp.where(iota(zeros.shape, 1) < counts, zeros, 0.0)
    first, second = zeros[: plan.all_pairs], zeros[plan.all_pairs : 2 * plan.all_pairs]
    lane = iota((plan.all_pairs, radial), 1)
    zero_ref[...] = jnp.where(lane < narrow, first, pltpu.roll(second, narrow, axis=1)).astype(
        jnp.int32
    )
    square = (radial, radial)
    ones = jnp.ones((8, radial), jnp.bfloat16)
    for s in range(quota):
        at = 2 * plan.all_pairs + s
        chosen = low_bits(iota(square, 0) + 1 == zeros[at : at + 1].astype(jnp.int32))
        info_ref[s : s + 1, :] = nt(ones, chosen)[0:1]
    mine = named[2 * plan.all_pairs : 2 * plan.all_pairs + 8]
    noise = jnp.sum(jnp.where(mine, noise_ref[...], 0.0), axis=1, keepdims=True)
    info_ref[8:16, :] = jnp.broadcast_to(noise, (8, 128))
    info_ref[16:32, :] = zeros[2 * plan.all_pairs :]
    images = images_ref[...].reshape(plan.count_img * radial, angles)
    for two in range(plan.count_img // 2):
        spectrum = nt(table_ref[...], images[2 * two * radial : 2 * (two + 1) * radial])
        lows = []
        for i in range(2):
            part = spectrum[:, i * radial : (i + 1) * radial]
            turned = jnp.concatenate(
                [(part * cb_ref[...]).astype(jnp.bfloat16), (part * sb_ref[...]).astype(jnp.bfloat16)],
                axis=1,
            )
            coef = nn(turned, wave_ref[...])
            lows.append(coef[:total].reshape(plan.devices, 2 * quota, radial))
            span = 2 * plan.all_pairs
            for e in range(2):
                at = 8 * (e * plan.count_img + 2 * two + i)
                part = coef[total + e * span : total + (e + 1) * span]
                wide_ref[:, at : at + 8, :] = part.reshape(span // 8, 8, radial)
        size = 4 * quota
        coef_ref[:, size * two : size * (two + 1), :] = jnp.concatenate(lows, axis=1).astype(
            jnp.bfloat16
        )
    lane = iota((plan.vecs, radial), 1)
    zero_here = iota((radial, radial), 0) + 1
    for device in range(plan.devices):
        rows, chosen = [], []
        for i in range(pairs):
            at = device * pairs + i
            rows.append(wide_ref[at // 4, pl.ds(at % 4, 2 * plan.vecs, stride=4), :])
            chosen.append(low_bits(zero_here == zero_ref[at : at + 1, :]))
        rows = jnp.concatenate(rows, axis=0).astype(jnp.bfloat16)
        packed = nn(rows, jnp.concatenate(chosen, axis=1))
        tiles = []
        for i in range(pairs):
            start = 2 * i * plan.vecs
            both = packed[start : start + 2 * plan.vecs, i * radial : (i + 1) * radial]
            tiles.append(jnp.where(lane < narrow, both[: plan.vecs], both[plan.vecs :]))
        coef_ref[device, plan.low_rows : plan.rows, :] = jnp.concatenate(tiles, axis=0).astype(
            jnp.bfloat16
        )


def thirds(x):
    first = x.astype(jnp.bfloat16)
    rest = x - first.astype(jnp.float32)
    second = rest.astype(jnp.bfloat16)
    third = (rest - second.astype(jnp.float32)).astype(jnp.bfloat16)
    return first, second, third


def outer(u, v):
    u1, u2, u3 = thirds(u)
    v1, v2, v3 = thirds(v)
    return lax.dot_general(
        jnp.concatenate([u1, u1, u1, u2, u2, u3], axis=0),
        jnp.concatenate([v1, v2, v3, v1, v2, v1], axis=0),
        (((0,), (0,)), ((), ())),
        preferred_element_type=jnp.float32,
    )


def columns(panel, halved, first):
    lane = iota(panel.shape, 1)
    base = (lane & 64 if halved else jnp.zeros_like(lane)) + first
    return [jnp.take_along_axis(panel, base + j, axis=1) for j in range(8)]


def offset_of(shape, halved, first):
    lane = iota(shape, 1)
    return (lane & 63 if halved else lane) - first


def spread_row(panel, j):
    return jnp.broadcast_to(panel[j : j + 1], panel.shape)


def eliminate(panels, kinds):
    sub = iota((8, 128), 0)
    blocks, lines = [], []
    for panel, (halved, first) in zip(panels, kinds):
        offset = offset_of(panel.shape, halved, first)
        unit = (sub == offset).astype(jnp.float32)
        blocks.append(columns(panel, halved, first))
        lines.append(jnp.where((offset < 0) | (offset >= 8), panel, unit))
    for i in range(8):
        unit = (sub == i).astype(jnp.float32)
        for at, cols in enumerate(blocks):
            weight = (cols[i] - unit) * (1.0 / spread_row(cols[i], i))
            for j in range(i + 1, 8):
                cols[j] = cols[j] - weight * spread_row(cols[j], i)
            lines[at] = lines[at] - weight * spread_row(lines[at], i)
    return lines


def take_away(panel, factors, solved, halved, first):
    offset = offset_of(panel.shape, halved, first)
    total = jnp.where((offset >= 0) & (offset < 8), 0.0, panel)
    other = factors[1] * spread_row(solved, 1)
    for j in range(0, 8, 2):
        total = total - factors[j] * spread_row(solved, j)
        if j:
            other = other + factors[j + 1] * spread_row(solved, j + 1)
    return total - other


def scales_of(matrix, halved):
    row, lane = iota(matrix.shape, 0), iota(matrix.shape, 1)
    diagonal = jnp.where(row == (lane & 63 if halved else lane), matrix, 0.0)
    across = lax.rsqrt(jnp.sum(diagonal, axis=0, keepdims=True))
    if not halved:
        return across * lax.rsqrt(jnp.sum(diagonal, axis=1, keepdims=True))
    left = lax.rsqrt(jnp.sum(jnp.where(lane < 64, diagonal, 0.0), axis=1, keepdims=True))
    right = lax.rsqrt(jnp.sum(jnp.where(lane < 64, 0.0, diagonal), axis=1, keepdims=True))
    return across * jnp.where(lane < 64, left, right)


def sweep(matrices):
    upper, lower, starts = [], [], []
    for ref, m, _, first in matrices:
        start = pl.multiple_of(first, 16)
        starts.append(start)
        upper.append(ref[m, pl.ds(start, 8), :])
        lower.append(ref[m, pl.ds(start + 8, 8), :])
    kinds = [(halved, first) for _, _, halved, first in matrices]
    factors = [columns(p, h, f) for p, (h, f) in zip(lower, kinds)]
    tops = eliminate(upper, kinds)
    rests = [take_away(p, c, t, h, f) for p, c, t, (h, f) in zip(lower, factors, tops, kinds)]
    factors = [columns(t, h, f + 8) for t, (h, f) in zip(tops, kinds)]
    bottoms = eliminate(rests, [(h, f + 8) for h, f in kinds])
    tops = [take_away(t, c, b, h, f + 8) for t, c, b, (h, f) in zip(tops, factors, bottoms, kinds)]
    shape = (16, 128)
    for at, (ref, m, halved, first) in enumerate(matrices):
        height = ref.shape[1]
        panel = jnp.concatenate([upper[at], lower[at]], axis=0)
        fresh = jnp.concatenate([tops[at], bottoms[at]], axis=0)
        offset = offset_of(shape, halved, first)
        unit = (iota(shape, 0) == offset).astype(jnp.float32)
        update = outer(jnp.where(offset < 0, -panel, panel), fresh + unit)
        if halved:
            update = jnp.where(iota((height, 128), 1) < 64, update[:height], update[height:])
        ref[m] = ref[m] - update
        ref[m, pl.ds(starts[at], 16), :] = fresh


def filter_kernel(
    plan, info_ref, recv_ref,
    back_ref, shrink_ref, wide_ref, full_ref, pair_ref, kept_ref, held_ref, full_scale_ref, pair_scale_ref,
):
    radial, quota, pairs, narrow = plan.radial, plan.quota, plan.pairs, plan.narrow
    low_rows = plan.low_rows
    rows = plan.devices * plan.vecs
    low_part = recv_ref[:, :low_rows, :].astype(jnp.float32)
    wide_ref[...] = low_part.reshape(plan.devices * low_rows, radial)
    square = (radial, radial)
    strip = (narrow, radial)
    eye = (iota(square, 0) == iota(square, 1)).astype(jnp.float32)
    twins = (iota(strip, 0) == (iota(strip, 1) & (narrow - 1))).astype(jnp.float32)
    first = iota(strip, 1) < narrow
    noises = []
    for s in range(quota):
        noises.append(info_ref[8 + s : 9 + s, :])
        coef = wide_ref[pl.ds(s, rows, stride=quota), :] * info_ref[s : s + 1, :]
        coef = coef.astype(jnp.bfloat16)
        kept_ref[s] = coef
        covariance = tn(coef, coef) / float(rows) + noises[s] * eye
        scale = scales_of(covariance, False)
        full_scale_ref[s] = scale
        full_ref[s] = covariance * scale
    high_part = recv_ref[:, low_rows:, :].astype(jnp.float32)
    for i in range(pairs):
        coef = high_part[:, i * plan.vecs : (i + 1) * plan.vecs, :].reshape(rows, radial)
        coef = coef.astype(jnp.bfloat16)
        held_ref[i] = coef
        gram = tn(coef, coef)
        gram = jnp.where(first, gram[:narrow], gram[narrow:])
        at = 8 + quota + 2 * i
        noise = jnp.where(first, info_ref[at : at + 1, :], info_ref[at + 1 : at + 2, :])
        noises.append(noise)
        covariance = gram / float(rows) + noise * twins
        scale = scales_of(covariance, True)
        pair_scale_ref[i] = scale
        pair_ref[i] = covariance * scale
    steps, half_steps = radial // 16, narrow // 16

    def body(step, carry):
        matrices = [(full_ref, m, False, 16 * step) for m in range(quota)]
        part = 16 * (step % half_steps)
        sweep(matrices + [(pair_ref, step // half_steps, True, part)])
        return carry

    lax.fori_loop(0, steps, body, 0)
    for s in range(quota):
        shrink = eye - noises[s] * (full_ref[s] * full_scale_ref[s])
        shrink_ref[s * radial : (s + 1) * radial, :] = shrink.astype(jnp.bfloat16)
        wide_ref[pl.ds(s, rows, stride=quota), :] = nt(kept_ref[s], shrink.astype(jnp.bfloat16))
    shape = (plan.devices, low_rows, radial)
    back_ref[:, :low_rows, :] = wide_ref[...].reshape(shape).astype(jnp.bfloat16)
    tiles = []
    for i in range(pairs):
        shrink = twins - noises[quota + i] * (pair_ref[i] * pair_scale_ref[i])
        start = quota * radial + i * narrow
        shrink_ref[start : start + narrow, :] = shrink.astype(jnp.bfloat16)
        blocks = jnp.concatenate(
            [jnp.where(first, shrink, 0.0), jnp.where(first, 0.0, shrink)], axis=0
        )
        filtered = nt(held_ref[i], blocks.astype(jnp.bfloat16))
        tiles.append(filtered.reshape(plan.devices, plan.vecs, radial))
    back_ref[:, low_rows:, :] = jnp.concatenate(tiles, axis=1).astype(jnp.bfloat16)


def synthesis_kernel(plan, table_ref, cb_ref, sb_ref, wave_ref, zero_ref, recv_ref, out_ref, wide_ref, held_ref):
    radial, total, quota, pairs = plan.radial, plan.total, plan.quota, plan.pairs
    lane = iota((plan.vecs, radial), 1)
    zero_here = iota((radial, radial), 0) + 1
    for device in range(plan.devices):
        tile = recv_ref[device, plan.low_rows : plan.rows, :].astype(jnp.float32)
        rows, chosen = [], []
        for i in range(pairs):
            at = device * pairs + i
            packed = tile[i * plan.vecs : (i + 1) * plan.vecs]
            rows += [jnp.where(lane < plan.narrow, packed, 0.0), jnp.where(lane < plan.narrow, 0.0, packed)]
            chosen.append(low_bits(zero_here == zero_ref[at : at + 1, :]))
        rows = jnp.concatenate(rows, axis=0).astype(jnp.bfloat16)
        spread = nt(rows, jnp.concatenate(chosen, axis=0))
        for i in range(pairs):
            at = device * pairs + i
            start = 2 * i * plan.vecs
            wide_ref[at // 4, pl.ds(at % 4, 2 * plan.vecs, stride=4), :] = spread[
                start : start + 2 * plan.vecs, i * radial : (i + 1) * radial
            ]
    span = 2 * plan.all_pairs
    for i in range(plan.count_img):
        low = recv_ref[:, 2 * quota * i : 2 * quota * (i + 1), :].astype(jnp.float32)
        at = [8 * (e * plan.count_img + i) for e in range(2)]
        high = [wide_ref[:, a : a + 8, :].reshape(span, radial) for a in at]
        filtered = jnp.concatenate([low.reshape(total, radial)] + high, axis=0)
        turned = nt(filtered.astype(jnp.bfloat16), wave_ref[...])
        spectrum = turned[:, :radial] * cb_ref[...] + turned[:, radial:] * sb_ref[...]
        held_ref[:, i * radial : (i + 1) * radial] = spectrum.astype(jnp.bfloat16)
    image = tn(held_ref[...], table_ref[...]).astype(jnp.bfloat16)
    out_ref[...] = image.reshape(out_ref.shape)


def wiener_kernel(plan, own_ref, other_ref, info_ref, out_ref):
    radial, quota, narrow = plan.radial, plan.quota, plan.narrow
    batch_at = lax.axis_index("batch")
    lane = iota((narrow, radial), 1)
    zero_here = iota((radial, radial), 0) + 1
    for batch, ref, start in ((batch_at, own_ref, 16), (1 - batch_at, other_ref, 24)):
        for s in range(quota):
            zero = info_ref[start + s : start + s + 1, :].astype(jnp.int32)
            chosen = low_bits(zero_here == zero)
            half_way = nn(ref[s * radial : (s + 1) * radial, :], chosen).astype(jnp.bfloat16)
            out_ref[batch * quota + s] = tn(chosen, half_way)
            at = plan.half + batch * quota + s
            first = quota * radial + (s // 2) * narrow
            pair = ref[first : first + narrow, :].astype(jnp.float32)
            if s % 2:
                pair = pltpu.roll(pair, narrow, axis=1)
            out_ref[at, 0:narrow, :] = jnp.where(lane < narrow, pair, 0.0)
            out_ref[at, narrow:radial, :] = jnp.zeros((radial - narrow, radial), jnp.float32)


VMEM = pl.BlockSpec(memory_space=pltpu.VMEM)
HBM = pl.BlockSpec(memory_space=pltpu.HBM)


def call(kernel, outs, ins, scratch=()):
    return pl.pallas_call(
        kernel,
        out_shape=outs,
        in_specs=ins,
        out_specs=jax.tree.map(lambda _: VMEM, outs),
        scratch_shapes=scratch,
        compiler_params=pltpu.CompilerParams(vmem_limit_bytes=16 << 20),
    )


def fast_device(plan, images, radial_counts, order, zeros_table, noise_var):
    both = ("batch", "freq")
    radial, total, quota, pairs = plan.radial, plan.total, plan.quota, plan.pairs
    shape = jax.ShapeDtypeStruct
    block = shape((plan.devices, plan.rows, radial), jnp.bfloat16)
    coef, table, cb, sb, wave, zero, info = call(
        functools.partial(analysis_kernel, plan),
        (
            block,
            shape((2 * total, plan.angles), jnp.bfloat16),
            shape((2 * total, radial), jnp.float32),
            shape((2 * total, radial), jnp.float32),
            shape((2 * radial, radial), jnp.bfloat16),
            shape((plan.all_pairs, radial), jnp.int32),
            shape((32, radial), jnp.float32),
        ),
        [HBM] * 5,
        [
            pltpu.VMEM((plan.all_pairs // 4, 8 * plan.vecs, radial), jnp.float32),
            pltpu.VMEM((1, total), jnp.int32),
            pltpu.VMEM((1, total), jnp.int32),
            pltpu.VMEM((1, total), jnp.float32),
            pltpu.VMEM(zeros_table.shape, jnp.int32),
            pltpu.VMEM(images.shape, jnp.bfloat16),
            pltpu.SemaphoreType.DMA((5,)),
        ],
    )(
        *(
            pltpu.with_memory_space_constraint(array, pltpu.HBM)
            for array in (
                order.reshape(1, total),
                radial_counts.reshape(1, total),
                noise_var.reshape(1, total),
                zeros_table,
                images,
            )
        )
    )
    recv = lax.all_to_all(coef, both, split_axis=0, concat_axis=0, tiled=True)
    back, shrink = call(
        functools.partial(filter_kernel, plan),
        (block, shape((quota * radial + pairs * plan.narrow, radial), jnp.bfloat16)),
        [VMEM, VMEM],
        [
            pltpu.VMEM((plan.devices * plan.low_rows, radial), jnp.float32),
            pltpu.VMEM((quota, radial, radial), jnp.float32),
            pltpu.VMEM((pairs, plan.narrow, radial), jnp.float32),
            pltpu.VMEM((quota, plan.devices * plan.vecs, radial), jnp.bfloat16),
            pltpu.VMEM((pairs, plan.devices * plan.vecs, radial), jnp.bfloat16),
            pltpu.VMEM((quota, radial, radial), jnp.float32),
            pltpu.VMEM((pairs, plan.narrow, radial), jnp.float32),
        ],
    )(info, recv)
    returned = lax.all_to_all(back, both, split_axis=0, concat_axis=0, tiled=True)
    other = lax.ppermute(shrink, "batch", [(0, 1), (1, 0)])
    wiener_blocks = call(
        functools.partial(wiener_kernel, plan),
        shape((plan.owned, radial, radial), jnp.float32),
        [VMEM] * 3,
    )(shrink, other, info)
    denoised = call(
        functools.partial(synthesis_kernel, plan),
        shape((plan.count_img, radial, plan.angles), jnp.bfloat16),
        [VMEM] * 6,
        [
            pltpu.VMEM((plan.all_pairs // 4, 8 * plan.vecs, radial), jnp.float32),
            pltpu.VMEM((2 * total, plan.count_img * radial), jnp.bfloat16),
        ],
    )(table, cb, sb, wave, zero, returned)
    return denoised, wiener_blocks


def solution(mesh):
    owners, batches = mesh.shape["freq"], mesh.shape["batch"]

    def body(images, radial_counts, order, zeros_table, noise_var):
        plan = Plan(images.shape, order.shape[0], owners, batches)
        device = functools.partial(fast_device, plan) if plan.fits else per_device
        return device(images, radial_counts, order, zeros_table, noise_var)

    return jax.shard_map(
        body,
        mesh=mesh,
        in_specs=(P(("batch", "freq"), None, None), P(), P(), P(), P()),
        out_specs=(P(("batch", "freq"), None, None), P("freq", None, None)),
        check_vma=False,
    )
```

```python
import functools
import math

import jax
import jax.numpy as jnp
from jax import lax
from jax.experimental import pallas as pl
from jax.experimental.pallas import tpu as pltpu
from jax.sharding import PartitionSpec as P


def make_table(freqs, angles):
    angle_index = jnp.arange(angles, dtype=jnp.int32)
    product = angle_index[:, None] * freqs[None, :] % angles
    phase = 2.0 * math.pi / angles * product.astype(jnp.float32)
    factor = math.sqrt(2.0 / angles)
    return jnp.concatenate([factor * jnp.cos(phase), factor * jnp.sin(phase)], axis=1).astype(
        jnp.bfloat16
    )


def make_basis(freqs, zero_rows, counts, radial):
    slots = zero_rows.shape[1]
    freq_float = freqs.astype(jnp.float32)[:, None, None]
    scaled = math.pi * (zero_rows.astype(jnp.float32)[:, :, None] + 0.5 * freq_float - 0.25)
    grid = (jnp.arange(radial, dtype=jnp.float32) + 0.5) / radial
    phase = scaled * grid[None, None, :] - 0.5 * math.pi * freq_float - 0.25 * math.pi
    keep = jnp.arange(slots, dtype=jnp.int32)[None, :, None] < counts[:, None, None]
    values = math.sqrt(2.0 / radial) * jnp.cos(phase)
    return jnp.where(keep, values, jnp.zeros_like(values)).astype(jnp.bfloat16)


def gram_of(blocks):
    return jnp.einsum("kvq,kvp->kqp", blocks, blocks, preferred_element_type=jnp.float32)


def shrink_from(gram, noise, vectors):
    width = gram.shape[1]
    eye = jnp.eye(width, dtype=jnp.float32)
    covariance = gram / vectors + noise[:, None, None] * eye
    lower = jnp.linalg.cholesky(covariance)
    inv_lower = jax.scipy.linalg.solve_triangular(
        lower, jnp.broadcast_to(eye, covariance.shape), lower=True
    )
    inverse = jnp.einsum("kmq,kmp->kqp", inv_lower, inv_lower, precision=lax.Precision.HIGHEST)
    return eye - noise[:, None, None] * inverse


def apply_shrink(shrinkage, blocks):
    return jnp.einsum(
        "kqp,kvp->kvq", shrinkage.astype(jnp.bfloat16), blocks, preferred_element_type=jnp.float32
    ).astype(jnp.bfloat16)


def per_device(images, radial_counts, order, zeros_table, noise_var):
    count_img, radial, angles = images.shape
    total_freq = order.shape[0]
    block = min(64, total_freq)
    nblocks = total_freq // block
    flat = images.reshape(count_img * radial, angles)
    slot_rows = jnp.take(zeros_table, order, axis=0)
    slot_counts = jnp.take(radial_counts, order)

    def block_tools(index):
        start = index * block
        freqs = lax.dynamic_slice_in_dim(order, start, block)
        table = make_table(freqs, angles)
        rows_here = lax.dynamic_slice_in_dim(slot_rows, start, block, 0)
        counts_here = lax.dynamic_slice_in_dim(slot_counts, start, block)
        return (table, make_basis(freqs, rows_here, counts_here, radial))

    def analyse(index):
        table, basis = block_tools(index)
        spectrum = jnp.dot(flat, table, preferred_element_type=jnp.float32)
        spectrum = spectrum.astype(jnp.bfloat16).reshape(count_img, radial, 2, block)
        return jnp.einsum(
            "ircj,jqr->jciq", spectrum, basis, preferred_element_type=jnp.float32
        ).astype(jnp.bfloat16)

    pieces = lax.map(analyse, jnp.arange(nblocks, dtype=jnp.int32))
    moved = pieces.reshape(total_freq, 2 * count_img, radial)
    owners = lax.axis_size("freq")
    owned = total_freq // owners
    batches = lax.axis_size("batch")
    mine = lax.dynamic_slice_in_dim(order, lax.axis_index("freq") * owned, owned)
    noise_mine = jnp.take(noise_var, mine)
    half_slots = owned // 2
    narrow = radial // 2
    grouped = moved.reshape(owners, owned, 2 * count_img, radial)
    lower_part = grouped[:, :half_slots].reshape(owners * half_slots, 2 * count_img, radial)
    upper_part = grouped[:, half_slots:, :, :narrow].reshape(
        owners * half_slots, 2 * count_img, narrow
    )
    low_recv, high_recv = (
        lax.all_to_all(lower_part, "freq", split_axis=0, concat_axis=1, tiled=True),
        lax.all_to_all(upper_part, "freq", split_axis=0, concat_axis=1, tiled=True),
    )
    gram_low, gram_high = lax.psum((gram_of(low_recv), gram_of(high_recv)), "batch")
    vectors = low_recv.shape[1] * batches
    shrink_lower = shrink_from(gram_low, noise_mine[:half_slots], vectors)
    shrink_upper = shrink_from(gram_high, noise_mine[half_slots:], vectors)
    low_back, high_back = (
        lax.all_to_all(
            apply_shrink(shrink_lower, low_recv), "freq", split_axis=1, concat_axis=0, tiled=True
        ),
        lax.all_to_all(
            apply_shrink(shrink_upper, high_recv), "freq", split_axis=1, concat_axis=0, tiled=True
        ),
    )
    high_wide = jnp.pad(high_back, ((0, 0), (0, 0), (0, radial - narrow)))
    returned = jnp.concatenate(
        [
            low_back.reshape(owners, half_slots, 2 * count_img, radial),
            high_wide.reshape(owners, half_slots, 2 * count_img, radial),
        ],
        axis=1,
    )
    returned = returned.reshape(total_freq, 2 * count_img, radial)
    upper_wide = jnp.pad(shrink_upper, ((0, 0), (0, radial - narrow), (0, radial - narrow)))
    wiener_blocks = jnp.concatenate([shrink_lower, upper_wide], axis=0)
    filtered_blocks = returned.reshape(nblocks, block, 2, count_img, radial)

    def synthesise(index, total):
        table, basis = block_tools(index)
        piece = lax.dynamic_index_in_dim(filtered_blocks, index, 0, keepdims=False)
        spectrum_out = jnp.einsum(
            "jciq,jqr->ircj", piece, basis, preferred_element_type=jnp.float32
        )
        spectrum_out = spectrum_out.astype(jnp.bfloat16).reshape(count_img * radial, 2 * block)
        return total + lax.dot_general(
            spectrum_out, table, (((1,), (1,)), ((), ())), preferred_element_type=jnp.float32
        )

    summed = lax.fori_loop(
        0, nblocks, synthesise, jnp.zeros((count_img * radial, angles), jnp.float32)
    )
    denoised = summed.astype(jnp.bfloat16).reshape(count_img, radial, angles)
    return (denoised, wiener_blocks)


COSINE = (
    -0.9999999889445799,
    4.934801116644238,
    -4.058694745523659,
    1.3351580223122241,
    -0.23502902263765682,
    0.025358285764913842,
    -0.0015936782168350142,
)


def cosine_of(turns, steps):
    x = ((turns & (steps - 1)) - steps // 2).astype(jnp.float32) * (2.0 / steps)
    y = x * x
    total = jnp.full_like(y, COSINE[-1])
    for term in COSINE[-2::-1]:
        total = total * y + term
    return total


def iota(shape, dim):
    return lax.broadcasted_iota(jnp.int32, shape, dim)


def nt(a, b):
    return lax.dot_general(a, b, (((1,), (1,)), ((), ())), preferred_element_type=jnp.float32)


def tn(a, b):
    return lax.dot_general(a, b, (((0,), (0,)), ((), ())), preferred_element_type=jnp.float32)


def nn(a, b):
    return jnp.dot(a, b, preferred_element_type=jnp.float32)


def low_bits(mask):
    return mask.astype(jnp.float32).astype(jnp.bfloat16)


class Plan:
    def __init__(self, images, order, owners, batches):
        self.count_img, self.radial, self.angles = images
        self.total = order
        self.owners, self.batches = owners, batches
        self.devices = owners * batches
        self.owned = order // owners
        self.half = self.owned // 2
        self.vecs = 2 * self.count_img
        self.quota = 4
        self.pairs = self.quota // 2
        self.narrow = self.radial // 2
        self.low_rows = self.vecs * self.quota
        self.rows = self.low_rows + self.vecs * self.pairs
        self.all_pairs = self.devices * self.pairs
        power = lambda n: n > 0 and n & (n - 1) == 0
        self.fits = (
            batches == 2
            and self.half == batches * self.quota
            and self.radial == 128
            and self.count_img == 4
            and all(power(n) for n in (self.angles, self.total, owners))
            and self.angles == 2 * self.total == 4 * self.radial
        )

    def slot_of(self, device, place):
        batch, owner = device // self.owners, device & (self.owners - 1)
        return owner * self.owned + batch * self.quota + place


def row_pairs(x, y):
    blocks, width = x.shape[0] // 8, x.shape[1]
    x, y = x.reshape(blocks, 8, width), y.reshape(blocks, 8, width)
    front = iota(x.shape, 1) < 4
    first = jnp.where(front, x, pltpu.roll(y, 4, axis=1))
    second = jnp.where(front, pltpu.roll(x, 4, axis=1), y)
    return jnp.concatenate([first, second], axis=1).reshape(16 * blocks, width)


def analysis_kernel(
    plan, order_hbm, counts_hbm, noise_hbm, zeros_hbm, images_hbm,
    coef_ref, table_ref, cb_ref, sb_ref, wave_ref, zero_ref, info_ref,
    wide_ref, order_ref, counts_ref, noise_ref, zeros_ref, images_ref, sems,
):
    radial, angles, total = plan.radial, plan.angles, plan.total
    quota, pairs, narrow = plan.quota, plan.pairs, plan.narrow
    copies = [
        pltpu.make_async_copy(source, target, sems.at[at])
        for at, (source, target) in enumerate(
            (
                (order_hbm, order_ref),
                (counts_hbm, counts_ref),
                (noise_hbm, noise_ref),
                (zeros_hbm, zeros_ref),
                (images_hbm, images_ref),
            )
        )
    ]
    for copy in copies:
        copy.start()
    turns = (iota((radial, radial), 1) + 1) * (2 * iota((radial, radial), 0) + 1)
    factor = math.sqrt(2.0 / radial)
    wave_ref[0:radial, :] = (factor * cosine_of(turns, 4 * radial)).astype(jnp.bfloat16)
    wave_ref[radial : 2 * radial, :] = (-factor * cosine_of(turns - radial, 4 * radial)).astype(
        jnp.bfloat16
    )
    sub, lane = iota((8, total), 0), iota((8, total), 1)
    place = sub & (quota - 1)
    jump = (sub // quota) * plan.owned + place
    slots = [jump + plan.slot_of(2 * two, 0) for two in range(plan.devices // 2)]
    jump = (sub // pairs) * plan.owned + 2 * (sub & (pairs - 1))
    slots += [
        jump + (plan.slot_of(4 * eight, 0) + plan.half + e)
        for e in range(2)
        for eight in range(plan.all_pairs // 8)
    ]
    device = lax.axis_index("batch") * plan.owners + lax.axis_index("freq")
    partner = (1 - lax.axis_index("batch")) * plan.owners + lax.axis_index("freq")
    slots += [plan.slot_of(d, (sub // quota) * plan.half + place) for d in (device, partner)]
    pick = jnp.concatenate([(slot == lane).astype(jnp.float32) for slot in slots], axis=0)
    pick = pick.astype(jnp.bfloat16)
    copies[0].wait()
    spread = lambda ref: jnp.broadcast_to(ref[...].astype(jnp.float32), (128, total)).astype(jnp.bfloat16)
    every_freq = nt(pick, spread(order_ref)).astype(jnp.int32)
    freq = every_freq[:total]
    lane = iota((total, 128), 1)
    factor = math.sqrt(2.0 / angles)
    turns = lane * freq
    cosine = cosine_of(turns, angles) * factor
    sine = cosine_of(turns - angles // 4, angles) * factor
    odd, flip = freq & 1, (1 - (freq & 2)).astype(jnp.float32)
    even_part, odd_part = (1 - odd).astype(jnp.float32) * flip, odd.astype(jnp.float32) * flip
    mirror = (1 - 2 * odd).astype(jnp.float32)
    turned_cosine = even_part * cosine - odd_part * sine
    turned_sine = even_part * sine + odd_part * cosine
    parts = [
        (cosine, sine),
        (turned_cosine, turned_sine),
        (mirror * cosine, mirror * sine),
        (mirror * turned_cosine, mirror * turned_sine),
    ]
    for part, (x, y) in enumerate(parts):
        table_ref[:, part * 128 : part * 128 + 128] = row_pairs(x, y).astype(jnp.bfloat16)
    steps = 16 * radial
    turns = (2 * freq - 1) * (2 * lane + 1) - 4 * radial * freq - 2 * radial
    cosine, sine = cosine_of(turns, steps), cosine_of(turns - steps // 4, steps)
    cb_ref[...] = row_pairs(cosine, cosine)
    sb_ref[...] = row_pairs(sine, sine)
    for copy in copies[1:]:
        copy.wait()
    named = every_freq[total - 2 * plan.all_pairs :]
    named = jnp.concatenate([named] * (total // 128), axis=1) == iota((named.shape[0], total), 1)
    pick = low_bits(named)
    zeros = nn(pick, zeros_ref[...].astype(jnp.float32).astype(jnp.bfloat16))
    counts = nt(pick, spread(counts_ref)).astype(jnp.int32)
    zeros = jnp.where(iota(zeros.shape, 1) < counts, zeros, 0.0)
    first, second = zeros[: plan.all_pairs], zeros[plan.all_pairs : 2 * plan.all_pairs]
    lane = iota((plan.all_pairs, radial), 1)
    zero_ref[...] = jnp.where(lane < narrow, first, pltpu.roll(second, narrow, axis=1)).astype(
        jnp.int32
    )
    square = (radial, radial)
    ones = jnp.ones((8, radial), jnp.bfloat16)
    for s in range(quota):
        at = 2 * plan.all_pairs + s
        chosen = low_bits(iota(square, 0) + 1 == zeros[at : at + 1].astype(jnp.int32))
        info_ref[s : s + 1, :] = nt(ones, chosen)[0:1]
    mine = named[2 * plan.all_pairs : 2 * plan.all_pairs + 8]
    noise = jnp.sum(jnp.where(mine, noise_ref[...], 0.0), axis=1, keepdims=True)
    info_ref[8:16, :] = jnp.broadcast_to(noise, (8, 128))
    info_ref[16:32, :] = zeros[2 * plan.all_pairs :]
    images = images_ref[...].reshape(plan.count_img * radial, angles)
    for two in range(plan.count_img // 2):
        spectrum = nt(table_ref[...], images[2 * two * radial : 2 * (two + 1) * radial])
        lows = []
        for i in range(2):
            part = spectrum[:, i * radial : (i + 1) * radial]
            turned = jnp.concatenate(
                [(part * cb_ref[...]).astype(jnp.bfloat16), (part * sb_ref[...]).astype(jnp.bfloat16)],
                axis=1,
            )
            coef = nn(turned, wave_ref[...])
            lows.append(coef[:total].reshape(plan.devices, 2 * quota, radial))
            span = 2 * plan.all_pairs
            for e in range(2):
                at = 8 * (e * plan.count_img + 2 * two + i)
                part = coef[total + e * span : total + (e + 1) * span]
                wide_ref[:, at : at + 8, :] = part.reshape(span // 8, 8, radial)
        size = 4 * quota
        coef_ref[:, size * two : size * (two + 1), :] = jnp.concatenate(lows, axis=1).astype(
            jnp.bfloat16
        )
    lane = iota((plan.vecs, radial), 1)
    zero_here = iota((radial, radial), 0) + 1
    for device in range(plan.devices):
        rows, chosen = [], []
        for i in range(pairs):
            at = device * pairs + i
            rows.append(wide_ref[at // 4, pl.ds(at % 4, 2 * plan.vecs, stride=4), :])
            chosen.append(low_bits(zero_here == zero_ref[at : at + 1, :]))
        rows = jnp.concatenate(rows, axis=0).astype(jnp.bfloat16)
        packed = nn(rows, jnp.concatenate(chosen, axis=1))
        tiles = []
        for i in range(pairs):
            start = 2 * i * plan.vecs
            both = packed[start : start + 2 * plan.vecs, i * radial : (i + 1) * radial]
            tiles.append(jnp.where(lane < narrow, both[: plan.vecs], both[plan.vecs :]))
        coef_ref[device, plan.low_rows : plan.rows, :] = jnp.concatenate(tiles, axis=0).astype(
            jnp.bfloat16
        )


def thirds(x):
    first = x.astype(jnp.bfloat16)
    rest = x - first.astype(jnp.float32)
    second = rest.astype(jnp.bfloat16)
    third = (rest - second.astype(jnp.float32)).astype(jnp.bfloat16)
    return first, second, third


def outer(u, v):
    u1, u2, u3 = thirds(u)
    v1, v2, v3 = thirds(v)
    return lax.dot_general(
        jnp.concatenate([u1, u1, u1, u2, u2, u3], axis=0),
        jnp.concatenate([v1, v2, v3, v1, v2, v1], axis=0),
        (((0,), (0,)), ((), ())),
        preferred_element_type=jnp.float32,
    )


def columns(panel, halved, first):
    lane = iota(panel.shape, 1)
    base = (lane & 64 if halved else jnp.zeros_like(lane)) + first
    return [jnp.take_along_axis(panel, base + j, axis=1) for j in range(8)]


def offset_of(shape, halved, first):
    lane = iota(shape, 1)
    return (lane & 63 if halved else lane) - first


def spread_row(panel, j):
    return jnp.broadcast_to(panel[j : j + 1], panel.shape)


def eliminate(panels, kinds):
    sub = iota((8, 128), 0)
    blocks, lines = [], []
    for panel, (halved, first) in zip(panels, kinds):
        offset = offset_of(panel.shape, halved, first)
        unit = (sub == offset).astype(jnp.float32)
        blocks.append(columns(panel, halved, first))
        lines.append(jnp.where((offset < 0) | (offset >= 8), panel, unit))
    for i in range(8):
        unit = (sub == i).astype(jnp.float32)
        for at, cols in enumerate(blocks):
            weight = (cols[i] - unit) * (1.0 / spread_row(cols[i], i))
            for j in range(i + 1, 8):
                cols[j] = cols[j] - weight * spread_row(cols[j], i)
            lines[at] = lines[at] - weight * spread_row(lines[at], i)
    return lines


def take_away(panel, factors, solved, halved, first):
    offset = offset_of(panel.shape, halved, first)
    total = jnp.where((offset >= 0) & (offset < 8), 0.0, panel)
    other = factors[1] * spread_row(solved, 1)
    for j in range(0, 8, 2):
        total = total - factors[j] * spread_row(solved, j)
        if j:
            other = other + factors[j + 1] * spread_row(solved, j + 1)
    return total - other


def scales_of(matrix, halved):
    row, lane = iota(matrix.shape, 0), iota(matrix.shape, 1)
    diagonal = jnp.where(row == (lane & 63 if halved else lane), matrix, 0.0)
    across = lax.rsqrt(jnp.sum(diagonal, axis=0, keepdims=True))
    if not halved:
        return across * lax.rsqrt(jnp.sum(diagonal, axis=1, keepdims=True))
    left = lax.rsqrt(jnp.sum(jnp.where(lane < 64, diagonal, 0.0), axis=1, keepdims=True))
    right = lax.rsqrt(jnp.sum(jnp.where(lane < 64, 0.0, diagonal), axis=1, keepdims=True))
    return across * jnp.where(lane < 64, left, right)


def sweep(matrices):
    upper, lower, starts = [], [], []
    for ref, m, _, first in matrices:
        start = first
        starts.append(start)
        upper.append(ref[m, pl.ds(start, 8), :])
        lower.append(ref[m, pl.ds(start + 8, 8), :])
    kinds = [(halved, first) for _, _, halved, first in matrices]
    factors = [columns(p, h, f) for p, (h, f) in zip(lower, kinds)]
    tops = eliminate(upper, kinds)
    rests = [take_away(p, c, t, h, f) for p, c, t, (h, f) in zip(lower, factors, tops, kinds)]
    factors = [columns(t, h, f + 8) for t, (h, f) in zip(tops, kinds)]
    bottoms = eliminate(rests, [(h, f + 8) for h, f in kinds])
    tops = [take_away(t, c, b, h, f + 8) for t, c, b, (h, f) in zip(tops, factors, bottoms, kinds)]
    shape = (16, 128)
    for at, (ref, m, halved, first) in enumerate(matrices):
        height = ref.shape[1]
        panel = jnp.concatenate([upper[at], lower[at]], axis=0)
        fresh = jnp.concatenate([tops[at], bottoms[at]], axis=0)
        offset = offset_of(shape, halved, first)
        unit = (iota(shape, 0) == offset).astype(jnp.float32)
        update = outer(jnp.where(offset < 0, -panel, panel), fresh + unit)
        if halved:
            update = jnp.where(iota((height, 128), 1) < 64, update[:height], update[height:])
        ref[m] = ref[m] - update
        ref[m, pl.ds(starts[at], 16), :] = fresh


def filter_kernel(
    plan, info_ref, recv_ref,
    back_ref, shrink_ref, wide_ref, full_ref, pair_ref, kept_ref, held_ref, full_scale_ref, pair_scale_ref,
):
    radial, quota, pairs, narrow = plan.radial, plan.quota, plan.pairs, plan.narrow
    low_rows = plan.low_rows
    rows = plan.devices * plan.vecs
    low_part = recv_ref[:, :low_rows, :].astype(jnp.float32)
    wide_ref[...] = low_part.reshape(plan.devices * low_rows, radial)
    square = (radial, radial)
    strip = (narrow, radial)
    eye = (iota(square, 0) == iota(square, 1)).astype(jnp.float32)
    twins = (iota(strip, 0) == (iota(strip, 1) & (narrow - 1))).astype(jnp.float32)
    first = iota(strip, 1) < narrow
    noises = []
    for s in range(quota):
        noises.append(info_ref[8 + s : 9 + s, :])
        coef = wide_ref[pl.ds(s, rows, stride=quota), :] * info_ref[s : s + 1, :]
        coef = coef.astype(jnp.bfloat16)
        kept_ref[s] = coef
        covariance = tn(coef, coef) / float(rows) + noises[s] * eye
        scale = scales_of(covariance, False)
        full_scale_ref[s] = scale
        full_ref[s] = covariance * scale
    high_part = recv_ref[:, low_rows:, :].astype(jnp.float32)
    for i in range(pairs):
        coef = high_part[:, i * plan.vecs : (i + 1) * plan.vecs, :].reshape(rows, radial)
        coef = coef.astype(jnp.bfloat16)
        held_ref[i] = coef
        gram = tn(coef, coef)
        gram = jnp.where(first, gram[:narrow], gram[narrow:])
        at = 8 + quota + 2 * i
        noise = jnp.where(first, info_ref[at : at + 1, :], info_ref[at + 1 : at + 2, :])
        noises.append(noise)
        covariance = gram / float(rows) + noise * twins
        scale = scales_of(covariance, True)
        pair_scale_ref[i] = scale
        pair_ref[i] = covariance * scale
    steps, half_steps = radial // 16, narrow // 16

    for step in range(steps):
        matrices = [(full_ref, m, False, 16 * step) for m in range(quota)]
        part = 16 * (step % half_steps)
        sweep(matrices + [(pair_ref, step // half_steps, True, part)])
    for s in range(quota):
        shrink = eye - noises[s] * (full_ref[s] * full_scale_ref[s])
        shrink_ref[s * radial : (s + 1) * radial, :] = shrink.astype(jnp.bfloat16)
        wide_ref[pl.ds(s, rows, stride=quota), :] = nt(kept_ref[s], shrink.astype(jnp.bfloat16))
    shape = (plan.devices, low_rows, radial)
    back_ref[:, :low_rows, :] = wide_ref[...].reshape(shape).astype(jnp.bfloat16)
    tiles = []
    for i in range(pairs):
        shrink = twins - noises[quota + i] * (pair_ref[i] * pair_scale_ref[i])
        start = quota * radial + i * narrow
        shrink_ref[start : start + narrow, :] = shrink.astype(jnp.bfloat16)
        blocks = jnp.concatenate(
            [jnp.where(first, shrink, 0.0), jnp.where(first, 0.0, shrink)], axis=0
        )
        filtered = nt(held_ref[i], blocks.astype(jnp.bfloat16))
        tiles.append(filtered.reshape(plan.devices, plan.vecs, radial))
    back_ref[:, low_rows:, :] = jnp.concatenate(tiles, axis=1).astype(jnp.bfloat16)


def synthesis_kernel(plan, table_ref, cb_ref, sb_ref, wave_ref, zero_ref, recv_ref, out_ref, wide_ref, held_ref):
    radial, total, quota, pairs = plan.radial, plan.total, plan.quota, plan.pairs
    lane = iota((plan.vecs, radial), 1)
    zero_here = iota((radial, radial), 0) + 1
    for device in range(plan.devices):
        tile = recv_ref[device, plan.low_rows : plan.rows, :].astype(jnp.float32)
        rows, chosen = [], []
        for i in range(pairs):
            at = device * pairs + i
            packed = tile[i * plan.vecs : (i + 1) * plan.vecs]
            rows += [jnp.where(lane < plan.narrow, packed, 0.0), jnp.where(lane < plan.narrow, 0.0, packed)]
            chosen.append(low_bits(zero_here == zero_ref[at : at + 1, :]))
        rows = jnp.concatenate(rows, axis=0).astype(jnp.bfloat16)
        spread = nt(rows, jnp.concatenate(chosen, axis=0))
        for i in range(pairs):
            at = device * pairs + i
            start = 2 * i * plan.vecs
            wide_ref[at // 4, pl.ds(at % 4, 2 * plan.vecs, stride=4), :] = spread[
                start : start + 2 * plan.vecs, i * radial : (i + 1) * radial
            ]
    span = 2 * plan.all_pairs
    for i in range(plan.count_img):
        low = recv_ref[:, 2 * quota * i : 2 * quota * (i + 1), :].astype(jnp.float32)
        at = [8 * (e * plan.count_img + i) for e in range(2)]
        high = [wide_ref[:, a : a + 8, :].reshape(span, radial) for a in at]
        filtered = jnp.concatenate([low.reshape(total, radial)] + high, axis=0)
        turned = nt(filtered.astype(jnp.bfloat16), wave_ref[...])
        spectrum = turned[:, :radial] * cb_ref[...] + turned[:, radial:] * sb_ref[...]
        held_ref[:, i * radial : (i + 1) * radial] = spectrum.astype(jnp.bfloat16)
    image = tn(held_ref[...], table_ref[...]).astype(jnp.bfloat16)
    out_ref[...] = image.reshape(out_ref.shape)


def wiener_kernel(plan, own_ref, other_ref, info_ref, out_ref):
    radial, quota, narrow = plan.radial, plan.quota, plan.narrow
    batch_at = lax.axis_index("batch")
    lane = iota((narrow, radial), 1)
    zero_here = iota((radial, radial), 0) + 1
    for batch, ref, start in ((batch_at, own_ref, 16), (1 - batch_at, other_ref, 24)):
        for s in range(quota):
            zero = info_ref[start + s : start + s + 1, :].astype(jnp.int32)
            chosen = low_bits(zero_here == zero)
            half_way = nn(ref[s * radial : (s + 1) * radial, :], chosen).astype(jnp.bfloat16)
            out_ref[batch * quota + s] = tn(chosen, half_way)
            at = plan.half + batch * quota + s
            first = quota * radial + (s // 2) * narrow
            pair = ref[first : first + narrow, :].astype(jnp.float32)
            if s % 2:
                pair = pltpu.roll(pair, narrow, axis=1)
            out_ref[at, 0:narrow, :] = jnp.where(lane < narrow, pair, 0.0)
            out_ref[at, narrow:radial, :] = jnp.zeros((radial - narrow, radial), jnp.float32)


VMEM = pl.BlockSpec(memory_space=pltpu.VMEM)
HBM = pl.BlockSpec(memory_space=pltpu.HBM)


def call(kernel, outs, ins, scratch=()):
    return pl.pallas_call(
        kernel,
        out_shape=outs,
        in_specs=ins,
        out_specs=jax.tree.map(lambda _: VMEM, outs),
        scratch_shapes=scratch,
        compiler_params=pltpu.CompilerParams(vmem_limit_bytes=16 << 20),
    )


def fast_device(plan, images, radial_counts, order, zeros_table, noise_var):
    both = ("batch", "freq")
    radial, total, quota, pairs = plan.radial, plan.total, plan.quota, plan.pairs
    shape = jax.ShapeDtypeStruct
    block = shape((plan.devices, plan.rows, radial), jnp.bfloat16)
    coef, table, cb, sb, wave, zero, info = call(
        functools.partial(analysis_kernel, plan),
        (
            block,
            shape((2 * total, plan.angles), jnp.bfloat16),
            shape((2 * total, radial), jnp.float32),
            shape((2 * total, radial), jnp.float32),
            shape((2 * radial, radial), jnp.bfloat16),
            shape((plan.all_pairs, radial), jnp.int32),
            shape((32, radial), jnp.float32),
        ),
        [HBM] * 5,
        [
            pltpu.VMEM((plan.all_pairs // 4, 8 * plan.vecs, radial), jnp.float32),
            pltpu.VMEM((1, total), jnp.int32),
            pltpu.VMEM((1, total), jnp.int32),
            pltpu.VMEM((1, total), jnp.float32),
            pltpu.VMEM(zeros_table.shape, jnp.int32),
            pltpu.VMEM(images.shape, jnp.bfloat16),
            pltpu.SemaphoreType.DMA((5,)),
        ],
    )(
        *(
            pltpu.with_memory_space_constraint(array, pltpu.HBM)
            for array in (
                order.reshape(1, total),
                radial_counts.reshape(1, total),
                noise_var.reshape(1, total),
                zeros_table,
                images,
            )
        )
    )
    recv = lax.all_to_all(coef, both, split_axis=0, concat_axis=0, tiled=True)
    back, shrink = call(
        functools.partial(filter_kernel, plan),
        (block, shape((quota * radial + pairs * plan.narrow, radial), jnp.bfloat16)),
        [VMEM, VMEM],
        [
            pltpu.VMEM((plan.devices * plan.low_rows, radial), jnp.float32),
            pltpu.VMEM((quota, radial, radial), jnp.float32),
            pltpu.VMEM((pairs, plan.narrow, radial), jnp.float32),
            pltpu.VMEM((quota, plan.devices * plan.vecs, radial), jnp.bfloat16),
            pltpu.VMEM((pairs, plan.devices * plan.vecs, radial), jnp.bfloat16),
            pltpu.VMEM((quota, radial, radial), jnp.float32),
            pltpu.VMEM((pairs, plan.narrow, radial), jnp.float32),
        ],
    )(info, recv)
    returned = lax.all_to_all(back, both, split_axis=0, concat_axis=0, tiled=True)
    other = lax.ppermute(shrink, "batch", [(0, 1), (1, 0)])
    wiener_blocks = call(
        functools.partial(wiener_kernel, plan),
        shape((plan.owned, radial, radial), jnp.float32),
        [VMEM] * 3,
    )(shrink, other, info)
    denoised = call(
        functools.partial(synthesis_kernel, plan),
        shape((plan.count_img, radial, plan.angles), jnp.bfloat16),
        [VMEM] * 6,
        [
            pltpu.VMEM((plan.all_pairs // 4, 8 * plan.vecs, radial), jnp.float32),
            pltpu.VMEM((2 * total, plan.count_img * radial), jnp.bfloat16),
        ],
    )(table, cb, sb, wave, zero, returned)
    return denoised, wiener_blocks


def solution(mesh):
    owners, batches = mesh.shape["freq"], mesh.shape["batch"]

    def body(images, radial_counts, order, zeros_table, noise_var):
        plan = Plan(images.shape, order.shape[0], owners, batches)
        device = functools.partial(fast_device, plan) if plan.fits else per_device
        return device(images, radial_counts, order, zeros_table, noise_var)

    return jax.shard_map(
        body,
        mesh=mesh,
        in_specs=(P(("batch", "freq"), None, None), P(), P(), P(), P()),
        out_specs=(P(("batch", "freq"), None, None), P("freq", None, None)),
        check_vma=False,
    )
```
